256 devices in a mesh: ctx: 32 (over x, z), fsdp: 8 (over y, core).
Axes of the slice: x: 4, y: 4, z: 8, core: 2. Of those that a mesh axis runs over, the one named last changes fastest.
Arguments:
- layer_in: bfloat16 [8, 4096, 4096], P('fsdp', 'ctx'), may hold values from -6 to 6
- w_bc: bfloat16 [4096, 256], P('fsdp'), may hold values from -0.09375 to 0.09375
- conv_w: float32 [4, 256], replicated, may hold values from -3 to 3
- conv_b: float32 [256], replicated, may hold values from -0.5 to 0.5
- ssm_in: bfloat16 [8, 4096, 4096], P('fsdp', 'ctx'), may hold values from -6 to 6
- dt_raw: float32 [8, 4096, 32], P('fsdp', 'ctx'), may hold values from -4 to 4
- dt_bias: float32 [32], replicated, as said below
- a_log: float32 [32], replicated, as said below
- skip_scale: float32 [32], replicated, may hold values from 0.5 to 1.5
- grad_out: bfloat16 [8, 4096, 4096], P('fsdp', 'ctx'), may hold values from -6 to 6
Outputs:
- ssm_out: bfloat16 [8, 4096, 4096], P('fsdp', 'ctx')
- grad_ssm_in: bfloat16 [8, 4096, 4096], P('fsdp', 'ctx')
- grad_layer_in: bfloat16 [8, 4096, 4096], P('fsdp', 'ctx')
- grad_dt_raw: float32 [8, 4096, 32], P('fsdp', 'ctx')
- grad_w_bc: float32 [4096, 256], P('fsdp')
- grad_conv_w: float32 [4, 256], replicated
- grad_conv_b: float32 [256], replicated
- grad_dt_bias: float32 [32], replicated
- grad_a_log: float32 [32], replicated
- grad_skip: float32 [32], replicated
The draws below stay inside these ranges and needn't reach their ends.
Inputs may be any that keep to these rules, and one draw needn't show every extreme that they name: `dt_bias`: drawn together with a_log. `a_log`: drawn together with dt_bias.
All inputs are finite; a program needn't handle non-finite values.
Results may differ from the reference program's by a relative error of at most 0.039.
Values may be sent and summed in bfloat16 or wider, within the bound.
A program may use at most 320 MiB of HBM per device.

```python
import math
import jax
import jax.numpy as jnp
from jax import lax

D = 4096
H = 32
P_SIZE = 128
N = 128
SPAN = 128
KW = 4
TOK_DEV = 128
TOKENS = 4096
SEQS = 8


def head_tables(key):
    head_key = jax.random.fold_in(key, 101)
    lowest = math.log(30.0)
    highest = math.log(40.0 * TOKENS)
    memory = jnp.exp(jax.random.uniform(head_key, (H,), jnp.float32, lowest, highest))
    step_level = 0.1 / jnp.sqrt(jnp.minimum(memory, float(TOKENS)))
    rate = 1.0 / (memory * step_level)
    return (jnp.log(jnp.expm1(step_level)), jnp.log(rate))


def draw_dt_bias(key, part):
    return head_tables(key)[0]


def draw_a_log(key, part):
    return head_tables(key)[1]


def draw_dt_raw(key, part):
    offset_key = jax.random.fold_in(key, 5)
    rough_key = jax.random.fold_in(key, 6)
    blocks = TOKENS // TOK_DEV
    offsets = jax.random.uniform(offset_key, (SEQS, blocks, 1, H), jnp.float32, -0.8, 0.8)
    rough = 0.5 * jax.random.normal(rough_key, (SEQS, blocks, TOK_DEV, H), jnp.float32)
    return jnp.clip((offsets + rough).reshape(SEQS, TOKENS, H), -4.0, 4.0)


def with_spikes(values, rng, source, target, parts, factor):
    def block_of(position):
        return (jnp.arange(values.shape[position]) // (values.shape[position] // parts)).reshape((-1,) + (1,) * (values.ndim - 1 - position))

    near = jax.random.permutation(rng, parts)[block_of(target)]
    other_side = (block_of(target) + parts // 2) % parts
    return jnp.where((block_of(source) == near) | (block_of(source) == other_side), factor * values, values)


def steps_of(rng, dims, pieces, low, top_value):
    level = 1.0
    for axis_at, parts in pieces:
        draws = jax.random.uniform(jax.random.fold_in(jax.random.fold_in(rng, 6), axis_at), (parts,), jnp.float32, low / len(pieces), top_value / len(pieces))
        level = level * jnp.repeat(jnp.exp(draws), dims[axis_at] // parts).reshape((-1,) + (1,) * (len(dims) - 1 - axis_at))
    return level


def scatter_about(rng, shape, deviation, reach, shards=(), kind=jnp.bfloat16):
    level = steps_of(rng, shape, shards, -0.22, 0.18) if shards else 1.0
    values = jax.random.normal(rng, shape, jnp.float32) * deviation * level
    return jnp.minimum(jnp.maximum(values, -reach), reach).astype(kind)


def gaussian_with(rng, extent, spread, limit, split, heavy, kind=jnp.bfloat16):
    drawn = spread * jax.random.normal(rng, extent, jnp.float32)
    if split:
        drawn = drawn * steps_of(rng, extent, split, -0.22, 0.18)
    return jnp.clip(with_spikes(drawn, jax.random.fold_in(rng, 3), *heavy), -limit, limit).astype(kind)


def setup_inputs(seed: int = 0) -> dict:
    key_list = jax.random.split(jax.random.key(seed), 11)
    return {
        "layer_in": gaussian_with(key_list[0], (SEQS, TOKENS, D), 1.0, 6.0, ((0, 8), (1, 32)), (0, 2, 8, 2.0)),
        "w_bc": scatter_about(key_list[1], (D, 2 * N), D ** -0.5, 0.09375, ((0, 8),)),
        "conv_w": scatter_about(key_list[2], (KW, 2 * N), KW ** -0.5, 3.0, (), jnp.float32),
        "conv_b": jnp.clip(jax.random.uniform(key_list[3], (2 * N,), jnp.float32, -0.5, 0.5), -0.5, 0.5),
        "ssm_in": scatter_about(key_list[4], (SEQS, TOKENS, H * P_SIZE), 1.0, 6.0, ((0, 8), (1, 32))),
        "dt_raw": draw_dt_raw(jax.random.fold_in(key_list[10], 71), 0),
        "dt_bias": draw_dt_bias(jax.random.fold_in(key_list[10], 71), 0),
        "a_log": draw_a_log(jax.random.fold_in(key_list[10], 71), 0),
        "skip_scale": jnp.clip(jax.random.uniform(key_list[8], (H,), jnp.float32, 0.5, 1.5), 0.5, 1.5),
        "grad_out": scatter_about(key_list[9], (SEQS, TOKENS, H * P_SIZE), 1.0, 6.0, ((0, 8), (1, 32))),
    }


def prepare(padded, conv_w, conv_b, dt_raw, dt_bias, a_log):
    row_count = dt_raw.shape[0]
    conv_width = conv_w.shape[0]
    conv_sum = conv_b[None, :] + conv_w[0][None, :] * padded[0:row_count]
    for offset in range(1, conv_width):
        conv_sum = conv_sum + conv_w[offset][None, :] * padded[offset:offset + row_count]
    activated = jax.nn.silu(conv_sum)
    half_width = activated.shape[1] // 2
    b_in = activated[:, :half_width].astype(jnp.bfloat16)
    c_out = activated[:, half_width:].astype(jnp.bfloat16)
    step_size = jax.nn.softplus(dt_raw + dt_bias[None, :])
    log_decay = -step_size * jnp.exp(a_log)[None, :]
    return (b_in, c_out, step_size, log_decay)

def span_local(b_in, c_out, step_size, log_decay, values, skip_scale):
    span_len = step_size.shape[0]
    cumulated = jnp.cumsum(log_decay, axis=0)
    scores = jnp.dot(c_out, b_in.T, preferred_element_type=jnp.float32)
    per_head = cumulated.T
    gap_log = per_head[:, :, None] - per_head[:, None, :]
    row_ids = lax.broadcasted_iota(jnp.int32, (span_len, span_len), 0)
    col_ids = lax.broadcasted_iota(jnp.int32, (span_len, span_len), 1)
    causal_mask = (row_ids >= col_ids)[None, :, :]
    decay_grid = jnp.where(causal_mask, jnp.exp(jnp.where(causal_mask, gap_log, 0.0)), 0.0)
    mixing = (scores[None, :, :] * decay_grid * step_size.T[:, None, :]).astype(jnp.bfloat16)
    mixing = lax.optimization_barrier(mixing)
    inside_out = jnp.einsum('hij,jhp->ihp', mixing.astype(jnp.float32), values.astype(jnp.float32))
    local_out = inside_out + skip_scale[None, :, None] * values.astype(jnp.float32)
    end_weight = jnp.exp(per_head[:, -1:] - per_head) * step_size.T
    deposit = (end_weight[:, :, None] * b_in.astype(jnp.float32)[None, :, :]).astype(jnp.bfloat16)
    deposit = lax.optimization_barrier(deposit)
    span_state = jnp.einsum('hjn,jhp->hnp', deposit.astype(jnp.float32), values.astype(jnp.float32))
    return (local_out, span_state, jnp.exp(per_head[:, -1]), jnp.exp(cumulated))

def span_output(local_out, growth, c_out, state):
    stored = lax.optimization_barrier(state.astype(jnp.bfloat16))
    carried_out = jnp.einsum('in,hnp->ihp', c_out.astype(jnp.float32), stored.astype(jnp.float32))
    return local_out + growth[:, :, None] * carried_out

def sequence_forward(projected, conv_w, conv_b, values, dt_raw, dt_bias, a_log, skip_scale):
    conv_width = conv_w.shape[0]
    padded = jnp.concatenate([jnp.zeros((conv_width - 1, projected.shape[1]), projected.dtype), projected], 0)
    b_in, c_out, step_size, log_decay = prepare(padded, conv_w, conv_b, dt_raw, dt_bias, a_log)
    span_count = step_size.shape[0] // SPAN
    head_count = step_size.shape[1]
    head_size = values.shape[1] // head_count
    state_size = b_in.shape[1]
    items = (b_in.reshape(span_count, SPAN, state_size), c_out.reshape(span_count, SPAN, state_size), step_size.reshape(span_count, SPAN, head_count), log_decay.reshape(span_count, SPAN, head_count), values.reshape(span_count, SPAN, head_count, head_size))

    def advance(state, item):
        b_part, c_part, step_part, decay_part, value_part = item
        local_out, span_state, span_decay, growth = span_local(b_part, c_part, step_part, decay_part, value_part, skip_scale)
        result = span_output(local_out, growth, c_part, state).astype(jnp.bfloat16)
        return (span_decay[:, None, None] * state + span_state, result.reshape(SPAN, head_count * head_size))
    start_state = jnp.zeros((head_count, state_size, head_size), jnp.float32)
    final_state, outputs = lax.scan(jax.checkpoint(advance), start_state, items)
    return outputs.reshape(span_count * SPAN, head_count * head_size)

def reference(layer_in, w_bc, conv_w, conv_b, ssm_in, dt_raw, dt_bias, a_log, skip_scale, grad_out):

    def one_sequence(totals, item):
        tokens_in, values_in, raw_steps, upstream = item
        projected = jnp.dot(tokens_in, w_bc, preferred_element_type=jnp.float32)
        result, backward = jax.vjp(sequence_forward, projected, conv_w, conv_b, values_in, raw_steps, dt_bias, a_log, skip_scale)
        grad_proj, grad_cw, grad_cb, grad_values, grad_raw, grad_bias, grad_log, grad_skip_one = backward(upstream)
        grad_rounded = grad_proj.astype(jnp.bfloat16)
        grad_tokens = jnp.dot(grad_rounded, w_bc.T, preferred_element_type=jnp.float32).astype(jnp.bfloat16)
        grad_weight = jnp.dot(tokens_in.T, grad_rounded, preferred_element_type=jnp.float32)
        terms = (grad_weight, grad_cw, grad_cb, grad_bias, grad_log, grad_skip_one)
        totals = tuple((first + second for first, second in zip(totals, terms)))
        return (totals, (result, grad_values, grad_tokens, grad_raw))
    start = (jnp.zeros(w_bc.shape, jnp.float32), jnp.zeros(conv_w.shape, jnp.float32), jnp.zeros(conv_b.shape, jnp.float32), jnp.zeros(dt_bias.shape, jnp.float32), jnp.zeros(a_log.shape, jnp.float32), jnp.zeros(skip_scale.shape, jnp.float32))
    totals, stacked = lax.scan(one_sequence, start, (layer_in, ssm_in, dt_raw, grad_out))
    ssm_out, grad_ssm_in, grad_layer_in, grad_dt_raw = stacked
    grad_w_bc, grad_conv_w, grad_conv_b, grad_dt_bias, grad_a_log, grad_skip = totals
    return (ssm_out, grad_ssm_in, grad_layer_in, grad_dt_raw, grad_w_bc, grad_conv_w, grad_conv_b, grad_dt_bias, grad_a_log, grad_skip)
```

```python
import functools

import jax
import jax.numpy as jnp
from jax import lax
from jax.experimental import pallas as pl
from jax.experimental.pallas import tpu as pltpu
from jax.sharding import PartitionSpec as P

BF = jnp.bfloat16
F32 = jnp.float32
MESH = pl.DeviceIdType.MESH
HIGH = lax.Precision.HIGHEST
VMEM = pl.BlockSpec(memory_space=pltpu.VMEM)
BIG = 60 * 1024 * 1024

H = 32
S = 128
D = 4096
W2 = 256
ROWS = 512
NX, NZ, NY, NC = 4, 8, 4, 2
CTX = NX * NZ


def dot(a, b, ca=1, cb=0, precision=None):
    return lax.dot_general(
        a, b, (((ca,), (cb,)), ((), ())), preferred_element_type=F32, precision=precision
    )


def tri_upper():
    r = lax.broadcasted_iota(jnp.int32, (S, S), 0)
    c = lax.broadcasted_iota(jnp.int32, (S, S), 1)
    return r, c


def remote(src, dst, sems, slot, **where):
    return pltpu.make_async_remote_copy(
        src_ref=src,
        dst_ref=dst,
        send_sem=sems[0].at[slot],
        recv_sem=sems[1].at[slot],
        device_id=where,
        device_id_type=MESH,
    )


def greet(partners):
    barrier = pltpu.get_barrier_semaphore()
    for who in partners:
        pl.semaphore_signal(barrier, inc=1, device_id=who, device_id_type=MESH)
    pl.semaphore_wait(barrier, len(partners))


def gather_kernel(w_ref, tail_ref, full_ref, halo_ref, land_ref, send, recv):
    k = lax.axis_index("ctx")
    f = lax.axis_index("fsdp")
    y, c = f // 2, f % 2
    sib = y * 2 + (1 - c)
    up = ((y + 1) % NY) * 2 + c
    down = ((y + NY - 1) % NY) * 2 + c
    far = ((y + 2) % NY) * 2 + c
    nxt = (k + 1) % CTX
    prv = (k + CTX - 1) % CTX
    greet([{"fsdp": sib}, {"fsdp": up}, {"fsdp": down}, {"ctx": nxt}, {"ctx": prv}])
    sems = (send, recv)
    half = ROWS // 2

    def rows(owner, first=0, size=ROWS):
        return full_ref.at[pl.ds(pl.multiple_of(owner * ROWS + first, half), size), :]

    to_up = remote(w_ref, rows(f), sems, 0, fsdp=up)
    to_down = remote(w_ref, rows(f), sems, 1, fsdp=down)
    to_sib = remote(w_ref, rows(f), sems, 2, fsdp=sib)
    halo = remote(tail_ref, land_ref, sems, 3, ctx=nxt)
    to_up.start()
    to_down.start()
    to_sib.start()
    halo.start()
    full_ref[pl.ds(pl.multiple_of(f * ROWS, ROWS), ROWS), :] = w_ref[...]
    to_up.wait_recv()
    on_up = remote(rows(down, 0, half), rows(down, 0, half), sems, 4, fsdp=up)
    on_up.start()
    sib_down = remote(rows(down), rows(down), sems, 6, fsdp=sib)
    sib_down.start()
    to_down.wait_recv()
    on_down = remote(rows(up, half, half), rows(up, half, half), sems, 5, fsdp=down)
    on_down.start()
    sib_up = remote(rows(up), rows(up), sems, 7, fsdp=sib)
    sib_up.start()
    on_up.wait_recv()
    sib_a = remote(rows(far, 0, half), rows(far, 0, half), sems, 8, fsdp=sib)
    sib_a.start()
    on_down.wait_recv()
    sib_b = remote(rows(far, half, half), rows(far, half, half), sems, 9, fsdp=sib)
    sib_b.start()
    halo.wait_recv()
    halo_ref[...] = jnp.where(k > 0, land_ref[...], jnp.zeros_like(land_ref))
    for copy in (to_sib, sib_down, sib_up, sib_a, sib_b):
        copy.wait_recv()
    for copy in (to_up, to_down, to_sib, halo, on_up, on_down, sib_down, sib_up, sib_a, sib_b):
        copy.wait_send()


def gather(w, tail):
    return pl.pallas_call(
        gather_kernel,
        out_shape=(
            jax.ShapeDtypeStruct((D, W2), BF),
            jax.ShapeDtypeStruct(tail.shape, BF),
        ),
        in_specs=[VMEM, VMEM],
        out_specs=(VMEM, VMEM),
        scratch_shapes=[
            pltpu.VMEM(tail.shape, BF),
            pltpu.SemaphoreType.DMA((10,)),
            pltpu.SemaphoreType.DMA((10,)),
        ],
        compiler_params=pltpu.CompilerParams(
            collective_id=0, has_side_effects=True, vmem_limit_bytes=BIG
        ),
        name="gather_w",
    )(w, tail)


def local_kernel(
    tok_ref, halo_ref, w_ref, cw_ref, cb_ref, v_ref, raw_ref, bias_ref, alog_ref, skip_ref, g_ref,
    pad_ref, conv_ref, b_ref, c_ref, cum_ref, dt_ref, sig_ref, rate_ref, dec_ref,
    yin_ref, dvin_ref, s_ref, de_ref, u_ref, q_ref, db_ref, dc_ref, dcum_ref, ddt_ref, dskip_ref,
    scores_ref, dscores_ref, skipt_ref,
):
    pad_ref[0:8, :] = dot(halo_ref[...], w_ref[...])[8:16, :]
    pad_ref[8:, :] = dot(tok_ref[...], w_ref[...])
    conv = cb_ref[...] + cw_ref[0:1, :] * pad_ref[5 : 5 + S, :]
    for tap in range(1, 4):
        conv = conv + cw_ref[tap : tap + 1, :] * pad_ref[5 + tap : 5 + tap + S, :]
    conv_ref[...] = conv
    act = conv * jax.nn.sigmoid(conv)
    b_ref[...] = act[:, :S].astype(BF)
    c_ref[...] = act[:, S:].astype(BF)
    x = raw_ref[...] + bias_ref[...]
    dt = jnp.maximum(x, 0.0) + jnp.log1p(jnp.exp(-jnp.abs(x)))
    rate = jnp.exp(alog_ref[...])
    dt_ref[...] = dt.T
    sig_ref[...] = jax.nn.sigmoid(x).T
    rate_ref[...] = jnp.broadcast_to(rate, (S, H)).T
    skipt_ref[...] = jnp.broadcast_to(skip_ref[...], (S, H)).T
    r, c = tri_upper()
    cum = dot((-dt * rate).T, (r <= c).astype(F32), precision=HIGH)
    cum_ref[...] = cum
    dec_ref[...] = jnp.broadcast_to(jnp.exp(cum[:, S - 1 : S]), (H, S))
    scores_ref[...] = dot(c_ref[...], b_ref[...], 1, 1)
    dscores_ref[...] = jnp.zeros_like(dscores_ref)
    mask = r >= c
    eye = r == c

    def head(h, _):
        cols = pl.ds(pl.multiple_of(h * S, S), S)
        one = pl.ds(h, 1)
        cum_r = cum_ref[one, :]
        dt_r = dt_ref[one, :]
        skip = skipt_ref[one, :]
        across = jnp.broadcast_to(cum_r, (S, S))
        down = across.T
        grid = jnp.where(mask, jnp.exp(jnp.where(mask, down - across, 0.0)), 0.0)
        v = v_ref[:, cols]
        g = g_ref[:, cols]
        v32 = v.astype(F32)
        g32 = g.astype(F32)
        a1 = scores_ref[...] * grid
        mix = (a1 * dt_r).astype(BF)
        yin_ref[:, cols] = dot(mix, v) + skip * v32
        dvin_ref[:, cols] = dot(mix, g, 0, 0) + skip * g32
        dm = dot(g, v, 1, 1)
        dskip_ref[one, :] = jnp.sum(jnp.where(eye, dm, 0.0), axis=0, keepdims=True)
        dscores_ref[...] += dm * (grid * dt_r)
        xx = dm * a1
        ddt_ref[one, :] = jnp.sum(xx, axis=0, keepdims=True)
        ww = xx * dt_r
        dcum_ref[one, :] = jnp.sum(ww.T - ww, axis=0, keepdims=True)
        ew = jnp.exp(cum_r[:, S - 1 : S] - cum_r) * dt_r
        u = (jnp.broadcast_to(ew, (S, S)).T * v32).astype(BF)
        u_ref[:, cols] = u
        s_ref[h] = dot(b_ref[...], u, 0, 0)
        q = (jnp.exp(down) * g32).astype(BF)
        q_ref[:, cols] = q
        de_ref[h] = dot(c_ref[...], q, 0, 0)
        return 0

    lax.fori_loop(0, H, head, 0)
    ds = dscores_ref[...].astype(BF)
    dc_ref[...] = dot(ds, b_ref[...])
    db_ref[...] = dot(ds, c_ref[...], 0, 0)


def local(tok, halo, w, cw, cb, v, raw, bias, alog, skip, g):
    hs = jax.ShapeDtypeStruct((H, S), F32)
    ss = jax.ShapeDtypeStruct((S, S), F32)
    outs = (
        jax.ShapeDtypeStruct((S + 8, W2), F32),
        jax.ShapeDtypeStruct((S, W2), F32),
        jax.ShapeDtypeStruct((S, S), BF),
        jax.ShapeDtypeStruct((S, S), BF),
        hs, hs, hs, hs, hs,
        jax.ShapeDtypeStruct((S, D), F32),
        jax.ShapeDtypeStruct((S, D), F32),
        jax.ShapeDtypeStruct((H, S, S), F32),
        jax.ShapeDtypeStruct((H, S, S), F32),
        jax.ShapeDtypeStruct((S, D), BF),
        jax.ShapeDtypeStruct((S, D), BF),
        ss, ss, hs, hs, hs,
    )
    return pl.pallas_call(
        local_kernel,
        out_shape=outs,
        in_specs=[VMEM] * 11,
        out_specs=tuple(VMEM for _ in outs),
        scratch_shapes=[
            pltpu.VMEM((S, S), F32),
            pltpu.VMEM((S, S), F32),
            pltpu.VMEM((H, S), F32),
        ],
        compiler_params=pltpu.CompilerParams(vmem_limit_bytes=BIG),
        name="block_local",
    )(tok, halo, w, cw, cb, v, raw, bias, alog, skip, g)


SUB = 1
PIECES = H * SUB
PIECE = S // SUB
SKEW = 2


def chain_kernel(
    s_ref, de_ref, dec_ref, e_ref, f_ref, fs_ref, bs_ref, fsend, frecv, bsend, brecv
):
    k = lax.axis_index("ctx")
    nxt = (k + 1) % CTX
    prv = (k + CTX - 1) % CTX
    greet([{"ctx": nxt}, {"ctx": prv}])

    def part(i):
        return i // SUB, pl.ds(pl.multiple_of((i % SUB) * PIECE, PIECE), PIECE)

    def to_next(i):
        h, rows = part(i)
        return remote(fs_ref.at[h, rows, :], e_ref.at[h, rows, :], (fsend, frecv), i, ctx=nxt)

    def to_prev(i):
        h, rows = part(i)
        return remote(bs_ref.at[h, rows, :], f_ref.at[h, rows, :], (bsend, brecv), i, ctx=prv)

    def move(i, first, last, copy, mine, arrived, out):
        h, rows = part(i)

        @pl.when(first)
        def _():
            arrived[h, rows, :] = jnp.zeros((PIECE, S), BF)

        @pl.when(jnp.logical_not(first))
        def _():
            copy(i).wait_recv()

        @pl.when(jnp.logical_not(last))
        def _():
            total = dec_ref[pl.ds(h, 1), :] * arrived[h, rows, :].astype(F32) + mine[h, rows, :]
            out[h, rows, :] = total.astype(BF)
            copy(i).start()

    ahead = (CTX - 1 - 2 * k) * SKEW
    wait_f = jnp.maximum(-ahead, 0)
    wait_b = jnp.maximum(ahead, 0)

    def step(t, _):
        i = t - wait_f
        j = t - wait_b

        @pl.when(jnp.logical_and(i >= 0, i < PIECES))
        def _():
            move(i, k == 0, k == CTX - 1, to_next, s_ref, e_ref, fs_ref)

        @pl.when(jnp.logical_and(j >= 0, j < PIECES))
        def _():
            move(j, k == CTX - 1, k == 0, to_prev, de_ref, f_ref, bs_ref)

        return 0

    lax.fori_loop(0, PIECES + (CTX - 1) * SKEW, step, 0)

    def finish(i, _):
        @pl.when(k < CTX - 1)
        def _():
            to_next(i).wait_send()

        @pl.when(k > 0)
        def _():
            to_prev(i).wait_send()

        return 0

    lax.fori_loop(0, PIECES, finish, 0)


def chain(s, de, dec):
    state = jax.ShapeDtypeStruct((H, S, S), BF)
    return pl.pallas_call(
        chain_kernel,
        out_shape=(state, state),
        in_specs=[VMEM] * 3,
        out_specs=(VMEM, VMEM),
        scratch_shapes=[pltpu.VMEM((H, S, S), BF)] * 2 + [pltpu.SemaphoreType.DMA((PIECES,))] * 4,
        compiler_params=pltpu.CompilerParams(
            collective_id=1, has_side_effects=True, vmem_limit_bytes=BIG
        ),
        name="state_chain",
    )(s, de, dec)


def post_kernel(
    v_ref, g_ref, cw_ref, pad_ref, conv_ref, b_ref, c_ref, cum_ref, dt_ref, sig_ref, rate_ref,
    dec_ref, yin_ref, dvin_ref, u_ref, q_ref, db_ref, dc_ref, dcum_ref, ddt_ref, dskip_ref,
    e_ref, f_ref,
    out_ref, gv_ref, graw_ref, gpad_ref, small_ref,
    dbt_ref, dct_ref, dgrow_ref, dew_ref, ddec_ref, dconv_ref,
):
    dbt_ref[...] = db_ref[...]
    dct_ref[...] = dc_ref[...]

    def head(h, _):
        cols = pl.ds(pl.multiple_of(h * S, S), S)
        one = pl.ds(h, 1)
        cum_r = cum_ref[one, :]
        growth = jnp.exp(jnp.broadcast_to(cum_r, (S, S)).T)
        ew = jnp.broadcast_to(
            jnp.exp(cum_r[:, S - 1 : S] - cum_r) * dt_ref[one, :], (S, S)
        ).T
        e = e_ref[h]
        f = f_ref[h]
        ce = dot(c_ref[...], e)
        bf = dot(b_ref[...], f)
        out_ref[:, cols] = (yin_ref[:, cols] + growth * ce).astype(BF)
        gv_ref[:, cols] = (dvin_ref[:, cols] + ew * bf).astype(BF)
        dgrow_ref[one, :] = jnp.sum((g_ref[:, cols].astype(F32) * ce).T, axis=0, keepdims=True)
        dew_ref[one, :] = jnp.sum((v_ref[:, cols].astype(F32) * bf).T, axis=0, keepdims=True)
        ddec_ref[one, :] = jnp.sum(e.astype(F32) * f.astype(F32), axis=0, keepdims=True)
        dct_ref[...] += dot(q_ref[:, cols], e, 1, 1)
        dbt_ref[...] += dot(u_ref[:, cols], f, 1, 1)
        return 0

    lax.fori_loop(0, H, head, 0)

    cum = cum_ref[...]
    dt = dt_ref[...]
    rate = rate_ref[...]
    tail = jnp.exp(cum[:, S - 1 : S] - cum)
    dew = dew_ref[...]
    pull = dew * tail * dt
    at_last = jnp.sum(pull, axis=1, keepdims=True) + jnp.sum(
        ddec_ref[...] * dec_ref[...], axis=1, keepdims=True
    )
    lanes = lax.broadcasted_iota(jnp.int32, (H, S), 1)
    dcum = dcum_ref[...] + dgrow_ref[...] * jnp.exp(cum) - pull
    dcum = dcum + jnp.where(lanes == S - 1, at_last, 0.0)
    r, c = tri_upper()
    dld = dot(dcum, (r >= c).astype(F32), precision=HIGH)
    ddt = ddt_ref[...] + dew * tail - rate * dld
    graw = ddt * sig_ref[...]
    graw_ref[...] = graw.T

    small_ref[...] = jnp.zeros_like(small_ref)
    small_ref[5:6, 0:H] = jnp.sum(graw.T, axis=0, keepdims=True)
    small_ref[6:7, 0:H] = jnp.sum((-dt * rate * dld).T, axis=0, keepdims=True)
    small_ref[7:8, 0:H] = jnp.sum(dskip_ref[...].T, axis=0, keepdims=True)

    conv = conv_ref[...]
    sig = jax.nn.sigmoid(conv)
    slope = sig * (1.0 + conv * (1.0 - sig))
    dconv_ref[...] = jnp.zeros_like(dconv_ref)
    dconv_ref[8 : 8 + S, 0:S] = dbt_ref[...] * slope[:, :S]
    dconv_ref[8 : 8 + S, S:] = dct_ref[...] * slope[:, S:]
    dconv = dconv_ref[8 : 8 + S, :]
    for tap in range(4):
        small_ref[tap : tap + 1, :] = jnp.sum(
            dconv * pad_ref[5 + tap : 5 + tap + S, :], axis=0, keepdims=True
        )
    small_ref[4:5, :] = jnp.sum(dconv, axis=0, keepdims=True)
    total = cw_ref[3:4, :] * dconv_ref[0 : 8 + S, :]
    for tap in range(3):
        total = total + cw_ref[tap : tap + 1, :] * dconv_ref[3 - tap : 3 - tap + 8 + S, :]
    gpad_ref[...] = total


def post(*args):
    outs = (
        jax.ShapeDtypeStruct((S, D), BF),
        jax.ShapeDtypeStruct((S, D), BF),
        jax.ShapeDtypeStruct((S, H), F32),
        jax.ShapeDtypeStruct((S + 8, W2), F32),
        jax.ShapeDtypeStruct((8, W2), F32),
    )
    return pl.pallas_call(
        post_kernel,
        out_shape=outs,
        in_specs=[VMEM] * len(args),
        out_specs=tuple(VMEM for _ in outs),
        scratch_shapes=[pltpu.VMEM((S, S), F32)] * 2
        + [pltpu.VMEM((H, S), F32)] * 3
        + [pltpu.VMEM((S + 16, W2), F32)],
        compiler_params=pltpu.CompilerParams(vmem_limit_bytes=BIG),
        name="block_post",
    )(*args)


def reduce_kernel(
    gpad_ref, tok_ref, w_ref, small_ref, gtok_ref, gw_ref, sums_ref,
    rim_ref, gr_ref, keep_ref, sa_ref, ra_ref, sb_ref, rb_ref, t_ref, sc_ref, rc_ref,
    pz_ref, sd_ref, rd_ref, fin_ref, all_ref,
    ma_ref, mra_ref, mb_ref, mrb_ref, mc_ref, mrc_ref, mrd_ref,
    rim_sem, a_sem, b_sem, c_sem, d_sem, e_sem, f_sem, ma_sem, mb_sem, mc_sem, md_sem,
):
    k = lax.axis_index("ctx")
    f = lax.axis_index("fsdp")
    y, c = f // 2, f % 2
    x, z = k // NZ, k % NZ
    nxt = (k + 1) % CTX
    prv = (k + CTX - 1) % CTX
    sib = {"fsdp": y * 2 + (1 - c)}

    def at_y(d):
        return (y + d) % NY

    def at_x(d):
        return (x + d) % NX

    def at_z(d):
        return (z + d) % NZ

    def y_dev(d):
        return {"fsdp": at_y(d) * 2 + c}

    def x_dev(d):
        return {"ctx": at_x(d) * NZ + z}

    def z_dev(d):
        return {"ctx": x * NZ + at_z(d)}

    partners = [sib, {"ctx": nxt}, {"ctx": prv}]
    partners += [y_dev(d) for d in range(1, NY)]
    partners += [x_dev(d) for d in range(1, NX)]
    partners += [z_dev(d) for d in range(1, NZ)]
    greet(partners)

    def sems(s):
        return (s.at[0], s.at[1])

    rim = remote(gpad_ref.at[0:8, :], rim_ref, sems(rim_sem), 0, ctx=prv)
    rim.start()
    ma_ref[...] = small_ref[...]
    m_a = remote(ma_ref, mra_ref, sems(ma_sem), 0, **sib)
    m_a.start()
    rim.wait_recv()
    rest = jnp.where(k < CTX - 1, rim_ref[...], jnp.zeros_like(rim_ref))
    gr_ref[0 : S - 8, :] = gpad_ref[8:S, :].astype(BF)
    gr_ref[S - 8 : S, :] = (gpad_ref[S : S + 8, :] + rest).astype(BF)
    gr = gr_ref[...]

    def term(row):
        block = tok_ref[:, pl.ds(pl.multiple_of(row * ROWS, ROWS), ROWS)]
        return dot(block, gr, 0, 0)

    order = (2, 1, 3, 0)
    copies = {}
    for d in order:
        sa_ref[d] = term(at_y(d) * 2 + (1 - c)).astype(BF)
        copies[d] = remote(sa_ref.at[d], ra_ref.at[d], sems(a_sem), d, **sib)
        copies[d].start()
    m_a.wait_recv()
    low = jnp.where(c == 0, ma_ref[...], mra_ref[...])
    high = jnp.where(c == 0, mra_ref[...], ma_ref[...])
    mb_ref[y] = low + high
    m_b = [remote(mb_ref.at[y], mb_ref.at[y], sems(mb_sem), d - 1, **y_dev(d)) for d in range(1, NY)]
    for copy in m_b:
        copy.start()
    to_y = {}
    for d in order:
        mine = term(at_y(d) * 2 + c)
        copies[d].wait_recv()
        mine = mine + ra_ref[d].astype(F32)
        if d:
            sb_ref[d - 1] = mine.astype(BF)
            to_y[d] = remote(sb_ref.at[d - 1], rb_ref.at[d - 1], sems(b_sem), d - 1, **y_dev(d))
            to_y[d].start()
        else:
            t_ref[...] = mine
    for i in range(D // 1024):
        cols = slice(i * 1024, i * 1024 + 1024)
        gtok_ref[:, cols] = dot(gr, w_ref[cols, :], 1, 1).astype(BF)
    for copy in m_b:
        copy.wait_recv()
    mc_ref[x] = mb_ref[0] + mb_ref[1] + mb_ref[2] + mb_ref[3]
    m_c = [remote(mc_ref.at[x], mc_ref.at[x], sems(mc_sem), d - 1, **x_dev(d)) for d in range(1, NX)]
    for copy in m_c:
        copy.start()
    for d in (1, 3, 2):
        to_y[d].wait_recv()
        t_ref[...] += rb_ref[d - 1].astype(F32)
    px = ROWS // NX
    to_x = {}
    for d in (2, 1, 3):
        sc_ref[d - 1] = t_ref[pl.ds(pl.multiple_of(at_x(d) * px, px), px), :].astype(BF)
        to_x[d] = remote(sc_ref.at[d - 1], rc_ref.at[d - 1], sems(c_sem), d - 1, **x_dev(d))
        to_x[d].start()
    for copy in m_c:
        copy.wait_recv()
    mrd_ref[z] = mc_ref[0] + mc_ref[1] + mc_ref[2] + mc_ref[3]
    m_d = [remote(mrd_ref.at[z], mrd_ref.at[z], sems(md_sem), d - 1, **z_dev(d)) for d in range(1, NZ)]
    for copy in m_d:
        copy.start()
    acc = t_ref[pl.ds(pl.multiple_of(x * px, px), px), :]
    for d in (1, 3, 2):
        to_x[d].wait_recv()
        acc = acc + rc_ref[d - 1].astype(F32)
    pz_ref[...] = acc
    pzr = px // NZ
    to_z = {}
    for d in (4, 3, 5, 2, 6, 1, 7):
        sd_ref[d - 1] = pz_ref[pl.ds(pl.multiple_of(at_z(d) * pzr, pzr), pzr), :].astype(BF)
        to_z[d] = remote(sd_ref.at[d - 1], rd_ref.at[d - 1], sems(d_sem), d - 1, **z_dev(d))
        to_z[d].start()
    acc = pz_ref[pl.ds(pl.multiple_of(z * pzr, pzr), pzr), :]
    for d in (1, 7, 2, 6, 3, 5, 4):
        to_z[d].wait_recv()
        acc = acc + rd_ref[d - 1].astype(F32)
    fin_ref[...] = acc.astype(BF)

    def piece(xx, first, size):
        return all_ref.at[pl.ds(pl.multiple_of(xx * px + first, pzr), size), :]

    done = [
        remote(fin_ref, piece(x, z * pzr, pzr), sems(e_sem), d - 1, **z_dev(d))
        for d in (4, 3, 5, 2, 6, 1, 7)
    ]
    for copy in done:
        copy.start()
    all_ref[pl.ds(pl.multiple_of(x * px + z * pzr, pzr), pzr), :] = fin_ref[...]
    for copy in m_d:
        copy.wait_recv()
    total = mrd_ref[0]
    for i in range(1, NZ):
        total = total + mrd_ref[i]
    sums_ref[...] = total
    for copy in done:
        copy.wait_recv()
    last = [
        remote(piece(x, 0, px), piece(x, 0, px), sems(f_sem), d - 1, **x_dev(d)) for d in (2, 1, 3)
    ]
    for copy in last:
        copy.start()
    for copy in last:
        copy.wait_recv()
    gw_ref[...] = all_ref[...].astype(F32)
    sent = [rim, m_a] + m_b + m_c + m_d + done + last
    sent += list(copies.values()) + list(to_y.values()) + list(to_x.values()) + list(to_z.values())
    for copy in sent:
        copy.wait_send()


def reduce_all(gpad, tok, w, small):
    dma = pltpu.SemaphoreType.DMA
    px = ROWS // NX
    pzr = px // NZ
    return pl.pallas_call(
        reduce_kernel,
        out_shape=(
            jax.ShapeDtypeStruct((S, D), BF),
            jax.ShapeDtypeStruct((ROWS, W2), F32),
            jax.ShapeDtypeStruct((8, W2), F32),
        ),
        in_specs=[VMEM] * 4,
        out_specs=(VMEM,) * 3,
        scratch_shapes=[
            pltpu.VMEM((8, W2), F32),
            pltpu.VMEM((S, W2), BF),
            pltpu.VMEM((8, W2), F32),
            pltpu.VMEM((NY, ROWS, W2), BF),
            pltpu.VMEM((NY, ROWS, W2), BF),
            pltpu.VMEM((NY - 1, ROWS, W2), BF),
            pltpu.VMEM((NY - 1, ROWS, W2), BF),
            pltpu.VMEM((ROWS, W2), F32),
            pltpu.VMEM((NX - 1, px, W2), BF),
            pltpu.VMEM((NX - 1, px, W2), BF),
            pltpu.VMEM((px, W2), F32),
            pltpu.VMEM((NZ - 1, pzr, W2), BF),
            pltpu.VMEM((NZ - 1, pzr, W2), BF),
            pltpu.VMEM((pzr, W2), BF),
            pltpu.VMEM((ROWS, W2), BF),
            pltpu.VMEM((8, W2), F32),
            pltpu.VMEM((8, W2), F32),
            pltpu.VMEM((NY, 8, W2), F32),
            pltpu.VMEM((NY, 8, W2), F32),
            pltpu.VMEM((NX, 8, W2), F32),
            pltpu.VMEM((NX, 8, W2), F32),
            pltpu.VMEM((NZ, 8, W2), F32),
            dma((2, 1)),
            dma((2, NY)),
            dma((2, NY - 1)),
            dma((2, NX - 1)),
            dma((2, NZ - 1)),
            dma((2, NZ - 1)),
            dma((2, NX - 1)),
            dma((2, 1)),
            dma((2, NY - 1)),
            dma((2, NX - 1)),
            dma((2, NZ - 1)),
        ],
        compiler_params=pltpu.CompilerParams(
            collective_id=2, has_side_effects=True, vmem_limit_bytes=BIG
        ),
        name="reduce_w",
    )(gpad, tok, w, small)


def body(layer_in, w_bc, conv_w, conv_b, ssm_in, dt_raw, dt_bias, a_log, skip_scale, grad_out):
    tok, v, raw, g = layer_in[0], ssm_in[0], dt_raw[0], grad_out[0]
    w, halo = gather(w_bc, tok[S - 16 :])
    (
        pad, conv, b, c, cum, dt, sig, rate, dec,
        yin, dvin, s, de, u, q, db, dc, dcum, ddt, dskip,
    ) = local(
        tok, halo, w, conv_w, conv_b[None], v, raw, dt_bias[None], a_log[None], skip_scale[None], g
    )
    e, f = chain(s, de, dec)
    out, gv, graw, gpad, small = post(
        v, g, conv_w, pad, conv, b, c, cum, dt, sig, rate, dec, yin, dvin, u, q, db, dc,
        dcum, ddt, dskip, e, f,
    )
    gtok, gw, sums = reduce_all(gpad, tok, w, small)
    return (
        out[None],
        gv[None],
        gtok[None],
        graw[None],
        gw,
        sums[0:4],
        sums[4],
        sums[5, :H],
        sums[6, :H],
        sums[7, :H],
    )


def solution(mesh):
    split = P("fsdp", "ctx", None)
    in_specs = (
        split, P("fsdp", None), P(), P(), split, split, P(), P(), P(), split,
    )
    out_specs = (
        split, split, split, split, P("fsdp", None), P(), P(), P(), P(), P(),
    )
    return jax.shard_map(body, mesh=mesh, in_specs=in_specs, out_specs=out_specs, check_vma=False)
```

```python
import functools

import jax
import jax.numpy as jnp
from jax import lax
from jax.experimental import pallas as pl
from jax.experimental.pallas import tpu as pltpu
from jax.sharding import PartitionSpec as P

BF = jnp.bfloat16
F32 = jnp.float32
MESH = pl.DeviceIdType.MESH
HIGH = lax.Precision.HIGHEST
VMEM = pl.BlockSpec(memory_space=pltpu.VMEM)
BIG = 60 * 1024 * 1024

H = 32
S = 128
D = 4096
W2 = 256
ROWS = 512
NX, NZ, NY, NC = 4, 8, 4, 2
CTX = NX * NZ


def dot(a, b, ca=1, cb=0, precision=None):
    return lax.dot_general(
        a, b, (((ca,), (cb,)), ((), ())), preferred_element_type=F32, precision=precision
    )


def tri_upper():
    r = lax.broadcasted_iota(jnp.int32, (S, S), 0)
    c = lax.broadcasted_iota(jnp.int32, (S, S), 1)
    return r, c


def remote(src, dst, sems, slot, **where):
    return pltpu.make_async_remote_copy(
        src_ref=src,
        dst_ref=dst,
        send_sem=sems[0].at[slot],
        recv_sem=sems[1].at[slot],
        device_id=where,
        device_id_type=MESH,
    )


def greet(partners):
    barrier = pltpu.get_barrier_semaphore()
    for who in partners:
        pl.semaphore_signal(barrier, inc=1, device_id=who, device_id_type=MESH)
    pl.semaphore_wait(barrier, len(partners))


def by_head(row):
    return jnp.broadcast_to(row, (S, H)).T


def steps_of(raw, bias, alog):
    x = raw + by_head(bias)
    dt = jnp.maximum(x, 0.0) + jnp.log1p(jnp.exp(-jnp.abs(x)))
    return x, dt, by_head(jnp.exp(alog))


def gather_kernel(
    w_ref, tok_ref, raw_ref, bias_ref, alog_ref, full_ref, halo_ref, decs_ref, land_ref,
    send, recv, dsend, drecv,
):
    k = lax.axis_index("ctx")
    f = lax.axis_index("fsdp")
    y, c = f // 2, f % 2
    x, z = k // NZ, k % NZ
    sib = y * 2 + (1 - c)
    up = ((y + 1) % NY) * 2 + c
    down = ((y + NY - 1) % NY) * 2 + c
    far = ((y + 2) % NY) * 2 + c
    nxt = (k + 1) % CTX
    prv = (k + CTX - 1) % CTX
    row = [{"ctx": x * NZ + (z + d) % NZ} for d in range(1, NZ)]
    greet([{"fsdp": sib}, {"fsdp": up}, {"fsdp": down}, {"ctx": nxt}, {"ctx": prv}] + row)
    sems = (send, recv)
    half = ROWS // 2

    def rows(owner, first=0, size=ROWS):
        return full_ref.at[pl.ds(pl.multiple_of(owner * ROWS + first, half), size), :]

    to_up = remote(w_ref, rows(f), sems, 0, fsdp=up)
    to_down = remote(w_ref, rows(f), sems, 1, fsdp=down)
    to_sib = remote(w_ref, rows(f), sems, 2, fsdp=sib)
    halo = remote(tok_ref.at[0, S - 16 : S, :], land_ref, sems, 3, ctx=nxt)
    to_up.start()
    to_down.start()
    to_sib.start()
    halo.start()
    full_ref[pl.ds(pl.multiple_of(f * ROWS, ROWS), ROWS), :] = w_ref[...]
    _, dt, rate = steps_of(raw_ref[0], bias_ref[...], alog_ref[...])
    dec = jnp.exp(jnp.sum(-dt * rate, axis=1, keepdims=True))
    decs_ref[z] = jnp.broadcast_to(dec, (H, S))
    decs = [
        remote(decs_ref.at[z], decs_ref.at[z], (dsend, drecv), d - 1, **row[d - 1])
        for d in range(1, NZ)
    ]
    for copy in decs:
        copy.start()
    to_up.wait_recv()
    on_up = remote(rows(down, 0, half), rows(down, 0, half), sems, 4, fsdp=up)
    on_up.start()
    sib_down = remote(rows(down), rows(down), sems, 6, fsdp=sib)
    sib_down.start()
    to_down.wait_recv()
    on_down = remote(rows(up, half, half), rows(up, half, half), sems, 5, fsdp=down)
    on_down.start()
    sib_up = remote(rows(up), rows(up), sems, 7, fsdp=sib)
    sib_up.start()
    on_up.wait_recv()
    sib_a = remote(rows(far, 0, half), rows(far, 0, half), sems, 8, fsdp=sib)
    sib_a.start()
    on_down.wait_recv()
    sib_b = remote(rows(far, half, half), rows(far, half, half), sems, 9, fsdp=sib)
    sib_b.start()
    halo.wait_recv()
    halo_ref[...] = jnp.where(k > 0, land_ref[...], jnp.zeros_like(land_ref))
    for copy in [to_sib, sib_down, sib_up, sib_a, sib_b] + decs:
        copy.wait_recv()
    for copy in [to_up, to_down, to_sib, halo, on_up, on_down, sib_down, sib_up, sib_a, sib_b]:
        copy.wait_send()
    for copy in decs:
        copy.wait_send()


def gather(w, tok, raw, bias, alog):
    return pl.pallas_call(
        gather_kernel,
        out_shape=(
            jax.ShapeDtypeStruct((D, W2), BF),
            jax.ShapeDtypeStruct((16, D), BF),
            jax.ShapeDtypeStruct((NZ, H, S), F32),
        ),
        in_specs=[
            VMEM,
            pl.BlockSpec(memory_space=pl.ANY),
            VMEM,
            VMEM,
            VMEM,
        ],
        out_specs=(VMEM, VMEM, VMEM),
        scratch_shapes=[
            pltpu.VMEM((16, D), BF),
            pltpu.SemaphoreType.DMA((10,)),
            pltpu.SemaphoreType.DMA((10,)),
            pltpu.SemaphoreType.DMA((NZ - 1,)),
            pltpu.SemaphoreType.DMA((NZ - 1,)),
        ],
        compiler_params=pltpu.CompilerParams(
            collective_id=0, has_side_effects=True, vmem_limit_bytes=BIG
        ),
        name="gather_w",
    )(w, tok, raw, bias, alog)


def local_kernel(
    tok_ref, halo_ref, w_ref, cw_ref, cb_ref, v_ref, raw_ref, bias_ref, alog_ref, skip_ref, g_ref,
    pad_ref, conv_ref, b_ref, c_ref, cum_ref, dt_ref, sig_ref, rate_ref, dec_ref,
    yin_ref, dvin_ref, s_ref, de_ref, u_ref, q_ref, db_ref, dc_ref, dcum_ref, ddt_ref, dskip_ref,
    scores_ref, dscores_ref, skipt_ref,
):
    pad_ref[0:8, :] = dot(halo_ref[...], w_ref[...])[8:16, :]
    pad_ref[8:, :] = dot(tok_ref[0], w_ref[...])
    conv = cb_ref[...] + cw_ref[0:1, :] * pad_ref[5 : 5 + S, :]
    for tap in range(1, 4):
        conv = conv + cw_ref[tap : tap + 1, :] * pad_ref[5 + tap : 5 + tap + S, :]
    conv_ref[...] = conv
    act = conv * jax.nn.sigmoid(conv)
    b_ref[...] = act[:, :S].astype(BF)
    c_ref[...] = act[:, S:].astype(BF)
    x, dt, rate = steps_of(raw_ref[0], bias_ref[...], alog_ref[...])
    dt_ref[...] = dt
    sig_ref[...] = jax.nn.sigmoid(x)
    rate_ref[...] = rate
    skipt_ref[...] = by_head(skip_ref[...])
    r, c = tri_upper()
    cum = dot(-dt * rate, (r <= c).astype(F32), precision=HIGH)
    cum_ref[...] = cum
    dec_ref[...] = jnp.broadcast_to(jnp.exp(cum[:, S - 1 : S]), (H, S))
    scores_ref[...] = dot(c_ref[...], b_ref[...], 1, 1)
    dscores_ref[...] = jnp.zeros_like(dscores_ref)
    mask = r >= c
    eye = r == c

    def head(h, _):
        cols = pl.ds(pl.multiple_of(h * S, S), S)
        one = pl.ds(h, 1)
        cum_r = cum_ref[one, :]
        dt_r = dt_ref[one, :]
        skip = skipt_ref[one, :]
        across = jnp.broadcast_to(cum_r, (S, S))
        down = across.T
        grid = jnp.where(mask, jnp.exp(jnp.where(mask, down - across, 0.0)), 0.0)
        v = v_ref[0, :, cols]
        g = g_ref[0, :, cols]
        v32 = v.astype(F32)
        g32 = g.astype(F32)
        a1 = scores_ref[...] * grid
        mix = (a1 * dt_r).astype(BF)
        yin_ref[:, cols] = dot(mix, v) + skip * v32
        dvin_ref[:, cols] = dot(mix, g, 0, 0) + skip * g32
        dm = dot(g, v, 1, 1)
        dskip_ref[one, :] = jnp.sum(jnp.where(eye, dm, 0.0), axis=0, keepdims=True)
        dscores_ref[...] += dm * (grid * dt_r)
        xx = dm * a1
        ddt_ref[one, :] = jnp.sum(xx, axis=0, keepdims=True)
        ww = xx * dt_r
        dcum_ref[one, :] = jnp.sum(ww.T - ww, axis=0, keepdims=True)
        ew = jnp.exp(cum_r[:, S - 1 : S] - cum_r) * dt_r
        u = (jnp.broadcast_to(ew, (S, S)).T * v32).astype(BF)
        u_ref[:, cols] = u
        s_ref[h] = dot(b_ref[...], u, 0, 0)
        q = (jnp.exp(down) * g32).astype(BF)
        q_ref[:, cols] = q
        de_ref[h] = dot(c_ref[...], q, 0, 0)
        return 0

    lax.fori_loop(0, H, head, 0, unroll=4)
    ds = dscores_ref[...].astype(BF)
    dc_ref[...] = dot(ds, b_ref[...])
    db_ref[...] = dot(ds, c_ref[...], 0, 0)


def local(tok, halo, w, cw, cb, v, raw, bias, alog, skip, g):
    hs = jax.ShapeDtypeStruct((H, S), F32)
    ss = jax.ShapeDtypeStruct((S, S), F32)
    outs = (
        jax.ShapeDtypeStruct((S + 8, W2), F32),
        jax.ShapeDtypeStruct((S, W2), F32),
        jax.ShapeDtypeStruct((S, S), BF),
        jax.ShapeDtypeStruct((S, S), BF),
        hs, hs, hs, hs, hs,
        jax.ShapeDtypeStruct((S, D), F32),
        jax.ShapeDtypeStruct((S, D), F32),
        jax.ShapeDtypeStruct((H, S, S), F32),
        jax.ShapeDtypeStruct((H, S, S), F32),
        jax.ShapeDtypeStruct((S, D), BF),
        jax.ShapeDtypeStruct((S, D), BF),
        ss, ss, hs, hs, hs,
    )
    return pl.pallas_call(
        local_kernel,
        out_shape=outs,
        in_specs=[VMEM] * 11,
        out_specs=tuple(VMEM for _ in outs),
        scratch_shapes=[
            pltpu.VMEM((S, S), F32),
            pltpu.VMEM((S, S), F32),
            pltpu.VMEM((H, S), F32),
        ],
        compiler_params=pltpu.CompilerParams(vmem_limit_bytes=BIG),
        name="block_local",
    )(tok, halo, w, cw, cb, v, raw, bias, alog, skip, g)


SKEW = 3


def chain_kernel(
    s_ref, de_ref, decs_ref, e_ref, f_ref,
    rs_ref, rr_ref, ls_ref, lr_ref, ds_ref, dr_ref, us_ref, ur_ref, mul_ref,
    rsend, rrecv, lsend, lrecv, dsend, drecv, usend, urecv,
):
    k = lax.axis_index("ctx")
    x, z = k // NZ, k % NZ
    right = {"ctx": x * NZ + (z + 1) % NZ}
    left = {"ctx": x * NZ + (z + NZ - 1) % NZ}
    below = {"ctx": ((x + 1) % NX) * NZ + z}
    above = {"ctx": ((x + NX - 1) % NX) * NZ + z}
    greet([right, left, below, above])

    before = jnp.ones((H, S), F32)
    after = jnp.ones((H, S), F32)
    for i in range(NZ):
        d = decs_ref[i]
        before = before * jnp.where(i < z, d, 1.0)
        after = after * jnp.where(i > z, d, 1.0)
    mine = decs_ref[z]
    mul_ref[0] = before
    mul_ref[1] = after
    mul_ref[2] = mine
    mul_ref[3] = before * mine * after

    def go_right(i):
        return remote(rs_ref.at[i], rr_ref.at[i], (rsend, rrecv), i, **right)

    def go_left(i):
        return remote(ls_ref.at[i], lr_ref.at[i], (lsend, lrecv), i, **left)

    def go_below(i):
        return remote(ds_ref.at[i], dr_ref.at[i], (dsend, drecv), i, **below)

    def go_above(i):
        return remote(us_ref.at[i], ur_ref.at[i], (usend, urecv), i, **above)

    def factor(which, i):
        return mul_ref[which, pl.ds(i, 1), :]

    def arrive(i, first, copy, land):
        @pl.when(first)
        def _():
            land[i] = jnp.zeros(land.shape[1:], BF)

        @pl.when(jnp.logical_not(first))
        def _():
            copy(i).wait_recv()

    def to_right(i):
        arrive(i, z == 0, go_right, rr_ref)

        @pl.when(z < NZ - 1)
        def _():
            rs_ref[i, 0] = (factor(2, i) * rr_ref[i, 0].astype(F32) + s_ref[i]).astype(BF)
            rs_ref[i, 1] = (rr_ref[i, 1].astype(F32) + factor(0, i) * de_ref[i]).astype(BF)
            go_right(i).start()

    def to_left(i):
        arrive(i, z == NZ - 1, go_left, lr_ref)

        @pl.when(z > 0)
        def _():
            ls_ref[i, 0] = (lr_ref[i, 0].astype(F32) + factor(1, i) * s_ref[i]).astype(BF)
            ls_ref[i, 1] = (factor(2, i) * lr_ref[i, 1].astype(F32) + de_ref[i]).astype(BF)
            go_left(i).start()

    def to_below(i):
        arrive(i, x == 0, go_below, dr_ref)
        entering = dr_ref[i].astype(F32)
        inside = rr_ref[i, 0].astype(F32)
        e_ref[i] = (factor(0, i) * entering + inside).astype(BF)

        @pl.when(x < NX - 1)
        def _():
            total = lr_ref[i, 0].astype(F32) + factor(1, i) * (factor(2, i) * inside + s_ref[i])
            ds_ref[i] = (factor(3, i) * entering + total).astype(BF)
            go_below(i).start()

    def to_above(i):
        arrive(i, x == NX - 1, go_above, ur_ref)
        entering = ur_ref[i].astype(F32)
        inside = lr_ref[i, 1].astype(F32)
        f_ref[i] = (factor(1, i) * entering + inside).astype(BF)

        @pl.when(x > 0)
        def _():
            total = rr_ref[i, 1].astype(F32) + factor(0, i) * (factor(2, i) * inside + de_ref[i])
            us_ref[i] = (factor(3, i) * entering + total).astype(BF)
            go_above(i).start()

    late = jnp.maximum(z, NZ - 1 - z)
    starts = (z * SKEW, (NZ - 1 - z) * SKEW, (late + x) * SKEW, (late + NX - 1 - x) * SKEW)
    early = jnp.minimum(z, NZ - 1 - z) * SKEW

    def step(t, _):
        for start, act in zip(starts, (to_right, to_left, to_below, to_above)):
            i = t - (start - early)

            @pl.when(jnp.logical_and(i >= 0, i < H))
            def _():
                act(i)

        return 0

    lax.fori_loop(0, H + (NZ + NX - 2) * SKEW, step, 0)

    def finish(i, _):
        for here, copy in (
            (z < NZ - 1, go_right), (z > 0, go_left), (x < NX - 1, go_below), (x > 0, go_above)
        ):
            @pl.when(here)
            def _():
                copy(i).wait_send()

        return 0

    lax.fori_loop(0, H, finish, 0)


def chain(s, de, decs):
    state = jax.ShapeDtypeStruct((H, S, S), BF)
    return pl.pallas_call(
        chain_kernel,
        out_shape=(state, state),
        in_specs=[VMEM] * 3,
        out_specs=(VMEM, VMEM),
        scratch_shapes=[pltpu.VMEM((H, 2, S, S), BF)] * 4
        + [pltpu.VMEM((H, S, S), BF)] * 4
        + [pltpu.VMEM((4, H, S), F32)]
        + [pltpu.SemaphoreType.DMA((H,))] * 8,
        compiler_params=pltpu.CompilerParams(
            collective_id=1, has_side_effects=True, vmem_limit_bytes=BIG
        ),
        name="state_chain",
    )(s, de, decs)


def post_kernel(
    v_ref, g_ref, cw_ref, pad_ref, conv_ref, b_ref, c_ref, cum_ref, dt_ref, sig_ref, rate_ref,
    dec_ref, yin_ref, dvin_ref, u_ref, q_ref, db_ref, dc_ref, dcum_ref, ddt_ref, dskip_ref,
    e_ref, f_ref,
    out_ref, gv_ref, graw_ref, gpad_ref, small_ref,
    dbt_ref, dct_ref, dgrow_ref, dew_ref, ddec_ref, dconv_ref,
):
    dbt_ref[...] = db_ref[...]
    dct_ref[...] = dc_ref[...]

    def head(h, _):
        cols = pl.ds(pl.multiple_of(h * S, S), S)
        one = pl.ds(h, 1)
        cum_r = cum_ref[one, :]
        growth = jnp.exp(jnp.broadcast_to(cum_r, (S, S)).T)
        ew = jnp.broadcast_to(
            jnp.exp(cum_r[:, S - 1 : S] - cum_r) * dt_ref[one, :], (S, S)
        ).T
        e = e_ref[h]
        f = f_ref[h]
        ce = dot(c_ref[...], e)
        bf = dot(b_ref[...], f)
        out_ref[0, :, cols] = (yin_ref[:, cols] + growth * ce).astype(BF)
        gv_ref[0, :, cols] = (dvin_ref[:, cols] + ew * bf).astype(BF)
        dgrow_ref[one, :] = jnp.sum((g_ref[0, :, cols].astype(F32) * ce).T, axis=0, keepdims=True)
        dew_ref[one, :] = jnp.sum((v_ref[0, :, cols].astype(F32) * bf).T, axis=0, keepdims=True)
        ddec_ref[one, :] = jnp.sum(e.astype(F32) * f.astype(F32), axis=0, keepdims=True)
        dct_ref[...] += dot(q_ref[:, cols], e, 1, 1)
        dbt_ref[...] += dot(u_ref[:, cols], f, 1, 1)
        return 0

    lax.fori_loop(0, H, head, 0, unroll=4)

    cum = cum_ref[...]
    dt = dt_ref[...]
    rate = rate_ref[...]
    tail = jnp.exp(cum[:, S - 1 : S] - cum)
    dew = dew_ref[...]
    pull = dew * tail * dt
    at_last = jnp.sum(pull, axis=1, keepdims=True) + jnp.sum(
        ddec_ref[...] * dec_ref[...], axis=1, keepdims=True
    )
    lanes = lax.broadcasted_iota(jnp.int32, (H, S), 1)
    dcum = dcum_ref[...] + dgrow_ref[...] * jnp.exp(cum) - pull
    dcum = dcum + jnp.where(lanes == S - 1, at_last, 0.0)
    r, c = tri_upper()
    dld = dot(dcum, (r >= c).astype(F32), precision=HIGH)
    ddt = ddt_ref[...] + dew * tail - rate * dld
    graw = ddt * sig_ref[...]
    graw_ref[0] = graw

    small_ref[...] = jnp.zeros_like(small_ref)
    small_ref[5:6, 0:H] = jnp.sum(graw.T, axis=0, keepdims=True)
    small_ref[6:7, 0:H] = jnp.sum((-dt * rate * dld).T, axis=0, keepdims=True)
    small_ref[7:8, 0:H] = jnp.sum(dskip_ref[...].T, axis=0, keepdims=True)

    conv = conv_ref[...]
    sig = jax.nn.sigmoid(conv)
    slope = sig * (1.0 + conv * (1.0 - sig))
    dconv_ref[...] = jnp.zeros_like(dconv_ref)
    dconv_ref[8 : 8 + S, 0:S] = dbt_ref[...] * slope[:, :S]
    dconv_ref[8 : 8 + S, S:] = dct_ref[...] * slope[:, S:]
    dconv = dconv_ref[8 : 8 + S, :]
    for tap in range(4):
        small_ref[tap : tap + 1, :] = jnp.sum(
            dconv * pad_ref[5 + tap : 5 + tap + S, :], axis=0, keepdims=True
        )
    small_ref[4:5, :] = jnp.sum(dconv, axis=0, keepdims=True)
    total = cw_ref[3:4, :] * dconv_ref[0 : 8 + S, :]
    for tap in range(3):
        total = total + cw_ref[tap : tap + 1, :] * dconv_ref[3 - tap : 3 - tap + 8 + S, :]
    gpad_ref[...] = total


def post(*args):
    outs = (
        jax.ShapeDtypeStruct((1, S, D), BF),
        jax.ShapeDtypeStruct((1, S, D), BF),
        jax.ShapeDtypeStruct((1, H, S), F32),
        jax.ShapeDtypeStruct((S + 8, W2), F32),
        jax.ShapeDtypeStruct((8, W2), F32),
    )
    return pl.pallas_call(
        post_kernel,
        out_shape=outs,
        in_specs=[VMEM] * len(args),
        out_specs=tuple(VMEM for _ in outs),
        scratch_shapes=[pltpu.VMEM((S, S), F32)] * 2
        + [pltpu.VMEM((H, S), F32)] * 3
        + [pltpu.VMEM((S + 16, W2), F32)],
        compiler_params=pltpu.CompilerParams(vmem_limit_bytes=BIG),
        name="block_post",
    )(*args)


def reduce_kernel(
    gpad_ref, tok_ref, small_ref, gr_ref, all_ref, sums_ref,
    rim_ref, sa_ref, ra_ref, sb_ref, rb_ref, t_ref, sc_ref, rc_ref,
    pz_ref, sd_ref, rd_ref, fin_ref,
    ma_ref, mra_ref, mb_ref, mc_ref, mrd_ref,
    rim_sem, a_sem, b_sem, c_sem, d_sem, e_sem, f_sem, ma_sem, mb_sem, mc_sem, md_sem,
):
    k = lax.axis_index("ctx")
    f = lax.axis_index("fsdp")
    y, c = f // 2, f % 2
    x, z = k // NZ, k % NZ
    nxt = (k + 1) % CTX
    prv = (k + CTX - 1) % CTX
    sib = {"fsdp": y * 2 + (1 - c)}

    def at_y(d):
        return (y + d) % NY

    def at_x(d):
        return (x + d) % NX

    def at_z(d):
        return (z + d) % NZ

    def y_dev(d):
        return {"fsdp": at_y(d) * 2 + c}

    def x_dev(d):
        return {"ctx": at_x(d) * NZ + z}

    def z_dev(d):
        return {"ctx": x * NZ + at_z(d)}

    partners = [sib, {"ctx": nxt}, {"ctx": prv}]
    partners += [y_dev(d) for d in range(1, NY)]
    partners += [x_dev(d) for d in range(1, NX)]
    partners += [z_dev(d) for d in range(1, NZ)]
    greet(partners)

    def sems(s):
        return (s.at[0], s.at[1])

    rim = remote(gpad_ref.at[0:8, :], rim_ref, sems(rim_sem), 0, ctx=prv)
    rim.start()
    ma_ref[...] = small_ref[...]
    m_a = remote(ma_ref, mra_ref, sems(ma_sem), 0, **sib)
    m_a.start()
    rim.wait_recv()
    rest = jnp.where(k < CTX - 1, rim_ref[...], jnp.zeros_like(rim_ref))
    gr_ref[0 : S - 8, :] = gpad_ref[8:S, :].astype(BF)
    gr_ref[S - 8 : S, :] = (gpad_ref[S : S + 8, :] + rest).astype(BF)
    gr = gr_ref[...]

    def term(row):
        block = tok_ref[0, :, pl.ds(pl.multiple_of(row * ROWS, ROWS), ROWS)]
        return dot(block, gr, 0, 0)

    order = (2, 1, 3, 0)
    copies = {}
    for d in order:
        sa_ref[d] = term(at_y(d) * 2 + (1 - c)).astype(BF)
        copies[d] = remote(sa_ref.at[d], ra_ref.at[d], sems(a_sem), d, **sib)
        copies[d].start()
    m_a.wait_recv()
    low = jnp.where(c == 0, ma_ref[...], mra_ref[...])
    high = jnp.where(c == 0, mra_ref[...], ma_ref[...])
    mb_ref[y] = low + high
    m_b = [remote(mb_ref.at[y], mb_ref.at[y], sems(mb_sem), d - 1, **y_dev(d)) for d in range(1, NY)]
    for copy in m_b:
        copy.start()
    to_y = {}
    for d in order:
        mine = term(at_y(d) * 2 + c)
        copies[d].wait_recv()
        mine = mine + ra_ref[d].astype(F32)
        if d:
            sb_ref[d - 1] = mine.astype(BF)
            to_y[d] = remote(sb_ref.at[d - 1], rb_ref.at[d - 1], sems(b_sem), d - 1, **y_dev(d))
            to_y[d].start()
        else:
            t_ref[...] = mine
    for copy in m_b:
        copy.wait_recv()
    mc_ref[x] = mb_ref[0] + mb_ref[1] + mb_ref[2] + mb_ref[3]
    m_c = [remote(mc_ref.at[x], mc_ref.at[x], sems(mc_sem), d - 1, **x_dev(d)) for d in range(1, NX)]
    for copy in m_c:
        copy.start()
    for d in (1, 3, 2):
        to_y[d].wait_recv()
        t_ref[...] += rb_ref[d - 1].astype(F32)
    px = ROWS // NX
    to_x = {}
    for d in (2, 1, 3):
        sc_ref[d - 1] = t_ref[pl.ds(pl.multiple_of(at_x(d) * px, px), px), :].astype(BF)
        to_x[d] = remote(sc_ref.at[d - 1], rc_ref.at[d - 1], sems(c_sem), d - 1, **x_dev(d))
        to_x[d].start()
    for copy in m_c:
        copy.wait_recv()
    mrd_ref[z] = mc_ref[0] + mc_ref[1] + mc_ref[2] + mc_ref[3]
    m_d = [remote(mrd_ref.at[z], mrd_ref.at[z], sems(md_sem), d - 1, **z_dev(d)) for d in range(1, NZ)]
    for copy in m_d:
        copy.start()
    acc = t_ref[pl.ds(pl.multiple_of(x * px, px), px), :]
    for d in (1, 3, 2):
        to_x[d].wait_recv()
        acc = acc + rc_ref[d - 1].astype(F32)
    pz_ref[...] = acc
    pzr = px // NZ
    to_z = {}
    for d in (4, 3, 5, 2, 6, 1, 7):
        sd_ref[d - 1] = pz_ref[pl.ds(pl.multiple_of(at_z(d) * pzr, pzr), pzr), :].astype(BF)
        to_z[d] = remote(sd_ref.at[d - 1], rd_ref.at[d - 1], sems(d_sem), d - 1, **z_dev(d))
        to_z[d].start()
    acc = pz_ref[pl.ds(pl.multiple_of(z * pzr, pzr), pzr), :]
    for d in (1, 7, 2, 6, 3, 5, 4):
        to_z[d].wait_recv()
        acc = acc + rd_ref[d - 1].astype(F32)
    fin_ref[...] = acc.astype(BF)

    def piece(xx, first, size):
        return all_ref.at[pl.ds(pl.multiple_of(xx * px + first, pzr), size), :]

    done = [
        remote(fin_ref, piece(x, z * pzr, pzr), sems(e_sem), d - 1, **z_dev(d))
        for d in (4, 3, 5, 2, 6, 1, 7)
    ]
    for copy in done:
        copy.start()
    all_ref[pl.ds(pl.multiple_of(x * px + z * pzr, pzr), pzr), :] = fin_ref[...]
    for copy in m_d:
        copy.wait_recv()
    total = mrd_ref[0]
    for i in range(1, NZ):
        total = total + mrd_ref[i]
    sums_ref[...] = total
    for copy in done:
        copy.wait_recv()
    last = [
        remote(piece(x, 0, px), piece(x, 0, px), sems(f_sem), d - 1, **x_dev(d)) for d in (2, 1, 3)
    ]
    for copy in last:
        copy.start()
    for copy in last:
        copy.wait_recv()
    sent = [rim, m_a] + m_b + m_c + m_d + done + last
    sent += list(copies.values()) + list(to_y.values()) + list(to_x.values()) + list(to_z.values())
    for copy in sent:
        copy.wait_send()


def reduce_all(gpad, tok, small):
    dma = pltpu.SemaphoreType.DMA
    px = ROWS // NX
    pzr = px // NZ
    return pl.pallas_call(
        reduce_kernel,
        out_shape=(
            jax.ShapeDtypeStruct((S, W2), BF),
            jax.ShapeDtypeStruct((ROWS, W2), BF),
            jax.ShapeDtypeStruct((8, W2), F32),
        ),
        in_specs=[VMEM] * 3,
        out_specs=(VMEM,) * 3,
        scratch_shapes=[
            pltpu.VMEM((8, W2), F32),
            pltpu.VMEM((NY, ROWS, W2), BF),
            pltpu.VMEM((NY, ROWS, W2), BF),
            pltpu.VMEM((NY - 1, ROWS, W2), BF),
            pltpu.VMEM((NY - 1, ROWS, W2), BF),
            pltpu.VMEM((ROWS, W2), F32),
            pltpu.VMEM((NX - 1, px, W2), BF),
            pltpu.VMEM((NX - 1, px, W2), BF),
            pltpu.VMEM((px, W2), F32),
            pltpu.VMEM((NZ - 1, pzr, W2), BF),
            pltpu.VMEM((NZ - 1, pzr, W2), BF),
            pltpu.VMEM((pzr, W2), BF),
            pltpu.VMEM((8, W2), F32),
            pltpu.VMEM((8, W2), F32),
            pltpu.VMEM((NY, 8, W2), F32),
            pltpu.VMEM((NX, 8, W2), F32),
            pltpu.VMEM((NZ, 8, W2), F32),
            dma((2, 1)),
            dma((2, NY)),
            dma((2, NY - 1)),
            dma((2, NX - 1)),
            dma((2, NZ - 1)),
            dma((2, NZ - 1)),
            dma((2, NX - 1)),
            dma((2, 1)),
            dma((2, NY - 1)),
            dma((2, NX - 1)),
            dma((2, NZ - 1)),
        ],
        compiler_params=pltpu.CompilerParams(
            collective_id=2, has_side_effects=True, vmem_limit_bytes=BIG
        ),
        name="reduce_w",
    )(gpad, tok, small)


def last_kernel(
    gr_ref, w_ref, all_ref, sums_ref, gtok_ref, gw_ref, gcw_ref, gcb_ref, gbias_ref, galog_ref,
    gskip_ref,
):
    for i in range(D // 1024):
        cols = slice(i * 1024, i * 1024 + 1024)
        gtok_ref[0, :, cols] = dot(gr_ref[...], w_ref[cols, :], 1, 1).astype(BF)
    gw_ref[...] = all_ref[...].astype(F32)
    gcw_ref[...] = sums_ref[0:4, :]
    gcb_ref[...] = sums_ref[4:5, :]
    gbias_ref[...] = sums_ref[5:6, 0:H]
    galog_ref[...] = sums_ref[6:7, 0:H]
    gskip_ref[...] = sums_ref[7:8, 0:H]


def finish_all(gr, w, total, sums):
    head = jax.ShapeDtypeStruct((1, H), F32)
    return pl.pallas_call(
        last_kernel,
        out_shape=(
            jax.ShapeDtypeStruct((1, S, D), BF),
            jax.ShapeDtypeStruct((ROWS, W2), F32),
            jax.ShapeDtypeStruct((4, W2), F32),
            jax.ShapeDtypeStruct((1, W2), F32),
            head, head, head,
        ),
        in_specs=[VMEM] * 4,
        out_specs=(VMEM,) * 7,
        compiler_params=pltpu.CompilerParams(vmem_limit_bytes=BIG),
        name="finish_w",
    )(gr, w, total, sums)


def body(layer_in, w_bc, conv_w, conv_b, ssm_in, dt_raw, dt_bias, a_log, skip_scale, grad_out):
    bias, alog = dt_bias[None], a_log[None]
    raw = jnp.swapaxes(dt_raw, 1, 2)
    w, halo, decs = gather(w_bc, layer_in, raw, bias, alog)
    (
        pad, conv, b, c, cum, dt, sig, rate, dec,
        yin, dvin, s, de, u, q, db, dc, dcum, ddt, dskip,
    ) = local(
        layer_in, halo, w, conv_w, conv_b[None], ssm_in, raw, bias, alog, skip_scale[None],
        grad_out,
    )
    e, f = chain(s, de, decs)
    out, gv, graw, gpad, small = post(
        ssm_in, grad_out, conv_w, pad, conv, b, c, cum, dt, sig, rate, dec, yin, dvin, u, q, db, dc,
        dcum, ddt, dskip, e, f,
    )
    gr, total, sums = reduce_all(gpad, layer_in, small)
    gtok, gw, gcw, gcb, gbias, galog, gskip = finish_all(gr, w, total, sums)
    return (out, gv, gtok, jnp.swapaxes(graw, 1, 2), gw, gcw, gcb[0], gbias[0], galog[0], gskip[0])


def solution(mesh):
    split = P("fsdp", "ctx", None)
    in_specs = (
        split, P("fsdp", None), P(), P(), split, split, P(), P(), P(), split,
    )
    out_specs = (
        split, split, split, split, P("fsdp", None), P(), P(), P(), P(), P(),
    )
    return jax.shard_map(body, mesh=mesh, in_specs=in_specs, out_specs=out_specs, check_vma=False)
```

```python
import functools

import jax
import jax.numpy as jnp
from jax import lax
from jax.experimental import pallas as pl
from jax.experimental.pallas import tpu as pltpu
from jax.sharding import PartitionSpec as P

BF = jnp.bfloat16
F32 = jnp.float32
MESH = pl.DeviceIdType.MESH
HIGH = lax.Precision.HIGHEST
VMEM = pl.BlockSpec(memory_space=pltpu.VMEM)
BIG = 60 * 1024 * 1024

H = 32
S = 128
D = 4096
W2 = 256
ROWS = 512
NX, NZ, NY, NC = 4, 8, 4, 2
CTX = NX * NZ


def dot(a, b, ca=1, cb=0, precision=None):
    return lax.dot_general(
        a, b, (((ca,), (cb,)), ((), ())), preferred_element_type=F32, precision=precision
    )


def tri_upper():
    r = lax.broadcasted_iota(jnp.int32, (S, S), 0)
    c = lax.broadcasted_iota(jnp.int32, (S, S), 1)
    return r, c


def remote(src, dst, sems, slot, **where):
    return pltpu.make_async_remote_copy(
        src_ref=src,
        dst_ref=dst,
        send_sem=sems[0].at[slot],
        recv_sem=sems[1].at[slot],
        device_id=where,
        device_id_type=MESH,
    )


def greet(partners):
    barrier = pltpu.get_barrier_semaphore()
    for who in partners:
        pl.semaphore_signal(barrier, inc=1, device_id=who, device_id_type=MESH)
    pl.semaphore_wait(barrier, len(partners))


def by_head(row):
    return jnp.broadcast_to(row, (S, H)).T


def steps_of(raw, bias, alog):
    x = raw + by_head(bias)
    dt = jnp.maximum(x, 0.0) + jnp.log1p(jnp.exp(-jnp.abs(x)))
    return x, dt, by_head(jnp.exp(alog))


def flip(tile):
    return tile.T


def row_sums(tile):
    return jnp.sum(tile.T, axis=0, keepdims=True)


SKEW = 3
PX = ROWS // NX
PZ = PX // NZ

INPUTS = ("w_ref", "tok_hbm", "cw_ref", "cb_ref", "v_hbm", "raw_ref", "bias_ref", "alog_ref",
          "skip_ref", "g_hbm")
OUTPUTS = (
    ("out_hbm", (1, S, D), BF, False),
    ("gv_hbm", (1, S, D), BF, False),
    ("gtok_hbm", (1, S, D), BF, False),
    ("graw_ref", (1, H, S), F32, True),
    ("all_ref", (ROWS, W2), BF, True),
    ("sums_ref", (8, W2), F32, True),
)
BUFFERS = (
    ("full_ref", (D, W2), BF),
    ("halo_ref", (16, D), BF),
    ("tok_ref", (S, D), BF),
    ("v_ref", (S, D), BF),
    ("g_ref", (S, D), BF),
    ("out_ref", (S, D), BF),
    ("gv_ref", (S, D), BF),
    ("gtok_ref", (S, D), BF),
    ("decs_ref", (NZ, H, S), F32),
    ("pad_ref", (S + 8, W2), F32),
    ("conv_ref", (S, W2), F32),
    ("b_ref", (S, S), BF),
    ("c_ref", (S, S), BF),
    ("cum_ref", (H, S), F32),
    ("dt_ref", (H, S), F32),
    ("sig_ref", (H, S), F32),
    ("rate_ref", (H, S), F32),
    ("skipt_ref", (H, S), F32),
    ("dcum_ref", (H, S), F32),
    ("ddt_ref", (H, S), F32),
    ("dskip_ref", (H, S), F32),
    ("dgrow_ref", (H, S), F32),
    ("dew_ref", (H, S), F32),
    ("ddec_ref", (H, S), F32),
    ("yin_ref", (S, D), F32),
    ("dvin_ref", (S, D), F32),
    ("s_ref", (H, S, S), F32),
    ("de_ref", (H, S, S), F32),
    ("down_ref", (H, S, S), F32),
    ("ew_ref", (H, S, S), F32),
    ("u_ref", (S, D), BF),
    ("q_ref", (S, D), BF),
    ("scores_ref", (S, S), F32),
    ("dscores_ref", (S, S), F32),
    ("dbt_ref", (S, S), F32),
    ("dct_ref", (S, S), F32),
    ("e_ref", (H, S, S), BF),
    ("f_ref", (H, S, S), BF),
    ("rs_ref", (H, 2, S, S), BF),
    ("rr_ref", (H, 2, S, S), BF),
    ("ls_ref", (H, 2, S, S), BF),
    ("lr_ref", (H, 2, S, S), BF),
    ("ds_ref", (H, S, S), BF),
    ("dr_ref", (H, S, S), BF),
    ("us_ref", (H, S, S), BF),
    ("ur_ref", (H, S, S), BF),
    ("mul_ref", (4, H, S), F32),
    ("dconv_ref", (S + 16, W2), F32),
    ("gpad_ref", (S + 8, W2), F32),
    ("gr_ref", (S, W2), BF),
    ("rim_ref", (8, W2), F32),
    ("sa_ref", (NY, ROWS, W2), BF),
    ("ra_ref", (NY, ROWS, W2), BF),
    ("sb_ref", (NY - 1, ROWS, W2), BF),
    ("rb_ref", (NY - 1, ROWS, W2), BF),
    ("t_ref", (ROWS, W2), F32),
    ("sc_ref", (NX - 1, PX, W2), BF),
    ("rc_ref", (NX - 1, PX, W2), BF),
    ("pz_ref", (PX, W2), F32),
    ("sd_ref", (NZ - 1, PZ, W2), BF),
    ("rd_ref", (NZ - 1, PZ, W2), BF),
    ("fin_ref", (PZ, W2), BF),
    ("ma_ref", (8, W2), F32),
    ("mra_ref", (8, W2), F32),
    ("mb_ref", (NY, 8, W2), F32),
    ("mc_ref", (NX, 8, W2), F32),
    ("mrd_ref", (NZ, 8, W2), F32),
)
SEMAPHORES = (
    ("here_sem", (6,)),
    ("w_sem", (2, 10)),
    ("dec_sem", (2, NZ - 1)),
    ("r_sem", (2, H)),
    ("l_sem", (2, H)),
    ("d_sem2", (2, H)),
    ("u_sem", (2, H)),
    ("rim_sem", (2, 1)),
    ("a_sem", (2, NY)),
    ("b_sem", (2, NY - 1)),
    ("c_sem", (2, NX - 1)),
    ("d_sem", (2, NZ - 1)),
    ("e_sem", (2, NZ - 1)),
    ("f_sem", (2, NX - 1)),
    ("ma_sem", (2, 1)),
    ("mb_sem", (2, NY - 1)),
    ("mc_sem", (2, NX - 1)),
    ("md_sem", (2, NZ - 1)),
)


def layer_kernel(*refs):
    names = list(INPUTS) + [o[0] for o in OUTPUTS] + [b[0] for b in BUFFERS]
    names += [m[0] for m in SEMAPHORES]
    run_layer(**dict(zip(names, refs)))


def run_layer(
    w_ref, tok_hbm, cw_ref, cb_ref, v_hbm, raw_ref, bias_ref, alog_ref, skip_ref, g_hbm, out_hbm,
    gv_hbm, gtok_hbm, graw_ref, all_ref, sums_ref, full_ref, halo_ref, tok_ref, v_ref, g_ref,
    out_ref, gv_ref, gtok_ref, decs_ref, pad_ref, conv_ref, b_ref, c_ref, cum_ref, dt_ref,
    sig_ref, rate_ref, skipt_ref, dcum_ref, ddt_ref, dskip_ref, dgrow_ref, dew_ref, ddec_ref,
    yin_ref, dvin_ref, s_ref, de_ref, down_ref, ew_ref, u_ref, q_ref, scores_ref, dscores_ref,
    dbt_ref, dct_ref, e_ref, f_ref, rs_ref, rr_ref, ls_ref, lr_ref, ds_ref, dr_ref, us_ref,
    ur_ref, mul_ref, dconv_ref, gpad_ref, gr_ref, rim_ref, sa_ref, ra_ref, sb_ref, rb_ref, t_ref,
    sc_ref, rc_ref, pz_ref, sd_ref, rd_ref, fin_ref, ma_ref, mra_ref, mb_ref, mc_ref, mrd_ref,
    here_sem, w_sem, dec_sem, r_sem, l_sem, d_sem2, u_sem, rim_sem, a_sem, b_sem, c_sem, d_sem,
    e_sem, f_sem, ma_sem, mb_sem, mc_sem, md_sem,
):
    k = lax.axis_index("ctx")
    f = lax.axis_index("fsdp")
    y, c = f // 2, f % 2
    x, z = k // NZ, k % NZ
    up = ((y + 1) % NY) * 2 + c
    down = ((y + NY - 1) % NY) * 2 + c
    far = ((y + 2) % NY) * 2 + c
    nxt = (k + 1) % CTX
    prv = (k + CTX - 1) % CTX
    sib = {"fsdp": y * 2 + (1 - c)}

    def at_y(d):
        return (y + d) % NY

    def at_x(d):
        return (x + d) % NX

    def at_z(d):
        return (z + d) % NZ

    def y_dev(d):
        return {"fsdp": at_y(d) * 2 + c}

    def x_dev(d):
        return {"ctx": at_x(d) * NZ + z}

    def z_dev(d):
        return {"ctx": x * NZ + at_z(d)}

    def sems(s):
        return (s.at[0], s.at[1])

    loads = [
        pltpu.make_async_copy(src.at[0], dst, here_sem.at[i])
        for i, (src, dst) in enumerate(((tok_hbm, tok_ref), (v_hbm, v_ref), (g_hbm, g_ref)))
    ]
    for copy in loads:
        copy.start()
    row = [z_dev(d) for d in range(1, NZ)]
    partners = [sib, {"ctx": nxt}, {"ctx": prv}]
    partners += [y_dev(d) for d in range(1, NY)]
    partners += [x_dev(d) for d in range(1, NX)]
    partners += row
    greet(partners)

    half = ROWS // 2

    def rows(owner, first=0, size=ROWS):
        return full_ref.at[pl.ds(pl.multiple_of(owner * ROWS + first, half), size), :]

    ws = sems(w_sem)
    to_up = remote(w_ref, rows(f), ws, 0, fsdp=up)
    to_down = remote(w_ref, rows(f), ws, 1, fsdp=down)
    to_sib = remote(w_ref, rows(f), ws, 2, **sib)
    halo = remote(tok_hbm.at[0, S - 16 : S, :], halo_ref, ws, 3, ctx=nxt)
    to_up.start()
    to_down.start()
    to_sib.start()
    halo.start()
    full_ref[pl.ds(pl.multiple_of(f * ROWS, ROWS), ROWS), :] = w_ref[...]
    raw, dt, rate = steps_of(raw_ref[0], bias_ref[...], alog_ref[...])
    r_id = lax.broadcasted_iota(jnp.int32, (S, S), 0)
    c_id = lax.broadcasted_iota(jnp.int32, (S, S), 1)
    dt_ref[...] = dt
    rate_ref[...] = rate
    sig_ref[...] = jax.nn.sigmoid(raw)
    skipt_ref[...] = by_head(skip_ref[...])
    cum = dot(-dt * rate, (r_id <= c_id).astype(F32), precision=HIGH)
    cum_ref[...] = cum
    decs_ref[z] = jnp.broadcast_to(jnp.exp(cum[:, S - 1 : S]), (H, S))
    decs = [
        remote(decs_ref.at[z], decs_ref.at[z], sems(dec_sem), d - 1, **row[d - 1])
        for d in range(1, NZ)
    ]
    for copy in decs:
        copy.start()
    to_up.wait_recv()
    on_up = remote(rows(down, 0, half), rows(down, 0, half), ws, 4, fsdp=up)
    on_up.start()
    sib_down = remote(rows(down), rows(down), ws, 6, **sib)
    sib_down.start()
    to_down.wait_recv()
    on_down = remote(rows(up, half, half), rows(up, half, half), ws, 5, fsdp=down)
    on_down.start()
    sib_up = remote(rows(up), rows(up), ws, 7, **sib)
    sib_up.start()
    on_up.wait_recv()
    sib_a = remote(rows(far, 0, half), rows(far, 0, half), ws, 8, **sib)
    sib_a.start()
    on_down.wait_recv()
    sib_b = remote(rows(far, half, half), rows(far, half, half), ws, 9, **sib)
    sib_b.start()
    for copy in loads:
        copy.wait()
    for copy in [halo] + decs:
        copy.wait_recv()
    before = jnp.ones((H, S), F32)
    after = jnp.ones((H, S), F32)
    for i in range(NZ):
        d = decs_ref[i]
        before = before * jnp.where(i < z, d, 1.0)
        after = after * jnp.where(i > z, d, 1.0)
    mine = decs_ref[z]
    mul_ref[0] = before
    mul_ref[1] = after
    mul_ref[2] = mine
    mul_ref[3] = before * mine * after
    dscores_ref[...] = jnp.zeros_like(dscores_ref)
    dbt_ref[...] = jnp.zeros_like(dbt_ref)
    dct_ref[...] = jnp.zeros_like(dct_ref)
    for copy in (to_sib, sib_down, sib_up, sib_a, sib_b):
        copy.wait_recv()

    rim_rows = dot(halo_ref[...], full_ref[...])[8:16, :]
    pad_ref[0:8, :] = jnp.where(k > 0, rim_rows, jnp.zeros_like(rim_rows))
    pad_ref[8:, :] = dot(tok_ref[...], full_ref[...])
    conv = cb_ref[...] + cw_ref[0:1, :] * pad_ref[5 : 5 + S, :]
    for tap in range(1, 4):
        conv = conv + cw_ref[tap : tap + 1, :] * pad_ref[5 + tap : 5 + tap + S, :]
    conv_ref[...] = conv
    act = conv * jax.nn.sigmoid(conv)
    b_ref[...] = act[:, :S].astype(BF)
    c_ref[...] = act[:, S:].astype(BF)
    scores_ref[...] = dot(c_ref[...], b_ref[...], 1, 1)
    mask = r_id >= c_id
    eye = r_id == c_id

    def at(h):
        return pl.ds(pl.multiple_of(h * S, S), S)

    def prep(h):
        one = pl.ds(h, 1)
        cum_r = cum_ref[one, :]
        falling = jnp.broadcast_to(cum_r, (S, S)).T
        down_ref[h] = falling
        ew = jnp.exp(cum_r[:, S - 1 : S] - cum_r) * dt_ref[one, :]
        ew = jnp.broadcast_to(ew, (S, S)).T
        ew_ref[h] = ew
        u = (ew * v_ref[:, at(h)].astype(F32)).astype(BF)
        u_ref[:, at(h)] = u
        s_ref[h] = dot(b_ref[...], u, 0, 0)
        q = (jnp.exp(falling) * g_ref[:, at(h)].astype(F32)).astype(BF)
        q_ref[:, at(h)] = q
        de_ref[h] = dot(c_ref[...], q, 0, 0)

    def mix(h):
        one = pl.ds(h, 1)
        dt_r = dt_ref[one, :]
        gap = down_ref[h] - cum_ref[one, :]
        grid = jnp.where(mask, jnp.exp(jnp.where(mask, gap, 0.0)), 0.0)
        v = v_ref[:, at(h)]
        g = g_ref[:, at(h)]
        skip = skipt_ref[one, :]
        a1 = scores_ref[...] * grid
        weight = (a1 * dt_r).astype(BF)
        yin_ref[:, at(h)] = dot(weight, v) + skip * v.astype(F32)
        dvin_ref[:, at(h)] = dot(weight, g, 0, 0) + skip * g.astype(F32)
        dm = dot(g, v, 1, 1)
        dskip_ref[one, :] = jnp.sum(jnp.where(eye, dm, 0.0), axis=0, keepdims=True)
        xx = dm * a1
        ddt_ref[one, :] = jnp.sum(xx, axis=0, keepdims=True)
        ww = xx * dt_r
        dcum_ref[one, :] = jnp.sum(ww.T - ww, axis=0, keepdims=True)
        return dm * (grid * dt_r)

    def post(h):
        one = pl.ds(h, 1)
        e = e_ref[h]
        f = f_ref[h]
        ce = dot(c_ref[...], e)
        bf = dot(b_ref[...], f)
        out_ref[:, at(h)] = (yin_ref[:, at(h)] + jnp.exp(down_ref[h]) * ce).astype(BF)
        gv_ref[:, at(h)] = (dvin_ref[:, at(h)] + ew_ref[h] * bf).astype(BF)
        dgrow_ref[one, :] = row_sums(g_ref[:, at(h)].astype(F32) * ce)
        dew_ref[one, :] = row_sums(v_ref[:, at(h)].astype(F32) * bf)
        ddec_ref[one, :] = jnp.sum(e.astype(F32) * f.astype(F32), axis=0, keepdims=True)
        return dot(q_ref[:, at(h)], e, 1, 1), dot(u_ref[:, at(h)], f, 1, 1)

    def go_right(i):
        return remote(rs_ref.at[i], rr_ref.at[i], sems(r_sem), i, **z_dev(1))

    def go_left(i):
        return remote(ls_ref.at[i], lr_ref.at[i], sems(l_sem), i, **z_dev(NZ - 1))

    def go_below(i):
        return remote(ds_ref.at[i], dr_ref.at[i], sems(d_sem2), i, **x_dev(1))

    def go_above(i):
        return remote(us_ref.at[i], ur_ref.at[i], sems(u_sem), i, **x_dev(NX - 1))

    def factor(which, i):
        return mul_ref[which, pl.ds(i, 1), :]

    def arrive(i, first, copy, land):
        @pl.when(first)
        def _():
            land[i] = jnp.zeros(land.shape[1:], BF)

        @pl.when(jnp.logical_not(first))
        def _():
            copy(i).wait_recv()

    def to_right(i):
        arrive(i, z == 0, go_right, rr_ref)

        @pl.when(z < NZ - 1)
        def _():
            rs_ref[i, 0] = (factor(2, i) * rr_ref[i, 0].astype(F32) + s_ref[i]).astype(BF)
            rs_ref[i, 1] = (rr_ref[i, 1].astype(F32) + factor(0, i) * de_ref[i]).astype(BF)
            go_right(i).start()

    def to_left(i):
        arrive(i, z == NZ - 1, go_left, lr_ref)

        @pl.when(z > 0)
        def _():
            ls_ref[i, 0] = (lr_ref[i, 0].astype(F32) + factor(1, i) * s_ref[i]).astype(BF)
            ls_ref[i, 1] = (factor(2, i) * lr_ref[i, 1].astype(F32) + de_ref[i]).astype(BF)
            go_left(i).start()

    def to_below(i):
        arrive(i, x == 0, go_below, dr_ref)
        entering = dr_ref[i].astype(F32)
        inside = rr_ref[i, 0].astype(F32)
        e_ref[i] = (factor(0, i) * entering + inside).astype(BF)

        @pl.when(x < NX - 1)
        def _():
            total = lr_ref[i, 0].astype(F32) + factor(1, i) * (factor(2, i) * inside + s_ref[i])
            ds_ref[i] = (factor(3, i) * entering + total).astype(BF)
            go_below(i).start()

    def to_above(i):
        arrive(i, x == NX - 1, go_above, ur_ref)
        entering = ur_ref[i].astype(F32)
        inside = lr_ref[i, 1].astype(F32)
        f_ref[i] = (factor(1, i) * entering + inside).astype(BF)

        @pl.when(x > 0)
        def _():
            total = rr_ref[i, 1].astype(F32) + factor(0, i) * (factor(2, i) * inside + de_ref[i])
            us_ref[i] = (factor(3, i) * entering + total).astype(BF)
            go_above(i).start()

    late = jnp.maximum(z, NZ - 1 - z)
    starts = (z * SKEW, (NZ - 1 - z) * SKEW, (late + x) * SKEW, (late + NX - 1 - x) * SKEW)
    lag = jnp.maximum(starts[2], starts[3])
    lag = lag + lag % 2

    def turns(t):
        for start, turn in zip(starts, (to_right, to_left, to_below, to_above)):
            i = t - start

            @pl.when(jnp.logical_and(i >= 0, i < H))
            def _():
                turn(i)

    def slots(pair, _):
        h = 2 * pair

        @pl.when(h < H)
        def _():
            prep(h)
            prep(h + 1)

        turns(h)

        @pl.when(h < H)
        def _():
            dscores_ref[...] += mix(h) + mix(h + 1)

        turns(h + 1)
        i = h - lag

        @pl.when(jnp.logical_and(i >= 0, i < H))
        def _():
            dc0, db0 = post(i)
            dc1, db1 = post(i + 1)
            dct_ref[...] += dc0 + dc1
            dbt_ref[...] += db0 + db1

        return 0

    lax.fori_loop(0, (H + (NZ + NX - 2) * SKEW + 2) // 2, slots, 0)

    stores = [
        pltpu.make_async_copy(out_ref, out_hbm.at[0], here_sem.at[3]),
        pltpu.make_async_copy(gv_ref, gv_hbm.at[0], here_sem.at[4]),
    ]
    for copy in stores:
        copy.start()

    ds = dscores_ref[...].astype(BF)
    dct = dct_ref[...] + dot(ds, b_ref[...])
    dbt = dbt_ref[...] + dot(ds, c_ref[...], 0, 0)
    conv = conv_ref[...]
    sig = jax.nn.sigmoid(conv)
    slope = sig * (1.0 + conv * (1.0 - sig))
    dconv_ref[0:8, :] = jnp.zeros((8, W2), F32)
    dconv_ref[8 + S :, :] = jnp.zeros((8, W2), F32)
    dconv_ref[8 : 8 + S, 0:S] = dbt * slope[:, :S]
    dconv_ref[8 : 8 + S, S:] = dct * slope[:, S:]
    grads = cw_ref[3:4, :] * dconv_ref[0 : 8 + S, :]
    for tap in range(3):
        grads = grads + cw_ref[tap : tap + 1, :] * dconv_ref[3 - tap : 3 - tap + 8 + S, :]
    gpad_ref[...] = grads
    rim = remote(gpad_ref.at[0:8, :], rim_ref, sems(rim_sem), 0, ctx=prv)
    rim.start()

    cum = cum_ref[...]
    dt = dt_ref[...]
    rate = rate_ref[...]
    tail = jnp.exp(cum[:, S - 1 : S] - cum)
    dew = dew_ref[...]
    pull = dew * tail * dt
    at_last = jnp.sum(pull, axis=1, keepdims=True) + jnp.sum(
        ddec_ref[...] * mul_ref[2], axis=1, keepdims=True
    )
    lanes = lax.broadcasted_iota(jnp.int32, (H, S), 1)
    dcum = dcum_ref[...] + dgrow_ref[...] * jnp.exp(cum) - pull
    dcum = dcum + jnp.where(lanes == S - 1, at_last, 0.0)
    dld = dot(dcum, mask.astype(F32), precision=HIGH)
    ddt = ddt_ref[...] + dew * tail - rate * dld
    graw = ddt * sig_ref[...]
    graw_ref[0] = graw
    ma_ref[...] = jnp.zeros_like(ma_ref)
    ma_ref[5:6, 0:H] = row_sums(graw)
    ma_ref[6:7, 0:H] = row_sums(-dt * rate * dld)
    ma_ref[7:8, 0:H] = row_sums(dskip_ref[...])
    dconv = dconv_ref[8 : 8 + S, :]
    for tap in range(4):
        ma_ref[tap : tap + 1, :] = jnp.sum(
            dconv * pad_ref[5 + tap : 5 + tap + S, :], axis=0, keepdims=True
        )
    ma_ref[4:5, :] = jnp.sum(dconv, axis=0, keepdims=True)

    m_a = remote(ma_ref, mra_ref, sems(ma_sem), 0, **sib)
    m_a.start()
    rim.wait_recv()
    rest = jnp.where(k < CTX - 1, rim_ref[...], jnp.zeros_like(rim_ref))
    gr_ref[0 : S - 8, :] = gpad_ref[8:S, :].astype(BF)
    gr_ref[S - 8 : S, :] = (gpad_ref[S : S + 8, :] + rest).astype(BF)
    gr = gr_ref[...]

    def term(row):
        block = tok_ref[:, pl.ds(pl.multiple_of(row * ROWS, ROWS), ROWS)]
        return dot(block, gr, 0, 0)

    order = (2, 1, 3, 0)
    copies = {}
    for d in order:
        sa_ref[d] = term(at_y(d) * 2 + (1 - c)).astype(BF)
        copies[d] = remote(sa_ref.at[d], ra_ref.at[d], sems(a_sem), d, **sib)
        copies[d].start()
    m_a.wait_recv()
    low = jnp.where(c == 0, ma_ref[...], mra_ref[...])
    high = jnp.where(c == 0, mra_ref[...], ma_ref[...])
    mb_ref[y] = low + high
    m_b = [remote(mb_ref.at[y], mb_ref.at[y], sems(mb_sem), d - 1, **y_dev(d)) for d in range(1, NY)]
    for copy in m_b:
        copy.start()
    to_y = {}
    for d in order:
        mine = term(at_y(d) * 2 + c)
        copies[d].wait_recv()
        mine = mine + ra_ref[d].astype(F32)
        if d:
            sb_ref[d - 1] = mine.astype(BF)
            to_y[d] = remote(sb_ref.at[d - 1], rb_ref.at[d - 1], sems(b_sem), d - 1, **y_dev(d))
            to_y[d].start()
        else:
            t_ref[...] = mine
    for i in range(D // 1024):
        cols = slice(i * 1024, i * 1024 + 1024)
        gtok_ref[:, cols] = dot(gr, full_ref[cols, :], 1, 1).astype(BF)
    stores.append(pltpu.make_async_copy(gtok_ref, gtok_hbm.at[0], here_sem.at[5]))
    stores[-1].start()
    for copy in m_b:
        copy.wait_recv()
    mc_ref[x] = mb_ref[0] + mb_ref[1] + mb_ref[2] + mb_ref[3]
    m_c = [remote(mc_ref.at[x], mc_ref.at[x], sems(mc_sem), d - 1, **x_dev(d)) for d in range(1, NX)]
    for copy in m_c:
        copy.start()
    for d in (1, 3, 2):
        to_y[d].wait_recv()
        t_ref[...] += rb_ref[d - 1].astype(F32)
    px = PX
    to_x = {}
    for d in (2, 1, 3):
        sc_ref[d - 1] = t_ref[pl.ds(pl.multiple_of(at_x(d) * px, px), px), :].astype(BF)
        to_x[d] = remote(sc_ref.at[d - 1], rc_ref.at[d - 1], sems(c_sem), d - 1, **x_dev(d))
        to_x[d].start()
    for copy in m_c:
        copy.wait_recv()
    mrd_ref[z] = mc_ref[0] + mc_ref[1] + mc_ref[2] + mc_ref[3]
    m_d = [remote(mrd_ref.at[z], mrd_ref.at[z], sems(md_sem), d - 1, **z_dev(d)) for d in range(1, NZ)]
    for copy in m_d:
        copy.start()
    acc = t_ref[pl.ds(pl.multiple_of(x * px, px), px), :]
    for d in (1, 3, 2):
        to_x[d].wait_recv()
        acc = acc + rc_ref[d - 1].astype(F32)
    pz_ref[...] = acc
    pzr = PZ
    to_z = {}
    for d in (4, 3, 5, 2, 6, 1, 7):
        sd_ref[d - 1] = pz_ref[pl.ds(pl.multiple_of(at_z(d) * pzr, pzr), pzr), :].astype(BF)
        to_z[d] = remote(sd_ref.at[d - 1], rd_ref.at[d - 1], sems(d_sem), d - 1, **z_dev(d))
        to_z[d].start()
    acc = pz_ref[pl.ds(pl.multiple_of(z * pzr, pzr), pzr), :]
    for d in (1, 7, 2, 6, 3, 5, 4):
        to_z[d].wait_recv()
        acc = acc + rd_ref[d - 1].astype(F32)
    fin_ref[...] = acc.astype(BF)

    def piece(xx, first, size):
        return all_ref.at[pl.ds(pl.multiple_of(xx * px + first, pzr), size), :]

    done = [
        remote(fin_ref, piece(x, z * pzr, pzr), sems(e_sem), d - 1, **z_dev(d))
        for d in (4, 3, 5, 2, 6, 1, 7)
    ]
    for copy in done:
        copy.start()
    all_ref[pl.ds(pl.multiple_of(x * px + z * pzr, pzr), pzr), :] = fin_ref[...]
    for copy in m_d:
        copy.wait_recv()
    total = mrd_ref[0]
    for i in range(1, NZ):
        total = total + mrd_ref[i]
    sums_ref[...] = total
    for copy in done:
        copy.wait_recv()
    last = [
        remote(piece(x, 0, px), piece(x, 0, px), sems(f_sem), d - 1, **x_dev(d)) for d in (2, 1, 3)
    ]
    for copy in last:
        copy.start()
    for copy in last:
        copy.wait_recv()
    sent = [rim, m_a] + m_b + m_c + m_d + done + last
    sent += list(copies.values()) + list(to_y.values()) + list(to_x.values()) + list(to_z.values())
    for copy in sent:
        copy.wait_send()

    def drain(i, _):
        for here, copy in (
            (z < NZ - 1, go_right), (z > 0, go_left), (x < NX - 1, go_below), (x > 0, go_above)
        ):
            @pl.when(here)
            def _():
                copy(i).wait_send()

        return 0

    lax.fori_loop(0, H, drain, 0)
    sent = [to_up, to_down, to_sib, halo, on_up, on_down, sib_down, sib_up, sib_a, sib_b]
    for copy in sent + decs:
        copy.wait_send()
    for copy in stores:
        copy.wait()


def run_all(*args):
    anywhere = pl.BlockSpec(memory_space=pl.ANY)
    return pl.pallas_call(
        layer_kernel,
        out_shape=tuple(jax.ShapeDtypeStruct(o[1], o[2]) for o in OUTPUTS),
        in_specs=[anywhere if name.endswith("_hbm") else VMEM for name in INPUTS],
        out_specs=tuple(VMEM if o[3] else anywhere for o in OUTPUTS),
        scratch_shapes=[pltpu.VMEM(b[1], b[2]) for b in BUFFERS]
        + [pltpu.SemaphoreType.DMA(m[1]) for m in SEMAPHORES],
        compiler_params=pltpu.CompilerParams(
            collective_id=0, has_side_effects=True, vmem_limit_bytes=BIG
        ),
        name="ssm_layer",
    )(*args)


def last_kernel(
    out_ref, gv_ref, gtok_ref, graw_ref, all_ref, sums_ref,
    out_to, gv_to, gtok_to, graw_to, gw_ref, gcw_ref, gcb_ref, gbias_ref, galog_ref, gskip_ref,
    hold_ref, sem,
):
    pairs = ((gv_ref, gv_to), (out_ref, out_to), (gtok_ref, gtok_to))
    halves = [(n, r) for n in range(3) for r in (slice(0, S // 2), slice(S // 2, S))]
    fetch = [
        pltpu.make_async_copy(pairs[n][0].at[0, r, :], hold_ref.at[n, r, :], sem.at[0, i])
        for i, (n, r) in enumerate(halves)
    ]
    put = [
        pltpu.make_async_copy(hold_ref.at[n, r, :], pairs[n][1].at[0, r, :], sem.at[1, i])
        for i, (n, r) in enumerate(halves)
    ]
    for copy in fetch:
        copy.start()
    for first, second in zip(fetch, put):
        first.wait()
        second.start()
    graw_to[...] = graw_ref[...]
    gw_ref[...] = all_ref[...].astype(F32)
    gcw_ref[...] = sums_ref[0:4, :]
    gcb_ref[...] = sums_ref[4:5, :]
    gbias_ref[...] = sums_ref[5:6, 0:H]
    galog_ref[...] = sums_ref[6:7, 0:H]
    gskip_ref[...] = sums_ref[7:8, 0:H]
    for copy in put:
        copy.wait()


def hand_out(*args):
    head = jax.ShapeDtypeStruct((1, H), F32)
    anywhere = pl.BlockSpec(memory_space=pl.ANY)
    wide = jax.ShapeDtypeStruct((1, S, D), BF)
    return pl.pallas_call(
        last_kernel,
        out_shape=(
            wide, wide, wide,
            jax.ShapeDtypeStruct((1, H, S), F32),
            jax.ShapeDtypeStruct((ROWS, W2), F32),
            jax.ShapeDtypeStruct((4, W2), F32),
            jax.ShapeDtypeStruct((1, W2), F32),
            head, head, head,
        ),
        in_specs=[anywhere] * 3 + [VMEM] * 3,
        out_specs=(anywhere,) * 3 + (VMEM,) * 7,
        scratch_shapes=[pltpu.VMEM((3, S, D), BF), pltpu.SemaphoreType.DMA((2, 6))],
        compiler_params=pltpu.CompilerParams(vmem_limit_bytes=BIG),
        name="hand_out",
    )(*args)


def body(layer_in, w_bc, conv_w, conv_b, ssm_in, dt_raw, dt_bias, a_log, skip_scale, grad_out):
    made = run_all(
        w_bc, layer_in, conv_w, conv_b[None], ssm_in, jnp.swapaxes(dt_raw, 1, 2), dt_bias[None],
        a_log[None], skip_scale[None], grad_out,
    )
    out, gv, gtok, graw, gw, gcw, gcb, gbias, galog, gskip = hand_out(*made)
    return (
        out, gv, gtok, jnp.swapaxes(graw, 1, 2), gw, gcw, gcb[0], gbias[0], galog[0], gskip[0]
    )


def solution(mesh):
    split = P("fsdp", "ctx", None)
    in_specs = (
        split, P("fsdp", None), P(), P(), split, split, P(), P(), P(), split,
    )
    out_specs = (
        split, split, split, split, P("fsdp", None), P(), P(), P(), P(), P(),
    )
    return jax.shard_map(body, mesh=mesh, in_specs=in_specs, out_specs=out_specs, check_vma=False)
```

```python
import functools

import jax
import jax.numpy as jnp
from jax import lax
from jax.experimental import pallas as pl
from jax.experimental.pallas import tpu as pltpu
from jax.sharding import PartitionSpec as P

BF = jnp.bfloat16
F32 = jnp.float32
MESH = pl.DeviceIdType.MESH
HIGH = lax.Precision.HIGHEST
VMEM = pl.BlockSpec(memory_space=pltpu.VMEM)
BIG = 60 * 1024 * 1024

H = 32
S = 128
D = 4096
W2 = 256
ROWS = 512
NX, NZ, NY, NC = 4, 8, 4, 2
CTX = NX * NZ


def dot(a, b, ca=1, cb=0, precision=None):
    return lax.dot_general(
        a, b, (((ca,), (cb,)), ((), ())), preferred_element_type=F32, precision=precision
    )


def tri_upper():
    r = lax.broadcasted_iota(jnp.int32, (S, S), 0)
    c = lax.broadcasted_iota(jnp.int32, (S, S), 1)
    return r, c


def remote(src, dst, sems, slot, **where):
    return pltpu.make_async_remote_copy(
        src_ref=src,
        dst_ref=dst,
        send_sem=sems[0].at[slot],
        recv_sem=sems[1].at[slot],
        device_id=where,
        device_id_type=MESH,
    )


def greet(partners):
    barrier = pltpu.get_barrier_semaphore()
    for who in partners:
        pl.semaphore_signal(barrier, inc=1, device_id=who, device_id_type=MESH)
    pl.semaphore_wait(barrier, len(partners))


def by_head(row):
    return jnp.broadcast_to(row, (S, H)).T


def steps_of(raw, bias, alog):
    x = raw + by_head(bias)
    dt = jnp.maximum(x, 0.0) + jnp.log1p(jnp.exp(-jnp.abs(x)))
    return x, dt, by_head(jnp.exp(alog))


def flip(tile):
    return tile.T


def row_sums(tile):
    return jnp.sum(tile.T, axis=0, keepdims=True)


SKEW = 5
SUB = 2
PIECES = H * SUB
PART = S // SUB
PX = ROWS // NX
PZ = PX // NZ

INPUTS = ("w_ref", "tok_hbm", "cw_ref", "cb_ref", "v_hbm", "raw_ref", "bias_ref", "alog_ref",
          "skip_ref", "g_hbm")
OUTPUTS = (
    ("out_hbm", (1, S, D), BF, False),
    ("gv_hbm", (1, S, D), BF, False),
    ("gtok_hbm", (1, S, D), BF, False),
    ("graw_ref", (1, H, S), F32, True),
    ("all_ref", (ROWS, W2), BF, True),
    ("sums_ref", (8, W2), F32, True),
)
BUFFERS = (
    ("full_ref", (D, W2), BF),
    ("tokx_ref", (16 + S, D), BF),
    ("v_ref", (S, D), BF),
    ("g_ref", (S, D), BF),
    ("out_ref", (S, D), BF),
    ("gv_ref", (S, D), BF),
    ("gtok_ref", (S, D), BF),
    ("decs_ref", (NZ, H, S), F32),
    ("pad_ref", (S + 8, W2), F32),
    ("conv_ref", (S, W2), F32),
    ("b_ref", (S, S), BF),
    ("c_ref", (S, S), BF),
    ("cum_ref", (H, S), F32),
    ("dt_ref", (H, S), F32),
    ("sig_ref", (H, S), F32),
    ("rate_ref", (H, S), F32),
    ("skipt_ref", (H, S), F32),
    ("dcum_ref", (H, S), F32),
    ("ddt_ref", (H, S), F32),
    ("dskip_ref", (H, S), F32),
    ("dgrow_ref", (H, S), F32),
    ("dew_ref", (H, S), F32),
    ("ddec_ref", (H, S), F32),
    ("yin_ref", (S, D), F32),
    ("dvin_ref", (S, D), F32),
    ("s_ref", (H, S, S), F32),
    ("de_ref", (H, S, S), F32),
    ("down_ref", (H, S, S), F32),
    ("ew_ref", (H, S, S), F32),
    ("u_ref", (S, D), BF),
    ("q_ref", (S, D), BF),
    ("scores_ref", (S, S), F32),
    ("dscores_ref", (S, S), F32),
    ("dbt_ref", (S, S), F32),
    ("dct_ref", (S, S), F32),
    ("e_ref", (H, S, S), BF),
    ("f_ref", (H, S, S), BF),
    ("rs_ref", (H, 2, S, S), BF),
    ("rr_ref", (H, 2, S, S), BF),
    ("ls_ref", (H, 2, S, S), BF),
    ("lr_ref", (H, 2, S, S), BF),
    ("ds_ref", (H, S, S), BF),
    ("dr_ref", (H, S, S), BF),
    ("us_ref", (H, S, S), BF),
    ("ur_ref", (H, S, S), BF),
    ("mul_ref", (4, H, S), F32),
    ("dconv_ref", (S + 16, W2), F32),
    ("gpad_ref", (S + 8, W2), F32),
    ("gr_ref", (S, W2), BF),
    ("gx_ref", (16 + S, W2), BF),
    ("rim_ref", (8, W2), F32),
    ("sa_ref", (NY, ROWS, W2), BF),
    ("ra_ref", (NY, ROWS, W2), BF),
    ("sb_ref", (NY - 1, ROWS, S), BF),
    ("rb_ref", (NY - 1, ROWS, S), BF),
    ("ta_ref", (ROWS, S), BF),
    ("rc_ref", (NX - 1, PX, S), BF),
    ("mx_ref", (NY, ROWS, S), BF),
    ("rx_ref", (NX - 1, NY, PX, S), BF),
    ("sy_ref", (NY - 1, PX, S), BF),
    ("ry_ref", (NY - 1, PX, S), BF),
    ("pz_ref", (PX, W2), F32),
    ("sd_ref", (NZ - 1, PZ, W2), BF),
    ("rd_ref", (NZ - 1, PZ, W2), BF),
    ("fin_ref", (PZ, W2), BF),
    ("ma_ref", (8, W2), F32),
    ("mra_ref", (8, W2), F32),
    ("mb_ref", (NY, 8, W2), F32),
    ("mc_ref", (NX, 8, W2), F32),
    ("mrd_ref", (NZ, 8, W2), F32),
)
SEMAPHORES = (
    ("here_sem", (6,)),
    ("w_sem", (2, 12)),
    ("dec_sem", (2, NZ - 1)),
    ("r_sem", (2, PIECES)),
    ("l_sem", (2, PIECES)),
    ("d_sem2", (2, PIECES)),
    ("u_sem", (2, PIECES)),
    ("rim_sem", (2, 1)),
    ("a_sem", (2, NY)),
    ("b_sem", (2, NY - 1)),
    ("c_sem", (2, NX - 1)),
    ("x_sem", (2, NY * (NX - 1))),
    ("y_sem", (2, NY - 1)),
    ("d_sem", (2, NZ - 1)),
    ("e_sem", (2, NZ - 1)),
    ("f_sem", (2, NX - 1)),
    ("ma_sem", (2, 1)),
    ("mb_sem", (2, NY - 1)),
    ("mc_sem", (2, NX - 1)),
    ("md_sem", (2, NZ - 1)),
)


def layer_kernel(*refs):
    names = list(INPUTS) + [o[0] for o in OUTPUTS] + [b[0] for b in BUFFERS]
    names += [m[0] for m in SEMAPHORES]
    run_layer(**dict(zip(names, refs)))


def run_layer(
    w_ref, tok_hbm, cw_ref, cb_ref, v_hbm, raw_ref, bias_ref, alog_ref, skip_ref, g_hbm, out_hbm,
    gv_hbm, gtok_hbm, graw_ref, all_ref, sums_ref, full_ref, tokx_ref, v_ref, g_ref, out_ref,
    gv_ref, gtok_ref, decs_ref, pad_ref, conv_ref, b_ref, c_ref, cum_ref, dt_ref, sig_ref,
    rate_ref, skipt_ref, dcum_ref, ddt_ref, dskip_ref, dgrow_ref, dew_ref, ddec_ref, yin_ref,
    dvin_ref, s_ref, de_ref, down_ref, ew_ref, u_ref, q_ref, scores_ref, dscores_ref, dbt_ref,
    dct_ref, e_ref, f_ref, rs_ref, rr_ref, ls_ref, lr_ref, ds_ref, dr_ref, us_ref, ur_ref,
    mul_ref, dconv_ref, gpad_ref, gr_ref, gx_ref, rim_ref, sa_ref, ra_ref, sb_ref, rb_ref,
    ta_ref, rc_ref, mx_ref, rx_ref, sy_ref, ry_ref, pz_ref, sd_ref, rd_ref, fin_ref, ma_ref,
    mra_ref, mb_ref, mc_ref, mrd_ref, here_sem, w_sem, dec_sem, r_sem, l_sem, d_sem2, u_sem,
    rim_sem, a_sem, b_sem, c_sem, x_sem, y_sem, d_sem, e_sem, f_sem, ma_sem, mb_sem, mc_sem,
    md_sem,
):
    k = lax.axis_index("ctx")
    f = lax.axis_index("fsdp")
    y, c = f // 2, f % 2
    x, z = k // NZ, k % NZ
    up = ((y + 1) % NY) * 2 + c
    down = ((y + NY - 1) % NY) * 2 + c
    far = ((y + 2) % NY) * 2 + c
    nxt = (k + 1) % CTX
    prv = (k + CTX - 1) % CTX
    sib = {"fsdp": y * 2 + (1 - c)}

    def at_y(d):
        return (y + d) % NY

    def at_x(d):
        return (x + d) % NX

    def at_z(d):
        return (z + d) % NZ

    def y_dev(d):
        return {"fsdp": at_y(d) * 2 + c}

    def x_dev(d):
        return {"ctx": at_x(d) * NZ + z}

    def z_dev(d):
        return {"ctx": x * NZ + at_z(d)}

    def sems(s):
        return (s.at[0], s.at[1])

    loads = [
        pltpu.make_async_copy(src.at[0], dst, here_sem.at[i])
        for i, (src, dst) in enumerate(((tok_hbm, tokx_ref.at[16 : 16 + S, :]), (v_hbm, v_ref), (g_hbm, g_ref)))
    ]
    for copy in loads:
        copy.start()
    row = [z_dev(d) for d in range(1, NZ)]
    partners = [sib, {"ctx": nxt}, {"ctx": prv}]
    partners += [y_dev(d) for d in range(1, NY)]
    partners += [x_dev(d) for d in range(1, NX)]
    partners += row
    greet(partners)

    half = ROWS // 2

    def rows(owner, first=0, size=ROWS):
        return full_ref.at[pl.ds(pl.multiple_of(owner * ROWS + first, half), size), :]

    ws = sems(w_sem)
    lower, upper = w_ref.at[0:half, :], w_ref.at[half:ROWS, :]
    up_a = remote(lower, rows(f, 0, half), ws, 0, fsdp=up)
    down_a = remote(upper, rows(f, half, half), ws, 1, fsdp=down)
    up_b = remote(upper, rows(f, half, half), ws, 10, fsdp=up)
    down_b = remote(lower, rows(f, 0, half), ws, 11, fsdp=down)
    to_sib = remote(w_ref, rows(f), ws, 2, **sib)
    halo = remote(tok_hbm.at[0, S - 16 : S, :], tokx_ref.at[0:16, :], ws, 3, ctx=nxt)
    for copy in (up_a, down_a, up_b, down_b, to_sib, halo):
        copy.start()
    full_ref[pl.ds(pl.multiple_of(f * ROWS, ROWS), ROWS), :] = w_ref[...]
    raw, dt, rate = steps_of(raw_ref[0], bias_ref[...], alog_ref[...])
    r_id = lax.broadcasted_iota(jnp.int32, (S, S), 0)
    c_id = lax.broadcasted_iota(jnp.int32, (S, S), 1)
    dt_ref[...] = dt
    rate_ref[...] = rate
    sig_ref[...] = jax.nn.sigmoid(raw)
    skipt_ref[...] = by_head(skip_ref[...])
    cum = dot(-dt * rate, (r_id <= c_id).astype(F32), precision=HIGH)
    cum_ref[...] = cum
    decs_ref[z] = jnp.broadcast_to(jnp.exp(cum[:, S - 1 : S]), (H, S))
    decs = [
        remote(decs_ref.at[z], decs_ref.at[z], sems(dec_sem), d - 1, **row[d - 1])
        for d in range(1, NZ)
    ]
    for copy in decs:
        copy.start()
    up_a.wait_recv()
    on_up = remote(rows(down, 0, half), rows(down, 0, half), ws, 4, fsdp=up)
    on_up.start()
    down_a.wait_recv()
    on_down = remote(rows(up, half, half), rows(up, half, half), ws, 5, fsdp=down)
    on_down.start()
    up_b.wait_recv()
    sib_down = remote(rows(down), rows(down), ws, 6, **sib)
    sib_down.start()
    down_b.wait_recv()
    sib_up = remote(rows(up), rows(up), ws, 7, **sib)
    sib_up.start()
    on_up.wait_recv()
    sib_a = remote(rows(far, 0, half), rows(far, 0, half), ws, 8, **sib)
    sib_a.start()
    on_down.wait_recv()
    sib_b = remote(rows(far, half, half), rows(far, half, half), ws, 9, **sib)
    sib_b.start()
    for copy in loads:
        copy.wait()
    for copy in [halo] + decs:
        copy.wait_recv()
    before = jnp.ones((H, S), F32)
    after = jnp.ones((H, S), F32)
    for i in range(NZ):
        d = decs_ref[i]
        before = before * jnp.where(i < z, d, 1.0)
        after = after * jnp.where(i > z, d, 1.0)
    mine = decs_ref[z]
    mul_ref[0] = before
    mul_ref[1] = after
    mul_ref[2] = mine
    mul_ref[3] = before * mine * after
    dscores_ref[...] = jnp.zeros_like(dscores_ref)
    dbt_ref[...] = jnp.zeros_like(dbt_ref)
    dct_ref[...] = jnp.zeros_like(dct_ref)
    for copy in (to_sib, sib_down, sib_up, sib_a, sib_b):
        copy.wait_recv()

    projected = dot(tokx_ref[...], full_ref[...])
    pad_ref[...] = projected[8:, :]
    pad_ref[0:8, :] = jnp.where(k > 0, pad_ref[0:8, :], jnp.zeros((8, W2), F32))
    conv = cb_ref[...] + cw_ref[0:1, :] * pad_ref[5 : 5 + S, :]
    for tap in range(1, 4):
        conv = conv + cw_ref[tap : tap + 1, :] * pad_ref[5 + tap : 5 + tap + S, :]
    conv_ref[...] = conv
    act = conv * jax.nn.sigmoid(conv)
    b_ref[...] = act[:, :S].astype(BF)
    c_ref[...] = act[:, S:].astype(BF)
    scores_ref[...] = dot(c_ref[...], b_ref[...], 1, 1)
    mask = r_id >= c_id
    eye = r_id == c_id

    def at(h):
        return pl.ds(pl.multiple_of(h * S, S), S)

    def prep(h):
        one = pl.ds(h, 1)
        cum_r = cum_ref[one, :]
        falling = jnp.broadcast_to(cum_r, (S, S)).T
        down_ref[h] = falling
        ew = jnp.exp(cum_r[:, S - 1 : S] - cum_r) * dt_ref[one, :]
        ew = jnp.broadcast_to(ew, (S, S)).T
        ew_ref[h] = ew
        u = (ew * v_ref[:, at(h)].astype(F32)).astype(BF)
        u_ref[:, at(h)] = u
        s_ref[h] = dot(b_ref[...], u, 0, 0)
        q = (jnp.exp(falling) * g_ref[:, at(h)].astype(F32)).astype(BF)
        q_ref[:, at(h)] = q
        de_ref[h] = dot(c_ref[...], q, 0, 0)

    def mix(h):
        one = pl.ds(h, 1)
        dt_r = dt_ref[one, :]
        gap = down_ref[h] - cum_ref[one, :]
        grid = jnp.where(mask, jnp.exp(jnp.where(mask, gap, 0.0)), 0.0)
        v = v_ref[:, at(h)]
        g = g_ref[:, at(h)]
        skip = skipt_ref[one, :]
        a1 = scores_ref[...] * grid
        weight = (a1 * dt_r).astype(BF)
        yin_ref[:, at(h)] = dot(weight, v) + skip * v.astype(F32)
        dvin_ref[:, at(h)] = dot(weight, g, 0, 0) + skip * g.astype(F32)
        dm = dot(g, v, 1, 1)
        dskip_ref[one, :] = jnp.sum(jnp.where(eye, dm, 0.0), axis=0, keepdims=True)
        xx = dm * a1
        ddt_ref[one, :] = jnp.sum(xx, axis=0, keepdims=True)
        ww = xx * dt_r
        dcum_ref[one, :] = jnp.sum(ww.T - ww, axis=0, keepdims=True)
        return dm * (grid * dt_r)

    def post(h):
        one = pl.ds(h, 1)
        e = e_ref[h]
        f = f_ref[h]
        ce = dot(c_ref[...], e)
        bf = dot(b_ref[...], f)
        out_ref[:, at(h)] = (yin_ref[:, at(h)] + jnp.exp(down_ref[h]) * ce).astype(BF)
        gv_ref[:, at(h)] = (dvin_ref[:, at(h)] + ew_ref[h] * bf).astype(BF)
        dgrow_ref[one, :] = row_sums(g_ref[:, at(h)].astype(F32) * ce)
        dew_ref[one, :] = row_sums(v_ref[:, at(h)].astype(F32) * bf)
        ddec_ref[one, :] = jnp.sum(e.astype(F32) * f.astype(F32), axis=0, keepdims=True)
        return dot(q_ref[:, at(h)], e, 1, 1), dot(u_ref[:, at(h)], f, 1, 1)

    def part(i):
        return i // SUB, pl.ds(pl.multiple_of((i % SUB) * PART, PART), PART)

    def both(ref, i):
        h, rr = part(i)
        return ref.at[h, :, rr, :]

    def single(ref, i):
        h, rr = part(i)
        return ref.at[h, rr, :]

    def go_right(i):
        return remote(both(rs_ref, i), both(rr_ref, i), sems(r_sem), i, **z_dev(1))

    def go_left(i):
        return remote(both(ls_ref, i), both(lr_ref, i), sems(l_sem), i, **z_dev(NZ - 1))

    def go_below(i):
        return remote(single(ds_ref, i), single(dr_ref, i), sems(d_sem2), i, **x_dev(1))

    def go_above(i):
        return remote(single(us_ref, i), single(ur_ref, i), sems(u_sem), i, **x_dev(NX - 1))

    def factor(which, h):
        return mul_ref[which, pl.ds(h, 1), :]

    def arrive(i, first, copy):
        @pl.when(jnp.logical_not(first))
        def _():
            copy(i).wait_recv()

    def to_right(i):
        h, p = part(i)
        arrive(i, z == 0, go_right)

        @pl.when(z < NZ - 1)
        def _():
            states = factor(2, h) * rr_ref[h, 0, p, :].astype(F32) + s_ref[h, p, :]
            rs_ref[h, 0, p, :] = states.astype(BF)
            sums = rr_ref[h, 1, p, :].astype(F32) + factor(0, h) * de_ref[h, p, :]
            rs_ref[h, 1, p, :] = sums.astype(BF)
            go_right(i).start()

    def to_left(i):
        h, p = part(i)
        arrive(i, z == NZ - 1, go_left)

        @pl.when(z > 0)
        def _():
            sums = lr_ref[h, 0, p, :].astype(F32) + factor(1, h) * s_ref[h, p, :]
            ls_ref[h, 0, p, :] = sums.astype(BF)
            states = factor(2, h) * lr_ref[h, 1, p, :].astype(F32) + de_ref[h, p, :]
            ls_ref[h, 1, p, :] = states.astype(BF)
            go_left(i).start()

    def to_below(i):
        h, p = part(i)
        arrive(i, x == 0, go_below)
        entering = dr_ref[h, p, :].astype(F32)
        inside = rr_ref[h, 0, p, :].astype(F32)
        e_ref[h, p, :] = (factor(0, h) * entering + inside).astype(BF)

        @pl.when(x < NX - 1)
        def _():
            total = factor(1, h) * (factor(2, h) * inside + s_ref[h, p, :])
            total = total + lr_ref[h, 0, p, :].astype(F32)
            ds_ref[h, p, :] = (factor(3, h) * entering + total).astype(BF)
            go_below(i).start()

    def to_above(i):
        h, p = part(i)
        arrive(i, x == NX - 1, go_above)
        entering = ur_ref[h, p, :].astype(F32)
        inside = lr_ref[h, 1, p, :].astype(F32)
        f_ref[h, p, :] = (factor(1, h) * entering + inside).astype(BF)

        @pl.when(x > 0)
        def _():
            total = factor(0, h) * (factor(2, h) * inside + de_ref[h, p, :])
            total = total + rr_ref[h, 1, p, :].astype(F32)
            us_ref[h, p, :] = (factor(3, h) * entering + total).astype(BF)
            go_above(i).start()

    for first, land in ((z == 0, rr_ref), (z == NZ - 1, lr_ref), (x == 0, dr_ref), (x == NX - 1, ur_ref)):
        @pl.when(first)
        def _():
            land[...] = jnp.zeros(land.shape, BF)

    late = jnp.maximum(z, NZ - 1 - z)
    starts = (z * SKEW, (NZ - 1 - z) * SKEW, (late + x) * SKEW, (late + NX - 1 - x) * SKEW)
    lag = (jnp.maximum(starts[2], starts[3]) + 2 * SUB - 1) // (2 * SUB)

    def turns(t):
        for start, turn in zip(starts, (to_right, to_left, to_below, to_above)):
            i = t - start

            @pl.when(jnp.logical_and(i >= 0, i < PIECES))
            def _():
                turn(i)

    def slots(n, _):
        h = 2 * n
        t = 2 * SUB * n
        todo = h < H

        @pl.when(todo)
        def _():
            prep(h)
            prep(h + 1)

        turns(t)

        @pl.when(todo)
        def _():
            dscores_ref[...] += mix(h)

        turns(t + 1)
        turns(t + 2)

        @pl.when(todo)
        def _():
            dscores_ref[...] += mix(h + 1)

        turns(t + 3)
        i = 2 * (n - lag)

        @pl.when(jnp.logical_and(i >= 0, i < H))
        def _():
            dc0, db0 = post(i)
            dc1, db1 = post(i + 1)
            dct_ref[...] += dc0 + dc1
            dbt_ref[...] += db0 + db1

        return 0

    most = ((NZ + NX - 2) * SKEW + 2 * SUB - 1) // (2 * SUB)
    lax.fori_loop(0, H // 2 + most, slots, 0)

    stores = [
        pltpu.make_async_copy(out_ref, out_hbm.at[0], here_sem.at[3]),
        pltpu.make_async_copy(gv_ref, gv_hbm.at[0], here_sem.at[4]),
    ]
    for copy in stores:
        copy.start()

    ds = dscores_ref[...].astype(BF)
    dct = dct_ref[...] + dot(ds, b_ref[...])
    dbt = dbt_ref[...] + dot(ds, c_ref[...], 0, 0)
    conv = conv_ref[...]
    sig = jax.nn.sigmoid(conv)
    slope = sig * (1.0 + conv * (1.0 - sig))
    dconv_ref[0:8, :] = jnp.zeros((8, W2), F32)
    dconv_ref[8 + S :, :] = jnp.zeros((8, W2), F32)
    dconv_ref[8 : 8 + S, 0:S] = dbt * slope[:, :S]
    dconv_ref[8 : 8 + S, S:] = dct * slope[:, S:]
    grads = cw_ref[3:4, :] * dconv_ref[0 : 8 + S, :]
    for tap in range(3):
        grads = grads + cw_ref[tap : tap + 1, :] * dconv_ref[3 - tap : 3 - tap + 8 + S, :]
    gpad_ref[...] = grads
    rim = remote(gpad_ref.at[0:8, :], rim_ref, sems(rim_sem), 0, ctx=prv)
    rim.start()
    gx_ref[...] = jnp.concatenate(
        [
            jnp.zeros((8, W2), F32),
            jnp.where(k > 0, gpad_ref[0:8, :], jnp.zeros((8, W2), F32)),
            gpad_ref[8:, :],
        ],
        axis=0,
    ).astype(BF)

    gx = gx_ref[...]

    def term(block):
        return dot(tokx_ref[:, pl.ds(pl.multiple_of(block * ROWS, ROWS), ROWS)], gx, 0, 0)

    def x_rows(d):
        return pl.ds(pl.multiple_of(at_x(d) * PX, PX), PX)

    order = (2, 1, 3, 0)
    copies = {}
    for d in order:
        sa_ref[d] = term(at_y(d) * 2 + (1 - c)).astype(BF)
        copies[d] = remote(sa_ref.at[d], ra_ref.at[d], sems(a_sem), d, **sib)
        copies[d].start()
    to_y, over_x = {}, {}
    for d in order:
        mine = term(at_y(d) * 2 + c)
        copies[d].wait_recv()
        mine = (mine + ra_ref[d].astype(F32)).astype(BF)
        if d:
            sb_ref[d - 1] = mine[:, :S]
            to_y[d] = remote(sb_ref.at[d - 1], rb_ref.at[d - 1], sems(b_sem), d - 1, **y_dev(d))
            to_y[d].start()
        else:
            ta_ref[...] = mine[:, :S]
        mx_ref[d] = mine[:, S:]
        for e in (2, 1, 3):
            over_x[e, d] = remote(
                mx_ref.at[d, x_rows(e), :], rx_ref.at[e - 1, d], sems(x_sem), (e - 1) * NY + d,
                **x_dev(e)
            )
            over_x[e, d].start()

    cum = cum_ref[...]
    dt = dt_ref[...]
    rate = rate_ref[...]
    tail = jnp.exp(cum[:, S - 1 : S] - cum)
    dew = dew_ref[...]
    pull = dew * tail * dt
    at_last = jnp.sum(pull, axis=1, keepdims=True) + jnp.sum(
        ddec_ref[...] * mul_ref[2], axis=1, keepdims=True
    )
    lanes = lax.broadcasted_iota(jnp.int32, (H, S), 1)
    dcum = dcum_ref[...] + dgrow_ref[...] * jnp.exp(cum) - pull
    dcum = dcum + jnp.where(lanes == S - 1, at_last, 0.0)
    dld = dot(dcum, mask.astype(F32), precision=HIGH)
    ddt = ddt_ref[...] + dew * tail - rate * dld
    graw = ddt * sig_ref[...]
    graw_ref[0] = graw
    ma_ref[...] = jnp.zeros_like(ma_ref)
    ma_ref[5:6, 0:H] = row_sums(graw)
    ma_ref[6:7, 0:H] = row_sums(-dt * rate * dld)
    ma_ref[7:8, 0:H] = row_sums(dskip_ref[...])
    dconv = dconv_ref[8 : 8 + S, :]
    for tap in range(4):
        ma_ref[tap : tap + 1, :] = jnp.sum(
            dconv * pad_ref[5 + tap : 5 + tap + S, :], axis=0, keepdims=True
        )
    ma_ref[4:5, :] = jnp.sum(dconv, axis=0, keepdims=True)
    m_a = remote(ma_ref, mra_ref, sems(ma_sem), 0, **sib)
    m_a.start()
    rim.wait_recv()
    rest = jnp.where(k < CTX - 1, rim_ref[...], jnp.zeros_like(rim_ref))
    gr_ref[0 : S - 8, :] = gpad_ref[8:S, :].astype(BF)
    gr_ref[S - 8 : S, :] = (gpad_ref[S : S + 8, :] + rest).astype(BF)
    gr = gr_ref[...]
    m_a.wait_recv()
    low = jnp.where(c == 0, ma_ref[...], mra_ref[...])
    high = jnp.where(c == 0, mra_ref[...], ma_ref[...])
    mb_ref[y] = low + high
    m_b = [remote(mb_ref.at[y], mb_ref.at[y], sems(mb_sem), d - 1, **y_dev(d)) for d in range(1, NY)]
    for copy in m_b:
        copy.start()
    for i in range(D // 1024):
        cols = slice(i * 1024, i * 1024 + 1024)
        gtok_ref[:, cols] = dot(gr, full_ref[cols, :], 1, 1).astype(BF)
    stores.append(pltpu.make_async_copy(gtok_ref, gtok_hbm.at[0], here_sem.at[5]))
    stores[-1].start()
    own = pl.ds(pl.multiple_of(x * PX, PX), PX)
    to_y2 = {}
    for d in order:
        acc = mx_ref[d, own, :].astype(F32)
        for e in (1, 3, 2):
            over_x[e, d].wait_recv()
            acc = acc + rx_ref[e - 1, d].astype(F32)
        if d:
            sy_ref[d - 1] = acc.astype(BF)
            to_y2[d] = remote(sy_ref.at[d - 1], ry_ref.at[d - 1], sems(y_sem), d - 1, **y_dev(d))
            to_y2[d].start()
        else:
            pz_ref[:, S:] = acc
    acc = ta_ref[...].astype(F32)
    for d in (1, 3, 2):
        to_y[d].wait_recv()
        acc = acc + rb_ref[d - 1].astype(F32)
    ta_ref[...] = acc.astype(BF)
    to_x = {}
    for d in (2, 1, 3):
        to_x[d] = remote(
            ta_ref.at[x_rows(d), :], rc_ref.at[d - 1], sems(c_sem), d - 1, **x_dev(d)
        )
        to_x[d].start()
    for copy in m_b:
        copy.wait_recv()
    mc_ref[x] = mb_ref[0] + mb_ref[1] + mb_ref[2] + mb_ref[3]
    m_c = [remote(mc_ref.at[x], mc_ref.at[x], sems(mc_sem), d - 1, **x_dev(d)) for d in range(1, NX)]
    for copy in m_c:
        copy.start()
    acc = pz_ref[:, S:]
    for d in (1, 3, 2):
        to_y2[d].wait_recv()
        acc = acc + ry_ref[d - 1].astype(F32)
    pz_ref[:, S:] = acc
    acc = ta_ref[own, :].astype(F32)
    for d in (1, 3, 2):
        to_x[d].wait_recv()
        acc = acc + rc_ref[d - 1].astype(F32)
    pz_ref[:, :S] = acc
    px, pzr = PX, PZ
    to_z = {}
    for d in (4, 3, 5, 2, 6, 1, 7):
        sd_ref[d - 1] = pz_ref[pl.ds(pl.multiple_of(at_z(d) * pzr, pzr), pzr), :].astype(BF)
        to_z[d] = remote(sd_ref.at[d - 1], rd_ref.at[d - 1], sems(d_sem), d - 1, **z_dev(d))
        to_z[d].start()
    for copy in m_c:
        copy.wait_recv()
    mrd_ref[z] = mc_ref[0] + mc_ref[1] + mc_ref[2] + mc_ref[3]
    m_d = [remote(mrd_ref.at[z], mrd_ref.at[z], sems(md_sem), d - 1, **z_dev(d)) for d in range(1, NZ)]
    for copy in m_d:
        copy.start()
    acc = pz_ref[pl.ds(pl.multiple_of(z * pzr, pzr), pzr), :]
    for d in (1, 7, 2, 6, 3, 5, 4):
        to_z[d].wait_recv()
        acc = acc + rd_ref[d - 1].astype(F32)
    fin_ref[...] = acc.astype(BF)

    def piece(xx, first, size):
        return all_ref.at[pl.ds(pl.multiple_of(xx * px + first, pzr), size), :]

    done = [
        remote(fin_ref, piece(x, z * pzr, pzr), sems(e_sem), d - 1, **z_dev(d))
        for d in (4, 3, 5, 2, 6, 1, 7)
    ]
    for copy in done:
        copy.start()
    all_ref[pl.ds(pl.multiple_of(x * px + z * pzr, pzr), pzr), :] = fin_ref[...]
    for copy in m_d:
        copy.wait_recv()
    total = mrd_ref[0]
    for i in range(1, NZ):
        total = total + mrd_ref[i]
    sums_ref[...] = total
    for copy in done:
        copy.wait_recv()
    last = [
        remote(piece(x, 0, px), piece(x, 0, px), sems(f_sem), d - 1, **x_dev(d)) for d in (2, 1, 3)
    ]
    for copy in last:
        copy.start()
    for copy in last:
        copy.wait_recv()
    sent = [rim, m_a] + m_b + m_c + m_d + done + last
    sent += list(over_x.values()) + list(to_y2.values()) + list(copies.values()) + list(to_y.values()) + list(to_x.values()) + list(to_z.values())
    for copy in sent:
        copy.wait_send()

    def drain(i, _):
        for here, copy in (
            (z < NZ - 1, go_right), (z > 0, go_left), (x < NX - 1, go_below), (x > 0, go_above)
        ):
            @pl.when(here)
            def _():
                copy(i).wait_send()

        return 0

    lax.fori_loop(0, PIECES, drain, 0)
    sent = [up_a, up_b, down_a, down_b, to_sib, halo, on_up, on_down, sib_down, sib_up, sib_a, sib_b]
    for copy in sent + decs:
        copy.wait_send()
    for copy in stores:
        copy.wait()


def run_all(*args):
    anywhere = pl.BlockSpec(memory_space=pl.ANY)
    return pl.pallas_call(
        layer_kernel,
        out_shape=tuple(jax.ShapeDtypeStruct(o[1], o[2]) for o in OUTPUTS),
        in_specs=[anywhere if name.endswith("_hbm") else VMEM for name in INPUTS],
        out_specs=tuple(VMEM if o[3] else anywhere for o in OUTPUTS),
        scratch_shapes=[pltpu.VMEM(b[1], b[2]) for b in BUFFERS]
        + [pltpu.SemaphoreType.DMA(m[1]) for m in SEMAPHORES],
        compiler_params=pltpu.CompilerParams(
            collective_id=0, has_side_effects=True, vmem_limit_bytes=BIG
        ),
        name="ssm_layer",
    )(*args)


def last_kernel(
    out_ref, gv_ref, gtok_ref, graw_ref, all_ref, sums_ref,
    out_to, gv_to, gtok_to, graw_to, gw_ref, gcw_ref, gcb_ref, gbias_ref, galog_ref, gskip_ref,
    hold_ref, sem,
):
    pairs = ((gv_ref, gv_to), (out_ref, out_to), (gtok_ref, gtok_to))
    halves = [(n, r) for n in range(3) for r in (slice(0, S // 2), slice(S // 2, S))]
    fetch = [
        pltpu.make_async_copy(pairs[n][0].at[0, r, :], hold_ref.at[n, r, :], sem.at[0, i])
        for i, (n, r) in enumerate(halves)
    ]
    put = [
        pltpu.make_async_copy(hold_ref.at[n, r, :], pairs[n][1].at[0, r, :], sem.at[1, i])
        for i, (n, r) in enumerate(halves)
    ]
    for copy in fetch:
        copy.start()
    for first, second in zip(fetch, put):
        first.wait()
        second.start()
    graw_to[...] = graw_ref[...]
    gw_ref[...] = all_ref[...].astype(F32)
    gcw_ref[...] = sums_ref[0:4, :]
    gcb_ref[...] = sums_ref[4:5, :]
    gbias_ref[...] = sums_ref[5:6, 0:H]
    galog_ref[...] = sums_ref[6:7, 0:H]
    gskip_ref[...] = sums_ref[7:8, 0:H]
    for copy in put:
        copy.wait()


def hand_out(*args):
    head = jax.ShapeDtypeStruct((1, H), F32)
    anywhere = pl.BlockSpec(memory_space=pl.ANY)
    wide = jax.ShapeDtypeStruct((1, S, D), BF)
    return pl.pallas_call(
        last_kernel,
        out_shape=(
            wide, wide, wide,
            jax.ShapeDtypeStruct((1, H, S), F32),
            jax.ShapeDtypeStruct((ROWS, W2), F32),
            jax.ShapeDtypeStruct((4, W2), F32),
            jax.ShapeDtypeStruct((1, W2), F32),
            head, head, head,
        ),
        in_specs=[anywhere] * 3 + [VMEM] * 3,
        out_specs=(anywhere,) * 3 + (VMEM,) * 7,
        scratch_shapes=[pltpu.VMEM((3, S, D), BF), pltpu.SemaphoreType.DMA((2, 6))],
        compiler_params=pltpu.CompilerParams(vmem_limit_bytes=BIG),
        name="hand_out",
    )(*args)


def body(layer_in, w_bc, conv_w, conv_b, ssm_in, dt_raw, dt_bias, a_log, skip_scale, grad_out):
    made = run_all(
        w_bc, layer_in, conv_w, conv_b[None], ssm_in, jnp.swapaxes(dt_raw, 1, 2), dt_bias[None],
        a_log[None], skip_scale[None], grad_out,
    )
    out, gv, gtok, graw, gw, gcw, gcb, gbias, galog, gskip = hand_out(*made)
    return (
        out, gv, gtok, jnp.swapaxes(graw, 1, 2), gw, gcw, gcb[0], gbias[0], galog[0], gskip[0]
    )


def solution(mesh):
    split = P("fsdp", "ctx", None)
    in_specs = (
        split, P("fsdp", None), P(), P(), split, split, P(), P(), P(), split,
    )
    out_specs = (
        split, split, split, split, P("fsdp", None), P(), P(), P(), P(), P(),
    )
    return jax.shard_map(body, mesh=mesh, in_specs=in_specs, out_specs=out_specs, check_vma=False)
```

```python
import functools

import jax
import jax.numpy as jnp
from jax import lax
from jax.experimental import pallas as pl
from jax.experimental.pallas import tpu as pltpu
from jax.sharding import PartitionSpec as P

BF = jnp.bfloat16
F32 = jnp.float32
MESH = pl.DeviceIdType.MESH
HIGH = lax.Precision.HIGHEST
VMEM = pl.BlockSpec(memory_space=pltpu.VMEM)
BIG = 50 * 1024 * 1024
SMALL = 16 * 1024 * 1024

H = 32
S = 128
D = 4096
W2 = 256
ROWS = 512
NX, NZ, NY, NC = 4, 8, 4, 2
CTX = NX * NZ


def dot(a, b, ca=1, cb=0, precision=None):
    return lax.dot_general(
        a, b, (((ca,), (cb,)), ((), ())), preferred_element_type=F32, precision=precision
    )


def tri_upper():
    r = lax.broadcasted_iota(jnp.int32, (S, S), 0)
    c = lax.broadcasted_iota(jnp.int32, (S, S), 1)
    return r, c


def remote(src, dst, sems, slot, **where):
    return pltpu.make_async_remote_copy(
        src_ref=src,
        dst_ref=dst,
        send_sem=sems[0].at[slot],
        recv_sem=sems[1].at[slot],
        device_id=where,
        device_id_type=MESH,
    )


def greet(partners):
    barrier = pltpu.get_barrier_semaphore()
    for who in partners:
        pl.semaphore_signal(barrier, inc=1, device_id=who, device_id_type=MESH)
    pl.semaphore_wait(barrier, len(partners))


def by_head(row):
    return jnp.broadcast_to(row, (S, H)).T


def steps_of(raw, bias, alog):
    x = raw + by_head(bias)
    dt = jnp.maximum(x, 0.0) + jnp.log1p(jnp.exp(-jnp.abs(x)))
    return x, dt, by_head(jnp.exp(alog))


def flip(tile):
    return tile.T


def row_sums(tile):
    return jnp.sum(tile.T, axis=0, keepdims=True)


SKEW = 5
X_SKEW = 5
SUB = 2
PIECES = H * SUB
PART = S // SUB
PX = ROWS // NX
PZ = PX // NZ

INPUTS = ("w_ref", "tok_hbm", "cw_ref", "cb_ref", "v_hbm", "raw_ref", "bias_ref", "alog_ref",
          "skip_ref", "g_hbm")
OUTPUTS = (
    ("out_hbm", (1, S, D), BF, False),
    ("gv_hbm", (1, S, D), BF, False),
    ("gtok_hbm", (1, S, D), BF, False),
    ("graw_ref", (1, H, S), F32, True),
    ("all_ref", (ROWS, W2), BF, True),
    ("sums_ref", (8, W2), F32, True),
)
BUFFERS = (
    ("full_ref", (D, W2), BF),
    ("tokx_ref", (16 + S, D), BF),
    ("v_ref", (S, D), BF),
    ("g_ref", (S, D), BF),
    ("out_ref", (S, D), BF),
    ("gv_ref", (S, D), BF),
    ("gtok_ref", (S, D), BF),
    ("decs_ref", (NZ, H, S), F32),
    ("pad_ref", (S + 8, W2), F32),
    ("conv_ref", (S, W2), F32),
    ("b_ref", (S, S), BF),
    ("c_ref", (S, S), BF),
    ("cum_ref", (H, S), F32),
    ("dt_ref", (H, S), F32),
    ("sig_ref", (H, S), F32),
    ("rate_ref", (H, S), F32),
    ("skipt_ref", (H, S), F32),
    ("dcum_ref", (H, S), F32),
    ("ddt_ref", (H, S), F32),
    ("dskip_ref", (H, S), F32),
    ("dgrow_ref", (H, S), F32),
    ("dew_ref", (H, S), F32),
    ("ddec_ref", (H, S), F32),
    ("yin_ref", (S, D), F32),
    ("dvin_ref", (S, D), F32),
    ("s_ref", (H, S, S), F32),
    ("de_ref", (H, S, S), F32),
    ("down_ref", (H, S, S), F32),
    ("ew_ref", (H, S, S), F32),
    ("u_ref", (S, D), BF),
    ("q_ref", (S, D), BF),
    ("scores_ref", (S, S), F32),
    ("dscores_ref", (S, S), F32),
    ("dbt_ref", (S, S), F32),
    ("dct_ref", (S, S), F32),
    ("e_ref", (H, S, S), BF),
    ("f_ref", (H, S, S), BF),
    ("rs_ref", (H, 2, S, S), BF),
    ("rr_ref", (H, 2, S, S), BF),
    ("ls_ref", (H, 2, S, S), BF),
    ("lr_ref", (H, 2, S, S), BF),
    ("ds_ref", (H, S, S), BF),
    ("dr_ref", (H, S, S), BF),
    ("us_ref", (H, S, S), BF),
    ("ur_ref", (H, S, S), BF),
    ("mul_ref", (4, H, S), F32),
    ("dconv_ref", (S + 16, W2), F32),
    ("gpad_ref", (S + 8, W2), F32),
    ("gr_ref", (S, W2), BF),
    ("gx_ref", (16 + S, W2), BF),
    ("rim_ref", (8, W2), F32),
    ("sa_ref", (NY, ROWS, W2), BF),
    ("ra_ref", (NY, ROWS, W2), BF),
    ("sb_ref", (NY - 1, ROWS, S), BF),
    ("rb_ref", (NY - 1, ROWS, S), BF),
    ("ta_ref", (ROWS, S), BF),
    ("rc_ref", (NX - 1, PX, S), BF),
    ("mx_ref", (NY, ROWS, S), BF),
    ("rx_ref", (NX - 1, NY, PX, S), BF),
    ("sy_ref", (NY - 1, PX, S), BF),
    ("ry_ref", (NY - 1, PX, S), BF),
    ("pz_ref", (PX, W2), F32),
    ("sd_ref", (NZ - 1, PZ, W2), BF),
    ("rd_ref", (NZ - 1, PZ, W2), BF),
    ("fin_ref", (PZ, W2), BF),
    ("ma_ref", (8, W2), F32),
    ("mra_ref", (8, W2), F32),
    ("mb_ref", (NY, 8, W2), F32),
    ("mc_ref", (NX, 8, W2), F32),
    ("mrd_ref", (NZ, 8, W2), F32),
)
SEMAPHORES = (
    ("here_sem", (6,)),
    ("w_sem", (2, 12)),
    ("dec_sem", (2, NZ - 1)),
    ("r_sem", (2, PIECES)),
    ("l_sem", (2, PIECES)),
    ("d_sem2", (2, PIECES)),
    ("u_sem", (2, PIECES)),
    ("rim_sem", (2, 1)),
    ("a_sem", (2, NY)),
    ("b_sem", (2, NY - 1)),
    ("c_sem", (2, NX - 1)),
    ("x_sem", (2, NY * (NX - 1))),
    ("y_sem", (2, NY - 1)),
    ("d_sem", (2, NZ - 1)),
    ("e_sem", (2, NZ - 1)),
    ("f_sem", (2, NX - 1)),
    ("ma_sem", (2, 1)),
    ("mb_sem", (2, NY - 1)),
    ("mc_sem", (2, NX - 1)),
    ("md_sem", (2, NZ - 1)),
)


def layer_kernel(*refs):
    names = list(INPUTS) + [o[0] for o in OUTPUTS] + [b[0] for b in BUFFERS]
    names += [m[0] for m in SEMAPHORES]
    run_layer(**dict(zip(names, refs)))


def run_layer(
    w_ref, tok_hbm, cw_ref, cb_ref, v_hbm, raw_ref, bias_ref, alog_ref, skip_ref, g_hbm, out_hbm,
    gv_hbm, gtok_hbm, graw_ref, all_ref, sums_ref, full_ref, tokx_ref, v_ref, g_ref, out_ref,
    gv_ref, gtok_ref, decs_ref, pad_ref, conv_ref, b_ref, c_ref, cum_ref, dt_ref, sig_ref,
    rate_ref, skipt_ref, dcum_ref, ddt_ref, dskip_ref, dgrow_ref, dew_ref, ddec_ref, yin_ref,
    dvin_ref, s_ref, de_ref, down_ref, ew_ref, u_ref, q_ref, scores_ref, dscores_ref, dbt_ref,
    dct_ref, e_ref, f_ref, rs_ref, rr_ref, ls_ref, lr_ref, ds_ref, dr_ref, us_ref, ur_ref,
    mul_ref, dconv_ref, gpad_ref, gr_ref, gx_ref, rim_ref, sa_ref, ra_ref, sb_ref, rb_ref,
    ta_ref, rc_ref, mx_ref, rx_ref, sy_ref, ry_ref, pz_ref, sd_ref, rd_ref, fin_ref, ma_ref,
    mra_ref, mb_ref, mc_ref, mrd_ref, here_sem, w_sem, dec_sem, r_sem, l_sem, d_sem2, u_sem,
    rim_sem, a_sem, b_sem, c_sem, x_sem, y_sem, d_sem, e_sem, f_sem, ma_sem, mb_sem, mc_sem,
    md_sem,
):
    k = lax.axis_index("ctx")
    f = lax.axis_index("fsdp")
    y, c = f // 2, f % 2
    x, z = k // NZ, k % NZ
    up = ((y + 1) % NY) * 2 + c
    down = ((y + NY - 1) % NY) * 2 + c
    far = ((y + 2) % NY) * 2 + c
    nxt = (k + 1) % CTX
    prv = (k + CTX - 1) % CTX
    sib = {"fsdp": y * 2 + (1 - c)}

    def at_y(d):
        return (y + d) % NY

    def at_x(d):
        return (x + d) % NX

    def at_z(d):
        return (z + d) % NZ

    def y_dev(d):
        return {"fsdp": at_y(d) * 2 + c}

    def x_dev(d):
        return {"ctx": at_x(d) * NZ + z}

    def z_dev(d):
        return {"ctx": x * NZ + at_z(d)}

    def sems(s):
        return (s.at[0], s.at[1])

    loads = [
        pltpu.make_async_copy(src.at[0], dst, here_sem.at[i])
        for i, (src, dst) in enumerate(((tok_hbm, tokx_ref.at[16 : 16 + S, :]), (v_hbm, v_ref), (g_hbm, g_ref)))
    ]
    for copy in loads:
        copy.start()
    row = [z_dev(d) for d in range(1, NZ)]
    partners = [sib, {"ctx": nxt}, {"ctx": prv}]
    partners += [y_dev(d) for d in range(1, NY)]
    partners += [x_dev(d) for d in range(1, NX)]
    partners += row
    greet(partners)

    half = ROWS // 2

    def rows(owner, first=0, size=ROWS):
        return full_ref.at[pl.ds(pl.multiple_of(owner * ROWS + first, half), size), :]

    ws = sems(w_sem)
    lower, upper = w_ref.at[0:half, :], w_ref.at[half:ROWS, :]
    up_a = remote(lower, rows(f, 0, half), ws, 0, fsdp=up)
    down_a = remote(upper, rows(f, half, half), ws, 1, fsdp=down)
    up_b = remote(upper, rows(f, half, half), ws, 10, fsdp=up)
    down_b = remote(lower, rows(f, 0, half), ws, 11, fsdp=down)
    to_sib = remote(w_ref, rows(f), ws, 2, **sib)
    halo = remote(tok_hbm.at[0, S - 16 : S, :], tokx_ref.at[0:16, :], ws, 3, ctx=nxt)
    for copy in (up_a, down_a, up_b, down_b, to_sib, halo):
        copy.start()
    full_ref[pl.ds(pl.multiple_of(f * ROWS, ROWS), ROWS), :] = w_ref[...]
    raw, dt, rate = steps_of(raw_ref[0], bias_ref[...], alog_ref[...])
    r_id = lax.broadcasted_iota(jnp.int32, (S, S), 0)
    c_id = lax.broadcasted_iota(jnp.int32, (S, S), 1)
    dt_ref[...] = dt
    rate_ref[...] = rate
    sig_ref[...] = jax.nn.sigmoid(raw)
    skipt_ref[...] = by_head(skip_ref[...])
    cum = dot(-dt * rate, (r_id <= c_id).astype(F32), precision=HIGH)
    cum_ref[...] = cum
    decs_ref[z] = jnp.broadcast_to(jnp.exp(cum[:, S - 1 : S]), (H, S))
    decs = [
        remote(decs_ref.at[z], decs_ref.at[z], sems(dec_sem), d - 1, **row[d - 1])
        for d in range(1, NZ)
    ]
    for copy in decs:
        copy.start()
    up_a.wait_recv()
    on_up = remote(rows(down, 0, half), rows(down, 0, half), ws, 4, fsdp=up)
    on_up.start()
    down_a.wait_recv()
    on_down = remote(rows(up, half, half), rows(up, half, half), ws, 5, fsdp=down)
    on_down.start()
    up_b.wait_recv()
    sib_down = remote(rows(down), rows(down), ws, 6, **sib)
    sib_down.start()
    down_b.wait_recv()
    sib_up = remote(rows(up), rows(up), ws, 7, **sib)
    sib_up.start()
    on_up.wait_recv()
    sib_a = remote(rows(far, 0, half), rows(far, 0, half), ws, 8, **sib)
    sib_a.start()
    on_down.wait_recv()
    sib_b = remote(rows(far, half, half), rows(far, half, half), ws, 9, **sib)
    sib_b.start()
    for copy in loads:
        copy.wait()
    for copy in [halo] + decs:
        copy.wait_recv()
    before = jnp.ones((H, S), F32)
    after = jnp.ones((H, S), F32)
    for i in range(NZ):
        d = decs_ref[i]
        before = before * jnp.where(i < z, d, 1.0)
        after = after * jnp.where(i > z, d, 1.0)
    mine = decs_ref[z]
    mul_ref[0] = before
    mul_ref[1] = after
    mul_ref[2] = mine
    mul_ref[3] = before * mine * after
    dscores_ref[...] = jnp.zeros_like(dscores_ref)
    dbt_ref[...] = jnp.zeros_like(dbt_ref)
    dct_ref[...] = jnp.zeros_like(dct_ref)
    for copy in (to_sib, sib_down, sib_up, sib_a, sib_b):
        copy.wait_recv()

    projected = dot(tokx_ref[...], full_ref[...])
    pad_ref[...] = projected[8:, :]
    pad_ref[0:8, :] = jnp.where(k > 0, pad_ref[0:8, :], jnp.zeros((8, W2), F32))
    conv = cb_ref[...] + cw_ref[0:1, :] * pad_ref[5 : 5 + S, :]
    for tap in range(1, 4):
        conv = conv + cw_ref[tap : tap + 1, :] * pad_ref[5 + tap : 5 + tap + S, :]
    conv_ref[...] = conv
    act = conv * jax.nn.sigmoid(conv)
    b_ref[...] = act[:, :S].astype(BF)
    c_ref[...] = act[:, S:].astype(BF)
    scores_ref[...] = dot(c_ref[...], b_ref[...], 1, 1)
    mask = r_id >= c_id
    eye = r_id == c_id

    def at(h):
        return pl.ds(pl.multiple_of(h * S, S), S)

    def prep(h):
        one = pl.ds(h, 1)
        cum_r = cum_ref[one, :]
        falling = jnp.broadcast_to(cum_r, (S, S)).T
        down_ref[h] = falling
        ew = jnp.exp(cum_r[:, S - 1 : S] - cum_r) * dt_ref[one, :]
        ew = jnp.broadcast_to(ew, (S, S)).T
        ew_ref[h] = ew
        u = (ew * v_ref[:, at(h)].astype(F32)).astype(BF)
        u_ref[:, at(h)] = u
        s_ref[h] = dot(b_ref[...], u, 0, 0)
        q = (jnp.exp(falling) * g_ref[:, at(h)].astype(F32)).astype(BF)
        q_ref[:, at(h)] = q
        de_ref[h] = dot(c_ref[...], q, 0, 0)

    def mix(h):
        one = pl.ds(h, 1)
        dt_r = dt_ref[one, :]
        gap = down_ref[h] - cum_ref[one, :]
        grid = jnp.where(mask, jnp.exp(jnp.where(mask, gap, 0.0)), 0.0)
        v = v_ref[:, at(h)]
        g = g_ref[:, at(h)]
        skip = skipt_ref[one, :]
        a1 = scores_ref[...] * grid
        weight = (a1 * dt_r).astype(BF)
        yin_ref[:, at(h)] = dot(weight, v) + skip * v.astype(F32)
        dvin_ref[:, at(h)] = dot(weight, g, 0, 0) + skip * g.astype(F32)
        dm = dot(g, v, 1, 1)
        dskip_ref[one, :] = jnp.sum(jnp.where(eye, dm, 0.0), axis=0, keepdims=True)
        xx = dm * a1
        ddt_ref[one, :] = jnp.sum(xx, axis=0, keepdims=True)
        ww = xx * dt_r
        dcum_ref[one, :] = jnp.sum(ww.T - ww, axis=0, keepdims=True)
        return dm * (grid * dt_r)

    def post(h):
        one = pl.ds(h, 1)
        e = e_ref[h]
        f = f_ref[h]
        ce = dot(c_ref[...], e)
        bf = dot(b_ref[...], f)
        out_ref[:, at(h)] = (yin_ref[:, at(h)] + jnp.exp(down_ref[h]) * ce).astype(BF)
        gv_ref[:, at(h)] = (dvin_ref[:, at(h)] + ew_ref[h] * bf).astype(BF)
        dgrow_ref[one, :] = row_sums(g_ref[:, at(h)].astype(F32) * ce)
        dew_ref[one, :] = row_sums(v_ref[:, at(h)].astype(F32) * bf)
        ddec_ref[one, :] = jnp.sum(e.astype(F32) * f.astype(F32), axis=0, keepdims=True)
        return dot(q_ref[:, at(h)], e, 1, 1), dot(u_ref[:, at(h)], f, 1, 1)

    def part(i):
        return i // SUB, pl.ds(pl.multiple_of((i % SUB) * PART, PART), PART)

    def both(ref, i):
        h, rr = part(i)
        return ref.at[h, :, rr, :]

    def single(ref, i):
        h, rr = part(i)
        return ref.at[h, rr, :]

    def go_right(i):
        return remote(both(rs_ref, i), both(rr_ref, i), sems(r_sem), i, **z_dev(1))

    def go_left(i):
        return remote(both(ls_ref, i), both(lr_ref, i), sems(l_sem), i, **z_dev(NZ - 1))

    def go_below(i):
        return remote(single(ds_ref, i), single(dr_ref, i), sems(d_sem2), i, **x_dev(1))

    def go_above(i):
        return remote(single(us_ref, i), single(ur_ref, i), sems(u_sem), i, **x_dev(NX - 1))

    def factor(which, h):
        return mul_ref[which, pl.ds(h, 1), :]

    def arrive(i, first, copy):
        @pl.when(jnp.logical_not(first))
        def _():
            copy(i).wait_recv()

    def to_right(i):
        h, p = part(i)
        arrive(i, z == 0, go_right)

        @pl.when(z < NZ - 1)
        def _():
            states = factor(2, h) * rr_ref[h, 0, p, :].astype(F32) + s_ref[h, p, :]
            rs_ref[h, 0, p, :] = states.astype(BF)
            sums = rr_ref[h, 1, p, :].astype(F32) + factor(0, h) * de_ref[h, p, :]
            rs_ref[h, 1, p, :] = sums.astype(BF)
            go_right(i).start()

    def to_left(i):
        h, p = part(i)
        arrive(i, z == NZ - 1, go_left)

        @pl.when(z > 0)
        def _():
            sums = lr_ref[h, 0, p, :].astype(F32) + factor(1, h) * s_ref[h, p, :]
            ls_ref[h, 0, p, :] = sums.astype(BF)
            states = factor(2, h) * lr_ref[h, 1, p, :].astype(F32) + de_ref[h, p, :]
            ls_ref[h, 1, p, :] = states.astype(BF)
            go_left(i).start()

    def to_below(i):
        h, p = part(i)
        arrive(i, x == 0, go_below)
        entering = dr_ref[h, p, :].astype(F32)
        inside = rr_ref[h, 0, p, :].astype(F32)
        e_ref[h, p, :] = (factor(0, h) * entering + inside).astype(BF)

        @pl.when(x < NX - 1)
        def _():
            total = factor(1, h) * (factor(2, h) * inside + s_ref[h, p, :])
            total = total + lr_ref[h, 0, p, :].astype(F32)
            ds_ref[h, p, :] = (factor(3, h) * entering + total).astype(BF)
            go_below(i).start()

    def to_above(i):
        h, p = part(i)
        arrive(i, x == NX - 1, go_above)
        entering = ur_ref[h, p, :].astype(F32)
        inside = lr_ref[h, 1, p, :].astype(F32)
        f_ref[h, p, :] = (factor(1, h) * entering + inside).astype(BF)

        @pl.when(x > 0)
        def _():
            total = factor(0, h) * (factor(2, h) * inside + de_ref[h, p, :])
            total = total + rr_ref[h, 1, p, :].astype(F32)
            us_ref[h, p, :] = (factor(3, h) * entering + total).astype(BF)
            go_above(i).start()

    for first, land in ((z == 0, rr_ref), (z == NZ - 1, lr_ref), (x == 0, dr_ref), (x == NX - 1, ur_ref)):
        @pl.when(first)
        def _():
            land[...] = jnp.zeros(land.shape, BF)

    late = jnp.maximum(z, NZ - 1 - z)
    late = late * SKEW
    starts = (z * SKEW, (NZ - 1 - z) * SKEW, late + x * X_SKEW, late + (NX - 1 - x) * X_SKEW)
    lag = (jnp.maximum(starts[2], starts[3]) + 2 * SUB - 1) // (2 * SUB)

    def turns(t):
        for start, turn in zip(starts, (to_right, to_left, to_below, to_above)):
            i = t - start

            @pl.when(jnp.logical_and(i >= 0, i < PIECES))
            def _():
                turn(i)

    def slots(n, _):
        h = 2 * n
        t = 2 * SUB * n
        todo = h < H

        @pl.when(todo)
        def _():
            prep(h)
            prep(h + 1)

        turns(t)

        @pl.when(todo)
        def _():
            dscores_ref[...] += mix(h)

        turns(t + 1)
        turns(t + 2)

        @pl.when(todo)
        def _():
            dscores_ref[...] += mix(h + 1)

        turns(t + 3)
        i = 2 * (n - lag)

        @pl.when(jnp.logical_and(i >= 0, i < H))
        def _():
            dc0, db0 = post(i)
            dc1, db1 = post(i + 1)
            dct_ref[...] += dc0 + dc1
            dbt_ref[...] += db0 + db1

        return 0

    most = ((NZ - 1) * SKEW + (NX - 1) * X_SKEW + 2 * SUB - 1) // (2 * SUB)
    lax.fori_loop(0, H // 2 + most, slots, 0)

    stores = [
        pltpu.make_async_copy(out_ref, out_hbm.at[0], here_sem.at[3]),
        pltpu.make_async_copy(gv_ref, gv_hbm.at[0], here_sem.at[4]),
    ]
    for copy in stores:
        copy.start()

    ds = dscores_ref[...].astype(BF)
    dct = dct_ref[...] + dot(ds, b_ref[...])
    dbt = dbt_ref[...] + dot(ds, c_ref[...], 0, 0)
    conv = conv_ref[...]
    sig = jax.nn.sigmoid(conv)
    slope = sig * (1.0 + conv * (1.0 - sig))
    dconv_ref[0:8, :] = jnp.zeros((8, W2), F32)
    dconv_ref[8 + S :, :] = jnp.zeros((8, W2), F32)
    dconv_ref[8 : 8 + S, 0:S] = dbt * slope[:, :S]
    dconv_ref[8 : 8 + S, S:] = dct * slope[:, S:]
    grads = cw_ref[3:4, :] * dconv_ref[0 : 8 + S, :]
    for tap in range(3):
        grads = grads + cw_ref[tap : tap + 1, :] * dconv_ref[3 - tap : 3 - tap + 8 + S, :]
    gpad_ref[...] = grads
    rim = remote(gpad_ref.at[0:8, :], rim_ref, sems(rim_sem), 0, ctx=prv)
    rim.start()
    gx_ref[...] = jnp.concatenate(
        [
            jnp.zeros((8, W2), F32),
            jnp.where(k > 0, gpad_ref[0:8, :], jnp.zeros((8, W2), F32)),
            gpad_ref[8:, :],
        ],
        axis=0,
    ).astype(BF)

    gx = gx_ref[...]

    def term(block):
        return dot(tokx_ref[:, pl.ds(pl.multiple_of(block * ROWS, ROWS), ROWS)], gx, 0, 0)

    def x_rows(d):
        return pl.ds(pl.multiple_of(at_x(d) * PX, PX), PX)

    order = (2, 1, 3, 0)
    copies = {}
    for d in order:
        sa_ref[d] = term(at_y(d) * 2 + (1 - c)).astype(BF)
        copies[d] = remote(sa_ref.at[d], ra_ref.at[d], sems(a_sem), d, **sib)
        copies[d].start()
    to_y, over_x = {}, {}
    for d in order:
        mine = term(at_y(d) * 2 + c)
        copies[d].wait_recv()
        mine = (mine + ra_ref[d].astype(F32)).astype(BF)
        if d:
            sb_ref[d - 1] = mine[:, :S]
            to_y[d] = remote(sb_ref.at[d - 1], rb_ref.at[d - 1], sems(b_sem), d - 1, **y_dev(d))
            to_y[d].start()
        else:
            ta_ref[...] = mine[:, :S]
        mx_ref[d] = mine[:, S:]
        for e in (2, 1, 3):
            over_x[e, d] = remote(
                mx_ref.at[d, x_rows(e), :], rx_ref.at[e - 1, d], sems(x_sem), (e - 1) * NY + d,
                **x_dev(e)
            )
            over_x[e, d].start()

    cum = cum_ref[...]
    dt = dt_ref[...]
    rate = rate_ref[...]
    tail = jnp.exp(cum[:, S - 1 : S] - cum)
    dew = dew_ref[...]
    pull = dew * tail * dt
    at_last = jnp.sum(pull, axis=1, keepdims=True) + jnp.sum(
        ddec_ref[...] * mul_ref[2], axis=1, keepdims=True
    )
    lanes = lax.broadcasted_iota(jnp.int32, (H, S), 1)
    dcum = dcum_ref[...] + dgrow_ref[...] * jnp.exp(cum) - pull
    dcum = dcum + jnp.where(lanes == S - 1, at_last, 0.0)
    dld = dot(dcum, mask.astype(F32), precision=HIGH)
    ddt = ddt_ref[...] + dew * tail - rate * dld
    graw = ddt * sig_ref[...]
    graw_ref[0] = graw
    ma_ref[...] = jnp.zeros_like(ma_ref)
    ma_ref[5:6, 0:H] = row_sums(graw)
    ma_ref[6:7, 0:H] = row_sums(-dt * rate * dld)
    ma_ref[7:8, 0:H] = row_sums(dskip_ref[...])
    dconv = dconv_ref[8 : 8 + S, :]
    for tap in range(4):
        ma_ref[tap : tap + 1, :] = jnp.sum(
            dconv * pad_ref[5 + tap : 5 + tap + S, :], axis=0, keepdims=True
        )
    ma_ref[4:5, :] = jnp.sum(dconv, axis=0, keepdims=True)
    m_a = remote(ma_ref, mra_ref, sems(ma_sem), 0, **sib)
    m_a.start()
    rim.wait_recv()
    rest = jnp.where(k < CTX - 1, rim_ref[...], jnp.zeros_like(rim_ref))
    gr_ref[0 : S - 8, :] = gpad_ref[8:S, :].astype(BF)
    gr_ref[S - 8 : S, :] = (gpad_ref[S : S + 8, :] + rest).astype(BF)
    gr = gr_ref[...]
    m_a.wait_recv()
    low = jnp.where(c == 0, ma_ref[...], mra_ref[...])
    high = jnp.where(c == 0, mra_ref[...], ma_ref[...])
    mb_ref[y] = low + high
    m_b = [remote(mb_ref.at[y], mb_ref.at[y], sems(mb_sem), d - 1, **y_dev(d)) for d in range(1, NY)]
    for copy in m_b:
        copy.start()
    for i in range(D // 1024):
        cols = slice(i * 1024, i * 1024 + 1024)
        gtok_ref[:, cols] = dot(gr, full_ref[cols, :], 1, 1).astype(BF)
    stores.append(pltpu.make_async_copy(gtok_ref, gtok_hbm.at[0], here_sem.at[5]))
    stores[-1].start()
    own = pl.ds(pl.multiple_of(x * PX, PX), PX)
    to_y2 = {}
    for d in order:
        acc = mx_ref[d, own, :].astype(F32)
        for e in (1, 3, 2):
            over_x[e, d].wait_recv()
            acc = acc + rx_ref[e - 1, d].astype(F32)
        if d:
            sy_ref[d - 1] = acc.astype(BF)
            to_y2[d] = remote(sy_ref.at[d - 1], ry_ref.at[d - 1], sems(y_sem), d - 1, **y_dev(d))
            to_y2[d].start()
        else:
            pz_ref[:, S:] = acc
    acc = ta_ref[...].astype(F32)
    for d in (1, 3, 2):
        to_y[d].wait_recv()
        acc = acc + rb_ref[d - 1].astype(F32)
    ta_ref[...] = acc.astype(BF)
    to_x = {}
    for d in (2, 1, 3):
        to_x[d] = remote(
            ta_ref.at[x_rows(d), :], rc_ref.at[d - 1], sems(c_sem), d - 1, **x_dev(d)
        )
        to_x[d].start()
    for copy in m_b:
        copy.wait_recv()
    mc_ref[x] = mb_ref[0] + mb_ref[1] + mb_ref[2] + mb_ref[3]
    m_c = [remote(mc_ref.at[x], mc_ref.at[x], sems(mc_sem), d - 1, **x_dev(d)) for d in range(1, NX)]
    for copy in m_c:
        copy.start()
    acc = pz_ref[:, S:]
    for d in (1, 3, 2):
        to_y2[d].wait_recv()
        acc = acc + ry_ref[d - 1].astype(F32)
    pz_ref[:, S:] = acc
    acc = ta_ref[own, :].astype(F32)
    for d in (1, 3, 2):
        to_x[d].wait_recv()
        acc = acc + rc_ref[d - 1].astype(F32)
    pz_ref[:, :S] = acc
    px, pzr = PX, PZ
    to_z = {}
    for d in (4, 3, 5, 2, 6, 1, 7):
        sd_ref[d - 1] = pz_ref[pl.ds(pl.multiple_of(at_z(d) * pzr, pzr), pzr), :].astype(BF)
        to_z[d] = remote(sd_ref.at[d - 1], rd_ref.at[d - 1], sems(d_sem), d - 1, **z_dev(d))
        to_z[d].start()
    for copy in m_c:
        copy.wait_recv()
    mrd_ref[z] = mc_ref[0] + mc_ref[1] + mc_ref[2] + mc_ref[3]
    m_d = [remote(mrd_ref.at[z], mrd_ref.at[z], sems(md_sem), d - 1, **z_dev(d)) for d in range(1, NZ)]
    for copy in m_d:
        copy.start()
    acc = pz_ref[pl.ds(pl.multiple_of(z * pzr, pzr), pzr), :]
    for d in (1, 7, 2, 6, 3, 5, 4):
        to_z[d].wait_recv()
        acc = acc + rd_ref[d - 1].astype(F32)
    fin_ref[...] = acc.astype(BF)

    def piece(xx, first, size):
        return all_ref.at[pl.ds(pl.multiple_of(xx * px + first, pzr), size), :]

    done = [
        remote(fin_ref, piece(x, z * pzr, pzr), sems(e_sem), d - 1, **z_dev(d))
        for d in (4, 3, 5, 2, 6, 1, 7)
    ]
    for copy in done:
        copy.start()
    all_ref[pl.ds(pl.multiple_of(x * px + z * pzr, pzr), pzr), :] = fin_ref[...]
    for copy in m_d:
        copy.wait_recv()
    total = mrd_ref[0]
    for i in range(1, NZ):
        total = total + mrd_ref[i]
    sums_ref[...] = total
    for copy in done:
        copy.wait_recv()
    last = [
        remote(piece(x, 0, px), piece(x, 0, px), sems(f_sem), d - 1, **x_dev(d)) for d in (2, 1, 3)
    ]
    for copy in last:
        copy.start()
    for copy in last:
        copy.wait_recv()
    sent = [rim, m_a] + m_b + m_c + m_d + done + last
    sent += list(over_x.values()) + list(to_y2.values()) + list(copies.values()) + list(to_y.values()) + list(to_x.values()) + list(to_z.values())
    for copy in sent:
        copy.wait_send()

    def drain(i, _):
        for here, copy in (
            (z < NZ - 1, go_right), (z > 0, go_left), (x < NX - 1, go_below), (x > 0, go_above)
        ):
            @pl.when(here)
            def _():
                copy(i).wait_send()

        return 0

    lax.fori_loop(0, PIECES, drain, 0)
    sent = [up_a, up_b, down_a, down_b, to_sib, halo, on_up, on_down, sib_down, sib_up, sib_a, sib_b]
    for copy in sent + decs:
        copy.wait_send()
    for copy in stores:
        copy.wait()


def run_all(*args):
    anywhere = pl.BlockSpec(memory_space=pl.ANY)
    return pl.pallas_call(
        layer_kernel,
        out_shape=tuple(jax.ShapeDtypeStruct(o[1], o[2]) for o in OUTPUTS),
        in_specs=[pl.BlockSpec(memory_space=pltpu.HBM) if name.endswith("_hbm") else VMEM for name in INPUTS],
        out_specs=tuple(VMEM if o[3] else anywhere for o in OUTPUTS),
        scratch_shapes=[pltpu.VMEM(b[1], b[2]) for b in BUFFERS]
        + [pltpu.SemaphoreType.DMA(m[1]) for m in SEMAPHORES],
        compiler_params=pltpu.CompilerParams(
            collective_id=0, has_side_effects=True, vmem_limit_bytes=BIG
        ),
        name="ssm_layer",
    )(*args)


def last_kernel(
    out_ref, gv_ref, gtok_ref, graw_ref, all_ref, sums_ref,
    out_to, gv_to, gtok_to, graw_to, gw_ref, gcw_ref, gcb_ref, gbias_ref, galog_ref, gskip_ref,
    sem,
):
    pairs = ((gv_ref, gv_to), (out_ref, out_to), (gtok_ref, gtok_to))
    put = [pltpu.make_async_copy(src, dst, sem.at[i]) for i, (src, dst) in enumerate(pairs)]
    for copy in put:
        copy.start()
    graw_to[...] = graw_ref[...]
    gw_ref[...] = all_ref[...].astype(F32)
    gcw_ref[...] = sums_ref[0:4, :]
    gcb_ref[...] = sums_ref[4:5, :]
    gbias_ref[...] = sums_ref[5:6, 0:H]
    galog_ref[...] = sums_ref[6:7, 0:H]
    gskip_ref[...] = sums_ref[7:8, 0:H]
    for copy in put:
        copy.wait()


def hand_out(*args):
    head = jax.ShapeDtypeStruct((1, H), F32)
    anywhere = pl.BlockSpec(memory_space=pl.ANY)
    wide = jax.ShapeDtypeStruct((1, S, D), BF)
    return pl.pallas_call(
        last_kernel,
        out_shape=(
            wide, wide, wide,
            jax.ShapeDtypeStruct((1, H, S), F32),
            jax.ShapeDtypeStruct((ROWS, W2), F32),
            jax.ShapeDtypeStruct((4, W2), F32),
            jax.ShapeDtypeStruct((1, W2), F32),
            head, head, head,
        ),
        in_specs=[VMEM] * 6,
        out_specs=(anywhere,) * 3 + (VMEM,) * 7,
        scratch_shapes=[pltpu.SemaphoreType.DMA((3,))],
        compiler_params=pltpu.CompilerParams(vmem_limit_bytes=SMALL),
        name="hand_out",
    )(*args)


def body(layer_in, w_bc, conv_w, conv_b, ssm_in, dt_raw, dt_bias, a_log, skip_scale, grad_out):
    made = run_all(
        w_bc, layer_in, conv_w, conv_b[None], ssm_in, jnp.swapaxes(dt_raw, 1, 2), dt_bias[None],
        a_log[None], skip_scale[None], grad_out,
    )
    out, gv, gtok, graw, gw, gcw, gcb, gbias, galog, gskip = hand_out(*made)
    return (
        out, gv, gtok, jnp.swapaxes(graw, 1, 2), gw, gcw, gcb[0], gbias[0], galog[0], gskip[0]
    )


def solution(mesh):
    split = P("fsdp", "ctx", None)
    in_specs = (
        split, P("fsdp", None), P(), P(), split, split, P(), P(), P(), split,
    )
    out_specs = (
        split, split, split, split, P("fsdp", None), P(), P(), P(), P(), P(),
    )
    return jax.shard_map(body, mesh=mesh, in_specs=in_specs, out_specs=out_specs, check_vma=False)
```

```python
import functools

import jax
import jax.numpy as jnp
from jax import lax
from jax.experimental import pallas as pl
from jax.experimental.pallas import tpu as pltpu
from jax.sharding import PartitionSpec as P

BF = jnp.bfloat16
F32 = jnp.float32
MESH = pl.DeviceIdType.MESH
HIGH = lax.Precision.HIGHEST
VMEM = pl.BlockSpec(memory_space=pltpu.VMEM)
BIG = 50 * 1024 * 1024
SMALL = 16 * 1024 * 1024

H = 32
S = 128
D = 4096
W2 = 256
ROWS = 512
NX, NZ, NY, NC = 4, 8, 4, 2
CTX = NX * NZ


def dot(a, b, ca=1, cb=0, precision=None):
    return lax.dot_general(
        a, b, (((ca,), (cb,)), ((), ())), preferred_element_type=F32, precision=precision
    )


def tri_upper():
    r = lax.broadcasted_iota(jnp.int32, (S, S), 0)
    c = lax.broadcasted_iota(jnp.int32, (S, S), 1)
    return r, c


def remote(src, dst, sems, slot, **where):
    return pltpu.make_async_remote_copy(
        src_ref=src,
        dst_ref=dst,
        send_sem=sems[0].at[slot],
        recv_sem=sems[1].at[slot],
        device_id=where,
        device_id_type=MESH,
    )


def greet(partners):
    barrier = pltpu.get_barrier_semaphore()
    for who in partners:
        pl.semaphore_signal(barrier, inc=1, device_id=who, device_id_type=MESH)
    pl.semaphore_wait(barrier, len(partners))


def by_head(row):
    return jnp.broadcast_to(row, (S, H)).T


def steps_of(raw, bias, alog):
    x = raw + by_head(bias)
    dt = jnp.maximum(x, 0.0) + jnp.log1p(jnp.exp(-jnp.abs(x)))
    return x, dt, by_head(jnp.exp(alog))


def flip(tile):
    return tile.T


def row_sums(tile):
    return jnp.sum(tile.T, axis=0, keepdims=True)


SKEW = 5
X_SKEW = 5
SUB = 2
PIECES = H * SUB
PART = S // SUB
PX = ROWS // NX
PZ = PX // NZ

INPUTS = ("w_ref", "tok_hbm", "cw_ref", "cb_ref", "v_hbm", "raw_ref", "bias_ref", "alog_ref",
          "skip_ref", "g_hbm")
OUTPUTS = (
    ("out_hbm", (1, S, D), BF, False),
    ("gv_hbm", (1, S, D), BF, False),
    ("gtok_hbm", (1, S, D), BF, False),
    ("graw_ref", (1, H, S), F32, True),
    ("all_ref", (ROWS, W2), BF, True),
    ("sums_ref", (8, W2), F32, True),
)
BUFFERS = (
    ("full_ref", (D, W2), BF),
    ("tokx_ref", (16 + S, D), BF),
    ("v_ref", (S, D), BF),
    ("g_ref", (S, D), BF),
    ("out_ref", (S, D), BF),
    ("gv_ref", (S, D), BF),
    ("gtok_ref", (S, D), BF),
    ("decs_ref", (NZ, H, S), F32),
    ("pad_ref", (S + 8, W2), F32),
    ("conv_ref", (S, W2), F32),
    ("b_ref", (S, S), BF),
    ("c_ref", (S, S), BF),
    ("cum_ref", (H, S), F32),
    ("dt_ref", (H, S), F32),
    ("sig_ref", (H, S), F32),
    ("rate_ref", (H, S), F32),
    ("skipt_ref", (H, S), F32),
    ("dcum_ref", (H, S), F32),
    ("ddt_ref", (H, S), F32),
    ("dskip_ref", (H, S), F32),
    ("dgrow_ref", (H, S), F32),
    ("dew_ref", (H, S), F32),
    ("ddec_ref", (H, S), F32),
    ("yin_ref", (S, D), F32),
    ("dvin_ref", (S, D), F32),
    ("s_ref", (H, S, S), F32),
    ("de_ref", (H, S, S), F32),
    ("down_ref", (H, S, S), F32),
    ("ew_ref", (H, S, S), F32),
    ("u_ref", (S, D), BF),
    ("q_ref", (S, D), BF),
    ("scores_ref", (S, S), F32),
    ("dscores_ref", (S, S), F32),
    ("dbt_ref", (S, S), F32),
    ("dct_ref", (S, S), F32),
    ("e_ref", (H, S, S), BF),
    ("f_ref", (H, S, S), BF),
    ("rs_ref", (H, 2, S, S), BF),
    ("rr_ref", (H, 2, S, S), BF),
    ("ls_ref", (H, 2, S, S), BF),
    ("lr_ref", (H, 2, S, S), BF),
    ("ds_ref", (H, S, S), BF),
    ("dr_ref", (H, S, S), BF),
    ("us_ref", (H, S, S), BF),
    ("ur_ref", (H, S, S), BF),
    ("mul_ref", (4, H, S), F32),
    ("dconv_ref", (S + 16, W2), F32),
    ("gpad_ref", (S + 8, W2), F32),
    ("gr_ref", (S, W2), BF),
    ("gx_ref", (16 + S, W2), BF),
    ("rim_ref", (8, W2), F32),
    ("sa_ref", (NY, ROWS, W2), BF),
    ("ra_ref", (NY, ROWS, W2), BF),
    ("sb_ref", (NY - 1, ROWS, S), BF),
    ("rb_ref", (NY - 1, ROWS, S), BF),
    ("ta_ref", (ROWS, S), BF),
    ("rc_ref", (NX - 1, PX, S), BF),
    ("mx_ref", (NY, ROWS, S), BF),
    ("rx_ref", (NX - 1, NY, PX, S), BF),
    ("sy_ref", (NY - 1, PX, S), BF),
    ("ry_ref", (NY - 1, PX, S), BF),
    ("pz_ref", (PX, W2), F32),
    ("sd_ref", (NZ - 1, PZ, W2), BF),
    ("rd_ref", (NZ - 1, PZ, W2), BF),
    ("fin_ref", (PZ, W2), BF),
    ("ma_ref", (8, W2), F32),
    ("mra_ref", (8, W2), F32),
    ("mb_ref", (NY, 8, W2), F32),
    ("mc_ref", (NX, 8, W2), F32),
    ("mrd_ref", (NZ, 8, W2), F32),
)
SEMAPHORES = (
    ("here_sem", (6,)),
    ("w_sem", (2, 12)),
    ("dec_sem", (2, NZ - 1)),
    ("r_sem", (2, PIECES)),
    ("l_sem", (2, PIECES)),
    ("d_sem2", (2, PIECES)),
    ("u_sem", (2, PIECES)),
    ("rim_sem", (2, 1)),
    ("a_sem", (2, NY)),
    ("b_sem", (2, NY - 1)),
    ("c_sem", (2, NX - 1)),
    ("x_sem", (2, NY * (NX - 1))),
    ("y_sem", (2, NY - 1)),
    ("d_sem", (2, NZ - 1)),
    ("e_sem", (2, NZ - 1)),
    ("f_sem", (2, NX - 1)),
    ("ma_sem", (2, 1)),
    ("mb_sem", (2, NY - 1)),
    ("mc_sem", (2, NX - 1)),
    ("md_sem", (2, NZ - 1)),
)


def layer_kernel(*refs):
    names = list(INPUTS) + [o[0] for o in OUTPUTS] + [b[0] for b in BUFFERS]
    names += [m[0] for m in SEMAPHORES]
    run_layer(**dict(zip(names, refs)))


def run_layer(
    w_ref, tok_hbm, cw_ref, cb_ref, v_hbm, raw_ref, bias_ref, alog_ref, skip_ref, g_hbm, out_hbm,
    gv_hbm, gtok_hbm, graw_ref, all_ref, sums_ref, full_ref, tokx_ref, v_ref, g_ref, out_ref,
    gv_ref, gtok_ref, decs_ref, pad_ref, conv_ref, b_ref, c_ref, cum_ref, dt_ref, sig_ref,
    rate_ref, skipt_ref, dcum_ref, ddt_ref, dskip_ref, dgrow_ref, dew_ref, ddec_ref, yin_ref,
    dvin_ref, s_ref, de_ref, down_ref, ew_ref, u_ref, q_ref, scores_ref, dscores_ref, dbt_ref,
    dct_ref, e_ref, f_ref, rs_ref, rr_ref, ls_ref, lr_ref, ds_ref, dr_ref, us_ref, ur_ref,
    mul_ref, dconv_ref, gpad_ref, gr_ref, gx_ref, rim_ref, sa_ref, ra_ref, sb_ref, rb_ref,
    ta_ref, rc_ref, mx_ref, rx_ref, sy_ref, ry_ref, pz_ref, sd_ref, rd_ref, fin_ref, ma_ref,
    mra_ref, mb_ref, mc_ref, mrd_ref, here_sem, w_sem, dec_sem, r_sem, l_sem, d_sem2, u_sem,
    rim_sem, a_sem, b_sem, c_sem, x_sem, y_sem, d_sem, e_sem, f_sem, ma_sem, mb_sem, mc_sem,
    md_sem,
):
    k = lax.axis_index("ctx")
    f = lax.axis_index("fsdp")
    y, c = f // 2, f % 2
    x, z = k // NZ, k % NZ
    up = ((y + 1) % NY) * 2 + c
    down = ((y + NY - 1) % NY) * 2 + c
    far = ((y + 2) % NY) * 2 + c
    nxt = (k + 1) % CTX
    prv = (k + CTX - 1) % CTX
    sib = {"fsdp": y * 2 + (1 - c)}

    def at_y(d):
        return (y + d) % NY

    def at_x(d):
        return (x + d) % NX

    def at_z(d):
        return (z + d) % NZ

    def y_dev(d):
        return {"fsdp": at_y(d) * 2 + c}

    def x_dev(d):
        return {"ctx": at_x(d) * NZ + z}

    def z_dev(d):
        return {"ctx": x * NZ + at_z(d)}

    def sems(s):
        return (s.at[0], s.at[1])

    loads = [
        pltpu.make_async_copy(src.at[0], dst, here_sem.at[i])
        for i, (src, dst) in enumerate(((tok_hbm, tokx_ref.at[16 : 16 + S, :]), (v_hbm, v_ref), (g_hbm, g_ref)))
    ]
    for copy in loads:
        copy.start()
    row = [z_dev(d) for d in range(1, NZ)]
    partners = [sib, {"ctx": nxt}, {"ctx": prv}]
    partners += [y_dev(d) for d in range(1, NY)]
    partners += [x_dev(d) for d in range(1, NX)]
    partners += row
    greet(partners)

    half = ROWS // 2

    def rows(owner, first=0, size=ROWS):
        return full_ref.at[pl.ds(pl.multiple_of(owner * ROWS + first, half), size), :]

    def shard(owner):
        here = pl.ds(pl.multiple_of(owner * ROWS, ROWS), ROWS)
        return dot(tokx_ref[:, here], full_ref[here, :])

    ws = sems(w_sem)
    lower, upper = w_ref.at[0:half, :], w_ref.at[half:ROWS, :]
    up_a = remote(lower, rows(f, 0, half), ws, 0, fsdp=up)
    down_a = remote(upper, rows(f, half, half), ws, 1, fsdp=down)
    up_b = remote(upper, rows(f, half, half), ws, 10, fsdp=up)
    down_b = remote(lower, rows(f, 0, half), ws, 11, fsdp=down)
    to_sib = remote(w_ref, rows(f), ws, 2, **sib)
    halo = remote(tok_hbm.at[0, S - 16 : S, :], tokx_ref.at[0:16, :], ws, 3, ctx=nxt)
    for copy in (up_a, down_a, up_b, down_b, to_sib, halo):
        copy.start()
    full_ref[pl.ds(pl.multiple_of(f * ROWS, ROWS), ROWS), :] = w_ref[...]
    raw, dt, rate = steps_of(raw_ref[0], bias_ref[...], alog_ref[...])
    r_id = lax.broadcasted_iota(jnp.int32, (S, S), 0)
    c_id = lax.broadcasted_iota(jnp.int32, (S, S), 1)
    dt_ref[...] = dt
    rate_ref[...] = rate
    sig_ref[...] = jax.nn.sigmoid(raw)
    skipt_ref[...] = by_head(skip_ref[...])
    cum = dot(-dt * rate, (r_id <= c_id).astype(F32), precision=HIGH)
    cum_ref[...] = cum
    decs_ref[z] = jnp.broadcast_to(jnp.exp(cum[:, S - 1 : S]), (H, S))
    decs = [
        remote(decs_ref.at[z], decs_ref.at[z], sems(dec_sem), d - 1, **row[d - 1])
        for d in range(1, NZ)
    ]
    for copy in decs:
        copy.start()
    up_a.wait_recv()
    on_up = remote(rows(down, 0, half), rows(down, 0, half), ws, 4, fsdp=up)
    on_up.start()
    down_a.wait_recv()
    on_down = remote(rows(up, half, half), rows(up, half, half), ws, 5, fsdp=down)
    on_down.start()
    up_b.wait_recv()
    sib_down = remote(rows(down), rows(down), ws, 6, **sib)
    sib_down.start()
    down_b.wait_recv()
    sib_up = remote(rows(up), rows(up), ws, 7, **sib)
    sib_up.start()
    on_up.wait_recv()
    sib_a = remote(rows(far, 0, half), rows(far, 0, half), ws, 8, **sib)
    sib_a.start()
    on_down.wait_recv()
    sib_b = remote(rows(far, half, half), rows(far, half, half), ws, 9, **sib)
    sib_b.start()
    for copy in loads:
        copy.wait()
    for copy in [halo] + decs:
        copy.wait_recv()
    before = jnp.ones((H, S), F32)
    after = jnp.ones((H, S), F32)
    for i in range(NZ):
        d = decs_ref[i]
        before = before * jnp.where(i < z, d, 1.0)
        after = after * jnp.where(i > z, d, 1.0)
    mine = decs_ref[z]
    mul_ref[0] = before
    mul_ref[1] = after
    mul_ref[2] = mine
    mul_ref[3] = before * mine * after
    dscores_ref[...] = jnp.zeros_like(dscores_ref)
    dbt_ref[...] = jnp.zeros_like(dbt_ref)
    dct_ref[...] = jnp.zeros_like(dct_ref)
    for first, land in ((z == 0, rr_ref), (z == NZ - 1, lr_ref), (x == 0, dr_ref), (x == NX - 1, ur_ref)):
        @pl.when(first)
        def _():
            land[...] = jnp.zeros(land.shape, BF)

    other = 1 - 2 * c
    projected = shard(f) + shard(down) + shard(up) + shard(far)
    for copy in (to_sib, sib_down, sib_up):
        copy.wait_recv()
    projected = projected + shard(f + other) + shard(down + other) + shard(up + other)
    sib_a.wait_recv()
    sib_b.wait_recv()
    projected = projected + shard(far + other)

    pad_ref[...] = projected[8:, :]
    pad_ref[0:8, :] = jnp.where(k > 0, pad_ref[0:8, :], jnp.zeros((8, W2), F32))
    conv = cb_ref[...] + cw_ref[0:1, :] * pad_ref[5 : 5 + S, :]
    for tap in range(1, 4):
        conv = conv + cw_ref[tap : tap + 1, :] * pad_ref[5 + tap : 5 + tap + S, :]
    conv_ref[...] = conv
    act = conv * jax.nn.sigmoid(conv)
    b_ref[...] = act[:, :S].astype(BF)
    c_ref[...] = act[:, S:].astype(BF)
    scores_ref[...] = dot(c_ref[...], b_ref[...], 1, 1)
    mask = r_id >= c_id
    eye = r_id == c_id

    def at(h):
        return pl.ds(pl.multiple_of(h * S, S), S)

    def prep(h):
        one = pl.ds(h, 1)
        cum_r = cum_ref[one, :]
        falling = jnp.broadcast_to(cum_r, (S, S)).T
        down_ref[h] = falling
        ew = jnp.exp(cum_r[:, S - 1 : S] - cum_r) * dt_ref[one, :]
        ew = jnp.broadcast_to(ew, (S, S)).T
        ew_ref[h] = ew
        u = (ew * v_ref[:, at(h)].astype(F32)).astype(BF)
        u_ref[:, at(h)] = u
        s_ref[h] = dot(b_ref[...], u, 0, 0)
        q = (jnp.exp(falling) * g_ref[:, at(h)].astype(F32)).astype(BF)
        q_ref[:, at(h)] = q
        de_ref[h] = dot(c_ref[...], q, 0, 0)

    def mix(h):
        one = pl.ds(h, 1)
        dt_r = dt_ref[one, :]
        gap = down_ref[h] - cum_ref[one, :]
        grid = jnp.where(mask, jnp.exp(jnp.where(mask, gap, 0.0)), 0.0)
        v = v_ref[:, at(h)]
        g = g_ref[:, at(h)]
        skip = skipt_ref[one, :]
        a1 = scores_ref[...] * grid
        weight = (a1 * dt_r).astype(BF)
        yin_ref[:, at(h)] = dot(weight, v) + skip * v.astype(F32)
        dvin_ref[:, at(h)] = dot(weight, g, 0, 0) + skip * g.astype(F32)
        dm = dot(g, v, 1, 1)
        dskip_ref[one, :] = jnp.sum(jnp.where(eye, dm, 0.0), axis=0, keepdims=True)
        xx = dm * a1
        ddt_ref[one, :] = jnp.sum(xx, axis=0, keepdims=True)
        ww = xx * dt_r
        dcum_ref[one, :] = jnp.sum(ww.T - ww, axis=0, keepdims=True)
        return dm * (grid * dt_r)

    def post(h):
        one = pl.ds(h, 1)
        e = e_ref[h]
        f = f_ref[h]
        ce = dot(c_ref[...], e)
        bf = dot(b_ref[...], f)
        out_ref[:, at(h)] = (yin_ref[:, at(h)] + jnp.exp(down_ref[h]) * ce).astype(BF)
        gv_ref[:, at(h)] = (dvin_ref[:, at(h)] + ew_ref[h] * bf).astype(BF)
        dgrow_ref[one, :] = row_sums(g_ref[:, at(h)].astype(F32) * ce)
        dew_ref[one, :] = row_sums(v_ref[:, at(h)].astype(F32) * bf)
        ddec_ref[one, :] = jnp.sum(e.astype(F32) * f.astype(F32), axis=0, keepdims=True)
        return dot(q_ref[:, at(h)], e, 1, 1), dot(u_ref[:, at(h)], f, 1, 1)

    def part(i):
        return i // SUB, pl.ds(pl.multiple_of((i % SUB) * PART, PART), PART)

    def both(ref, i):
        h, rr = part(i)
        return ref.at[h, :, rr, :]

    def single(ref, i):
        h, rr = part(i)
        return ref.at[h, rr, :]

    def go_right(i):
        return remote(both(rs_ref, i), both(rr_ref, i), sems(r_sem), i, **z_dev(1))

    def go_left(i):
        return remote(both(ls_ref, i), both(lr_ref, i), sems(l_sem), i, **z_dev(NZ - 1))

    def go_below(i):
        return remote(single(ds_ref, i), single(dr_ref, i), sems(d_sem2), i, **x_dev(1))

    def go_above(i):
        return remote(single(us_ref, i), single(ur_ref, i), sems(u_sem), i, **x_dev(NX - 1))

    def factor(which, h):
        return mul_ref[which, pl.ds(h, 1), :]

    def arrive(i, first, copy):
        @pl.when(jnp.logical_not(first))
        def _():
            copy(i).wait_recv()

    def to_right(i):
        h, p = part(i)
        arrive(i, z == 0, go_right)

        @pl.when(z < NZ - 1)
        def _():
            states = factor(2, h) * rr_ref[h, 0, p, :].astype(F32) + s_ref[h, p, :]
            rs_ref[h, 0, p, :] = states.astype(BF)
            sums = rr_ref[h, 1, p, :].astype(F32) + factor(0, h) * de_ref[h, p, :]
            rs_ref[h, 1, p, :] = sums.astype(BF)
            go_right(i).start()

    def to_left(i):
        h, p = part(i)
        arrive(i, z == NZ - 1, go_left)

        @pl.when(z > 0)
        def _():
            sums = lr_ref[h, 0, p, :].astype(F32) + factor(1, h) * s_ref[h, p, :]
            ls_ref[h, 0, p, :] = sums.astype(BF)
            states = factor(2, h) * lr_ref[h, 1, p, :].astype(F32) + de_ref[h, p, :]
            ls_ref[h, 1, p, :] = states.astype(BF)
            go_left(i).start()

    def to_below(i):
        h, p = part(i)
        arrive(i, x == 0, go_below)
        entering = dr_ref[h, p, :].astype(F32)
        inside = rr_ref[h, 0, p, :].astype(F32)
        e_ref[h, p, :] = (factor(0, h) * entering + inside).astype(BF)

        @pl.when(x < NX - 1)
        def _():
            total = factor(1, h) * (factor(2, h) * inside + s_ref[h, p, :])
            total = total + lr_ref[h, 0, p, :].astype(F32)
            ds_ref[h, p, :] = (factor(3, h) * entering + total).astype(BF)
            go_below(i).start()

    def to_above(i):
        h, p = part(i)
        arrive(i, x == NX - 1, go_above)
        entering = ur_ref[h, p, :].astype(F32)
        inside = lr_ref[h, 1, p, :].astype(F32)
        f_ref[h, p, :] = (factor(1, h) * entering + inside).astype(BF)

        @pl.when(x > 0)
        def _():
            total = factor(0, h) * (factor(2, h) * inside + de_ref[h, p, :])
            total = total + rr_ref[h, 1, p, :].astype(F32)
            us_ref[h, p, :] = (factor(3, h) * entering + total).astype(BF)
            go_above(i).start()

    late = jnp.maximum(z, NZ - 1 - z)
    late = late * SKEW
    starts = (z * SKEW, (NZ - 1 - z) * SKEW, late + x * X_SKEW, late + (NX - 1 - x) * X_SKEW)
    lag = (jnp.maximum(starts[2], starts[3]) + 2 * SUB - 1) // (2 * SUB)

    def turns(t):
        for start, turn in zip(starts, (to_right, to_left, to_below, to_above)):
            i = t - start

            @pl.when(jnp.logical_and(i >= 0, i < PIECES))
            def _():
                turn(i)

    def slots(n, _):
        h = 2 * n
        t = 2 * SUB * n
        todo = h < H

        @pl.when(todo)
        def _():
            prep(h)
            prep(h + 1)

        turns(t)

        @pl.when(todo)
        def _():
            dscores_ref[...] += mix(h)

        turns(t + 1)
        turns(t + 2)

        @pl.when(todo)
        def _():
            dscores_ref[...] += mix(h + 1)

        turns(t + 3)
        i = 2 * (n - lag)

        @pl.when(jnp.logical_and(i >= 0, i < H))
        def _():
            dc0, db0 = post(i)
            dc1, db1 = post(i + 1)
            dct_ref[...] += dc0 + dc1
            dbt_ref[...] += db0 + db1

        return 0

    most = ((NZ - 1) * SKEW + (NX - 1) * X_SKEW + 2 * SUB - 1) // (2 * SUB)
    lax.fori_loop(0, H // 2 + most, slots, 0)

    stores = [
        pltpu.make_async_copy(out_ref, out_hbm.at[0], here_sem.at[3]),
        pltpu.make_async_copy(gv_ref, gv_hbm.at[0], here_sem.at[4]),
    ]
    for copy in stores:
        copy.start()

    ds = dscores_ref[...].astype(BF)
    dct = dct_ref[...] + dot(ds, b_ref[...])
    dbt = dbt_ref[...] + dot(ds, c_ref[...], 0, 0)
    conv = conv_ref[...]
    sig = jax.nn.sigmoid(conv)
    slope = sig * (1.0 + conv * (1.0 - sig))
    dconv_ref[0:8, :] = jnp.zeros((8, W2), F32)
    dconv_ref[8 + S :, :] = jnp.zeros((8, W2), F32)
    dconv_ref[8 : 8 + S, 0:S] = dbt * slope[:, :S]
    dconv_ref[8 : 8 + S, S:] = dct * slope[:, S:]
    grads = cw_ref[3:4, :] * dconv_ref[0 : 8 + S, :]
    for tap in range(3):
        grads = grads + cw_ref[tap : tap + 1, :] * dconv_ref[3 - tap : 3 - tap + 8 + S, :]
    gpad_ref[...] = grads
    rim = remote(gpad_ref.at[0:8, :], rim_ref, sems(rim_sem), 0, ctx=prv)
    rim.start()
    gx_ref[...] = jnp.concatenate(
        [
            jnp.zeros((8, W2), F32),
            jnp.where(k > 0, gpad_ref[0:8, :], jnp.zeros((8, W2), F32)),
            gpad_ref[8:, :],
        ],
        axis=0,
    ).astype(BF)

    gx = gx_ref[...]

    def term(block):
        return dot(tokx_ref[:, pl.ds(pl.multiple_of(block * ROWS, ROWS), ROWS)], gx, 0, 0)

    def x_rows(d):
        return pl.ds(pl.multiple_of(at_x(d) * PX, PX), PX)

    order = (2, 1, 3, 0)
    copies = {}
    for d in order:
        sa_ref[d] = term(at_y(d) * 2 + (1 - c)).astype(BF)
        copies[d] = remote(sa_ref.at[d], ra_ref.at[d], sems(a_sem), d, **sib)
        copies[d].start()
    to_y, over_x = {}, {}
    for d in order:
        mine = term(at_y(d) * 2 + c)
        copies[d].wait_recv()
        mine = (mine + ra_ref[d].astype(F32)).astype(BF)
        if d:
            sb_ref[d - 1] = mine[:, :S]
            to_y[d] = remote(sb_ref.at[d - 1], rb_ref.at[d - 1], sems(b_sem), d - 1, **y_dev(d))
            to_y[d].start()
        else:
            ta_ref[...] = mine[:, :S]
        mx_ref[d] = mine[:, S:]
        for e in (2, 1, 3):
            over_x[e, d] = remote(
                mx_ref.at[d, x_rows(e), :], rx_ref.at[e - 1, d], sems(x_sem), (e - 1) * NY + d,
                **x_dev(e)
            )
            over_x[e, d].start()

    cum = cum_ref[...]
    dt = dt_ref[...]
    rate = rate_ref[...]
    tail = jnp.exp(cum[:, S - 1 : S] - cum)
    dew = dew_ref[...]
    pull = dew * tail * dt
    at_last = jnp.sum(pull, axis=1, keepdims=True) + jnp.sum(
        ddec_ref[...] * mul_ref[2], axis=1, keepdims=True
    )
    lanes = lax.broadcasted_iota(jnp.int32, (H, S), 1)
    dcum = dcum_ref[...] + dgrow_ref[...] * jnp.exp(cum) - pull
    dcum = dcum + jnp.where(lanes == S - 1, at_last, 0.0)
    dld = dot(dcum, mask.astype(F32), precision=HIGH)
    ddt = ddt_ref[...] + dew * tail - rate * dld
    graw = ddt * sig_ref[...]
    graw_ref[0] = graw
    ma_ref[...] = jnp.zeros_like(ma_ref)
    ma_ref[5:6, 0:H] = row_sums(graw)
    ma_ref[6:7, 0:H] = row_sums(-dt * rate * dld)
    ma_ref[7:8, 0:H] = row_sums(dskip_ref[...])
    dconv = dconv_ref[8 : 8 + S, :]
    for tap in range(4):
        ma_ref[tap : tap + 1, :] = jnp.sum(
            dconv * pad_ref[5 + tap : 5 + tap + S, :], axis=0, keepdims=True
        )
    ma_ref[4:5, :] = jnp.sum(dconv, axis=0, keepdims=True)
    m_a = remote(ma_ref, mra_ref, sems(ma_sem), 0, **sib)
    m_a.start()
    rim.wait_recv()
    rest = jnp.where(k < CTX - 1, rim_ref[...], jnp.zeros_like(rim_ref))
    gr_ref[0 : S - 8, :] = gpad_ref[8:S, :].astype(BF)
    gr_ref[S - 8 : S, :] = (gpad_ref[S : S + 8, :] + rest).astype(BF)
    gr = gr_ref[...]
    m_a.wait_recv()
    low = jnp.where(c == 0, ma_ref[...], mra_ref[...])
    high = jnp.where(c == 0, mra_ref[...], ma_ref[...])
    mb_ref[y] = low + high
    m_b = [remote(mb_ref.at[y], mb_ref.at[y], sems(mb_sem), d - 1, **y_dev(d)) for d in range(1, NY)]
    for copy in m_b:
        copy.start()
    for i in range(D // 1024):
        cols = slice(i * 1024, i * 1024 + 1024)
        gtok_ref[:, cols] = dot(gr, full_ref[cols, :], 1, 1).astype(BF)
    stores.append(pltpu.make_async_copy(gtok_ref, gtok_hbm.at[0], here_sem.at[5]))
    stores[-1].start()
    def drain(i, _):
        for here, copy in (
            (z < NZ - 1, go_right), (z > 0, go_left), (x < NX - 1, go_below), (x > 0, go_above)
        ):
            @pl.when(here)
            def _():
                copy(i).wait_send()

        return 0

    lax.fori_loop(0, PIECES, drain, 0)
    sent = [up_a, up_b, down_a, down_b, to_sib, halo, on_up, on_down, sib_down, sib_up, sib_a, sib_b]
    for copy in sent + decs:
        copy.wait_send()
    own = pl.ds(pl.multiple_of(x * PX, PX), PX)
    to_y2 = {}
    for d in order:
        acc = mx_ref[d, own, :].astype(F32)
        for e in (1, 3, 2):
            over_x[e, d].wait_recv()
            acc = acc + rx_ref[e - 1, d].astype(F32)
        if d:
            sy_ref[d - 1] = acc.astype(BF)
            to_y2[d] = remote(sy_ref.at[d - 1], ry_ref.at[d - 1], sems(y_sem), d - 1, **y_dev(d))
            to_y2[d].start()
        else:
            pz_ref[:, S:] = acc
    acc = ta_ref[...].astype(F32)
    for d in (1, 3, 2):
        to_y[d].wait_recv()
        acc = acc + rb_ref[d - 1].astype(F32)
    ta_ref[...] = acc.astype(BF)
    to_x = {}
    for d in (2, 1, 3):
        to_x[d] = remote(
            ta_ref.at[x_rows(d), :], rc_ref.at[d - 1], sems(c_sem), d - 1, **x_dev(d)
        )
        to_x[d].start()
    for copy in m_b:
        copy.wait_recv()
    mc_ref[x] = mb_ref[0] + mb_ref[1] + mb_ref[2] + mb_ref[3]
    m_c = [remote(mc_ref.at[x], mc_ref.at[x], sems(mc_sem), d - 1, **x_dev(d)) for d in range(1, NX)]
    for copy in m_c:
        copy.start()
    acc = pz_ref[:, S:]
    for d in (1, 3, 2):
        to_y2[d].wait_recv()
        acc = acc + ry_ref[d - 1].astype(F32)
    pz_ref[:, S:] = acc
    acc = ta_ref[own, :].astype(F32)
    for d in (1, 3, 2):
        to_x[d].wait_recv()
        acc = acc + rc_ref[d - 1].astype(F32)
    pz_ref[:, :S] = acc
    px, pzr = PX, PZ
    to_z = {}
    for d in (4, 3, 5, 2, 6, 1, 7):
        sd_ref[d - 1] = pz_ref[pl.ds(pl.multiple_of(at_z(d) * pzr, pzr), pzr), :].astype(BF)
        to_z[d] = remote(sd_ref.at[d - 1], rd_ref.at[d - 1], sems(d_sem), d - 1, **z_dev(d))
        to_z[d].start()
    for copy in m_c:
        copy.wait_recv()
    mrd_ref[z] = mc_ref[0] + mc_ref[1] + mc_ref[2] + mc_ref[3]
    m_d = [remote(mrd_ref.at[z], mrd_ref.at[z], sems(md_sem), d - 1, **z_dev(d)) for d in range(1, NZ)]
    for copy in m_d:
        copy.start()
    acc = pz_ref[pl.ds(pl.multiple_of(z * pzr, pzr), pzr), :]
    for d in (1, 7, 2, 6, 3, 5, 4):
        to_z[d].wait_recv()
        acc = acc + rd_ref[d - 1].astype(F32)
    fin_ref[...] = acc.astype(BF)

    def piece(xx, first, size):
        return all_ref.at[pl.ds(pl.multiple_of(xx * px + first, pzr), size), :]

    done = [
        remote(fin_ref, piece(x, z * pzr, pzr), sems(e_sem), d - 1, **z_dev(d))
        for d in (4, 3, 5, 2, 6, 1, 7)
    ]
    for copy in done:
        copy.start()
    all_ref[pl.ds(pl.multiple_of(x * px + z * pzr, pzr), pzr), :] = fin_ref[...]
    for copy in m_d:
        copy.wait_recv()
    total = mrd_ref[0]
    for i in range(1, NZ):
        total = total + mrd_ref[i]
    sums_ref[...] = total
    for copy in done:
        copy.wait_recv()
    last = [
        remote(piece(x, 0, px), piece(x, 0, px), sems(f_sem), d - 1, **x_dev(d)) for d in (2, 1, 3)
    ]
    for copy in last:
        copy.start()
    for copy in last:
        copy.wait_recv()
    late_sends = [rim, m_a] + m_b + m_c + m_d + done + last
    late_sends += list(over_x.values()) + list(to_y2.values()) + list(copies.values()) + list(to_y.values()) + list(to_x.values()) + list(to_z.values())
    for copy in late_sends:
        copy.wait_send()

    for copy in stores:
        copy.wait()


def run_all(*args):
    anywhere = pl.BlockSpec(memory_space=pl.ANY)
    return pl.pallas_call(
        layer_kernel,
        out_shape=tuple(jax.ShapeDtypeStruct(o[1], o[2]) for o in OUTPUTS),
        in_specs=[pl.BlockSpec(memory_space=pltpu.HBM) if name.endswith("_hbm") else VMEM for name in INPUTS],
        out_specs=tuple(VMEM if o[3] else anywhere for o in OUTPUTS),
        scratch_shapes=[pltpu.VMEM(b[1], b[2]) for b in BUFFERS]
        + [pltpu.SemaphoreType.DMA(m[1]) for m in SEMAPHORES],
        compiler_params=pltpu.CompilerParams(
            collective_id=0, has_side_effects=True, vmem_limit_bytes=BIG
        ),
        name="ssm_layer",
    )(*args)


def last_kernel(
    out_ref, gv_ref, gtok_ref, graw_ref, all_ref, sums_ref,
    out_to, gv_to, gtok_to, graw_to, gw_ref, gcw_ref, gcb_ref, gbias_ref, galog_ref, gskip_ref,
    sem,
):
    pairs = ((gv_ref, gv_to), (out_ref, out_to), (gtok_ref, gtok_to))
    put = [pltpu.make_async_copy(src, dst, sem.at[i]) for i, (src, dst) in enumerate(pairs)]
    for copy in put:
        copy.start()
    graw_to[...] = graw_ref[...]
    gw_ref[...] = all_ref[...].astype(F32)
    gcw_ref[...] = sums_ref[0:4, :]
    gcb_ref[...] = sums_ref[4:5, :]
    gbias_ref[...] = sums_ref[5:6, 0:H]
    galog_ref[...] = sums_ref[6:7, 0:H]
    gskip_ref[...] = sums_ref[7:8, 0:H]
    for copy in put:
        copy.wait()


def hand_out(*args):
    head = jax.ShapeDtypeStruct((1, H), F32)
    anywhere = pl.BlockSpec(memory_space=pl.ANY)
    wide = jax.ShapeDtypeStruct((1, S, D), BF)
    return pl.pallas_call(
        last_kernel,
        out_shape=(
            wide, wide, wide,
            jax.ShapeDtypeStruct((1, H, S), F32),
            jax.ShapeDtypeStruct((ROWS, W2), F32),
            jax.ShapeDtypeStruct((4, W2), F32),
            jax.ShapeDtypeStruct((1, W2), F32),
            head, head, head,
        ),
        in_specs=[VMEM] * 6,
        out_specs=(anywhere,) * 3 + (VMEM,) * 7,
        scratch_shapes=[pltpu.SemaphoreType.DMA((3,))],
        compiler_params=pltpu.CompilerParams(vmem_limit_bytes=SMALL),
        name="hand_out",
    )(*args)


def body(layer_in, w_bc, conv_w, conv_b, ssm_in, dt_raw, dt_bias, a_log, skip_scale, grad_out):
    made = run_all(
        w_bc, layer_in, conv_w, conv_b[None], ssm_in, jnp.swapaxes(dt_raw, 1, 2), dt_bias[None],
        a_log[None], skip_scale[None], grad_out,
    )
    out, gv, gtok, graw, gw, gcw, gcb, gbias, galog, gskip = hand_out(*made)
    return (
        out, gv, gtok, jnp.swapaxes(graw, 1, 2), gw, gcw, gcb[0], gbias[0], galog[0], gskip[0]
    )


def solution(mesh):
    split = P("fsdp", "ctx", None)
    in_specs = (
        split, P("fsdp", None), P(), P(), split, split, P(), P(), P(), split,
    )
    out_specs = (
        split, split, split, split, P("fsdp", None), P(), P(), P(), P(), P(),
    )
    return jax.shard_map(body, mesh=mesh, in_specs=in_specs, out_specs=out_specs, check_vma=False)
```

```python
import functools

import jax
import jax.numpy as jnp
from jax import lax
from jax.experimental import pallas as pl
from jax.experimental.pallas import tpu as pltpu
from jax.sharding import PartitionSpec as P

BF = jnp.bfloat16
F32 = jnp.float32
MESH = pl.DeviceIdType.MESH
HIGH = lax.Precision.HIGHEST
VMEM = pl.BlockSpec(memory_space=pltpu.VMEM)
BIG = 50 * 1024 * 1024
SMALL = 16 * 1024 * 1024

H = 32
S = 128
D = 4096
W2 = 256
ROWS = 512
NX, NZ, NY, NC = 4, 8, 4, 2
CTX = NX * NZ


def dot(a, b, ca=1, cb=0, precision=None):
    return lax.dot_general(
        a, b, (((ca,), (cb,)), ((), ())), preferred_element_type=F32, precision=precision
    )


def tri_upper():
    r = lax.broadcasted_iota(jnp.int32, (S, S), 0)
    c = lax.broadcasted_iota(jnp.int32, (S, S), 1)
    return r, c


def remote(src, dst, sems, slot, **where):
    return pltpu.make_async_remote_copy(
        src_ref=src,
        dst_ref=dst,
        send_sem=sems[0].at[slot],
        recv_sem=sems[1].at[slot],
        device_id=where,
        device_id_type=MESH,
    )


def greet(partners):
    barrier = pltpu.get_barrier_semaphore()
    for who in partners:
        pl.semaphore_signal(barrier, inc=1, device_id=who, device_id_type=MESH)
    pl.semaphore_wait(barrier, len(partners))


def by_head(row):
    return jnp.broadcast_to(row, (S, H)).T


def steps_of(raw, bias, alog):
    x = raw + by_head(bias)
    dt = jnp.maximum(x, 0.0) + jnp.log1p(jnp.exp(-jnp.abs(x)))
    return x, dt, by_head(jnp.exp(alog))


def flip(tile):
    return tile.T


def row_sums(tile):
    return jnp.sum(tile.T, axis=0, keepdims=True)


SKEW = 5
X_SKEW = 6
SUB = 2
PIECES = H * SUB
PART = S // SUB
PX = ROWS // NX
PZ = PX // NZ

INPUTS = ("w_ref", "tok_hbm", "cw_ref", "cb_ref", "v_hbm", "raw_ref", "bias_ref", "alog_ref",
          "skip_ref", "g_hbm")
OUTPUTS = (
    ("out_hbm", (1, S, D), BF, False),
    ("gv_hbm", (1, S, D), BF, False),
    ("gtok_hbm", (1, S, D), BF, False),
    ("graw_ref", (1, H, S), F32, True),
    ("all_ref", (ROWS, W2), BF, True),
    ("sums_ref", (8, W2), F32, True),
)
BUFFERS = (
    ("full_ref", (D, W2), BF),
    ("tokx_ref", (16 + S, D), BF),
    ("v_ref", (S, D), BF),
    ("g_ref", (S, D), BF),
    ("out_ref", (S, D), BF),
    ("gv_ref", (S, D), BF),
    ("gtok_ref", (S, D), BF),
    ("decs_ref", (NZ, H, S), F32),
    ("pad_ref", (S + 8, W2), F32),
    ("conv_ref", (S, W2), F32),
    ("b_ref", (S, S), BF),
    ("c_ref", (S, S), BF),
    ("cum_ref", (H, S), F32),
    ("dt_ref", (H, S), F32),
    ("sig_ref", (H, S), F32),
    ("rate_ref", (H, S), F32),
    ("skipt_ref", (H, S), F32),
    ("dcum_ref", (H, S), F32),
    ("ddt_ref", (H, S), F32),
    ("dskip_ref", (H, S), F32),
    ("dgrow_ref", (H, S), F32),
    ("dew_ref", (H, S), F32),
    ("ddec_ref", (H, S), F32),
    ("yin_ref", (S, D), F32),
    ("dvin_ref", (S, D), F32),
    ("s_ref", (H, S, S), F32),
    ("de_ref", (H, S, S), F32),
    ("down_ref", (H, S, S), F32),
    ("ew_ref", (H, S, S), F32),
    ("u_ref", (S, D), BF),
    ("q_ref", (S, D), BF),
    ("scores_ref", (S, S), F32),
    ("dscores_ref", (S, S), F32),
    ("dbt_ref", (S, S), F32),
    ("dct_ref", (S, S), F32),
    ("e_ref", (H, S, S), BF),
    ("f_ref", (H, S, S), BF),
    ("rs_ref", (H, 2, S, S), BF),
    ("rr_ref", (H, 2, S, S), BF),
    ("ls_ref", (H, 2, S, S), BF),
    ("lr_ref", (H, 2, S, S), BF),
    ("ds_ref", (H, S, S), BF),
    ("dr_ref", (H, S, S), BF),
    ("us_ref", (H, S, S), BF),
    ("ur_ref", (H, S, S), BF),
    ("mul_ref", (4, H, S), F32),
    ("dconv_ref", (S + 16, W2), F32),
    ("gpad_ref", (S + 8, W2), F32),
    ("gr_ref", (S, W2), BF),
    ("gx_ref", (16 + S, W2), BF),
    ("rim_ref", (8, W2), F32),
    ("sa_ref", (NY, ROWS, W2), BF),
    ("ra_ref", (NY, ROWS, W2), BF),
    ("sb_ref", (NY - 1, ROWS, S), BF),
    ("rb_ref", (NY - 1, ROWS, S), BF),
    ("ta_ref", (ROWS, S), BF),
    ("rc_ref", (NX - 1, PX, S), BF),
    ("mx_ref", (NY, ROWS, S), BF),
    ("rx_ref", (NX - 1, NY, PX, S), BF),
    ("sy_ref", (NY - 1, PX, S), BF),
    ("ry_ref", (NY - 1, PX, S), BF),
    ("pz_ref", (PX, W2), F32),
    ("sd_ref", (NZ - 1, PZ, W2), BF),
    ("rd_ref", (NZ - 1, PZ, W2), BF),
    ("fin_ref", (PZ, W2), BF),
    ("ma_ref", (8, W2), F32),
    ("mra_ref", (8, W2), F32),
    ("mb_ref", (NY, 8, W2), F32),
    ("mc_ref", (NX, 8, W2), F32),
    ("mrd_ref", (NZ, 8, W2), F32),
)
SEMAPHORES = (
    ("here_sem", (6,)),
    ("w_sem", (2, 12)),
    ("dec_sem", (2, NZ - 1)),
    ("r_sem", (2, PIECES)),
    ("l_sem", (2, PIECES)),
    ("d_sem2", (2, PIECES)),
    ("u_sem", (2, PIECES)),
    ("rim_sem", (2, 1)),
    ("a_sem", (2, NY)),
    ("b_sem", (2, NY - 1)),
    ("c_sem", (2, NX - 1)),
    ("x_sem", (2, NY * (NX - 1))),
    ("y_sem", (2, NY - 1)),
    ("d_sem", (2, NZ - 1)),
    ("e_sem", (2, NZ - 1)),
    ("f_sem", (2, NX - 1)),
    ("ma_sem", (2, 1)),
    ("mb_sem", (2, NY - 1)),
    ("mc_sem", (2, NX - 1)),
    ("md_sem", (2, NZ - 1)),
)


def layer_kernel(*refs):
    names = list(INPUTS) + [o[0] for o in OUTPUTS] + [b[0] for b in BUFFERS]
    names += [m[0] for m in SEMAPHORES]
    run_layer(**dict(zip(names, refs)))


def run_layer(
    w_ref, tok_hbm, cw_ref, cb_ref, v_hbm, raw_ref, bias_ref, alog_ref, skip_ref, g_hbm, out_hbm,
    gv_hbm, gtok_hbm, graw_ref, all_ref, sums_ref, full_ref, tokx_ref, v_ref, g_ref, out_ref,
    gv_ref, gtok_ref, decs_ref, pad_ref, conv_ref, b_ref, c_ref, cum_ref, dt_ref, sig_ref,
    rate_ref, skipt_ref, dcum_ref, ddt_ref, dskip_ref, dgrow_ref, dew_ref, ddec_ref, yin_ref,
    dvin_ref, s_ref, de_ref, down_ref, ew_ref, u_ref, q_ref, scores_ref, dscores_ref, dbt_ref,
    dct_ref, e_ref, f_ref, rs_ref, rr_ref, ls_ref, lr_ref, ds_ref, dr_ref, us_ref, ur_ref,
    mul_ref, dconv_ref, gpad_ref, gr_ref, gx_ref, rim_ref, sa_ref, ra_ref, sb_ref, rb_ref,
    ta_ref, rc_ref, mx_ref, rx_ref, sy_ref, ry_ref, pz_ref, sd_ref, rd_ref, fin_ref, ma_ref,
    mra_ref, mb_ref, mc_ref, mrd_ref, here_sem, w_sem, dec_sem, r_sem, l_sem, d_sem2, u_sem,
    rim_sem, a_sem, b_sem, c_sem, x_sem, y_sem, d_sem, e_sem, f_sem, ma_sem, mb_sem, mc_sem,
    md_sem,
):
    k = lax.axis_index("ctx")
    f = lax.axis_index("fsdp")
    y, c = f // 2, f % 2
    x, z = k // NZ, k % NZ
    up = ((y + 1) % NY) * 2 + c
    down = ((y + NY - 1) % NY) * 2 + c
    far = ((y + 2) % NY) * 2 + c
    nxt = (k + 1) % CTX
    prv = (k + CTX - 1) % CTX
    sib = {"fsdp": y * 2 + (1 - c)}

    def at_y(d):
        return (y + d) % NY

    def at_x(d):
        return (x + d) % NX

    def at_z(d):
        return (z + d) % NZ

    def y_dev(d):
        return {"fsdp": at_y(d) * 2 + c}

    def x_dev(d):
        return {"ctx": at_x(d) * NZ + z}

    def z_dev(d):
        return {"ctx": x * NZ + at_z(d)}

    def sems(s):
        return (s.at[0], s.at[1])

    loads = [
        pltpu.make_async_copy(src.at[0], dst, here_sem.at[i])
        for i, (src, dst) in enumerate(((tok_hbm, tokx_ref.at[16 : 16 + S, :]), (v_hbm, v_ref), (g_hbm, g_ref)))
    ]
    for copy in loads:
        copy.start()
    row = [z_dev(d) for d in range(1, NZ)]
    partners = [sib, {"ctx": nxt}, {"ctx": prv}]
    partners += [y_dev(d) for d in range(1, NY)]
    partners += [x_dev(d) for d in range(1, NX)]
    partners += row
    greet(partners)

    half = ROWS // 2

    def rows(owner, first=0, size=ROWS):
        return full_ref.at[pl.ds(pl.multiple_of(owner * ROWS + first, half), size), :]

    def shard(owner):
        here = pl.ds(pl.multiple_of(owner * ROWS, ROWS), ROWS)
        return dot(tokx_ref[:, here], full_ref[here, :])

    ws = sems(w_sem)
    lower, upper = w_ref.at[0:half, :], w_ref.at[half:ROWS, :]
    up_a = remote(lower, rows(f, 0, half), ws, 0, fsdp=up)
    down_a = remote(upper, rows(f, half, half), ws, 1, fsdp=down)
    up_b = remote(upper, rows(f, half, half), ws, 10, fsdp=up)
    down_b = remote(lower, rows(f, 0, half), ws, 11, fsdp=down)
    to_sib = remote(w_ref, rows(f), ws, 2, **sib)
    halo = remote(tok_hbm.at[0, S - 16 : S, :], tokx_ref.at[0:16, :], ws, 3, ctx=nxt)
    for copy in (up_a, down_a, up_b, down_b, to_sib, halo):
        copy.start()
    full_ref[pl.ds(pl.multiple_of(f * ROWS, ROWS), ROWS), :] = w_ref[...]
    raw, dt, rate = steps_of(raw_ref[0], bias_ref[...], alog_ref[...])
    r_id = lax.broadcasted_iota(jnp.int32, (S, S), 0)
    c_id = lax.broadcasted_iota(jnp.int32, (S, S), 1)
    dt_ref[...] = dt
    rate_ref[...] = rate
    sig_ref[...] = jax.nn.sigmoid(raw)
    skipt_ref[...] = by_head(skip_ref[...])
    cum = dot(-dt * rate, (r_id <= c_id).astype(F32), precision=HIGH)
    cum_ref[...] = cum
    decs_ref[z] = jnp.broadcast_to(jnp.exp(cum[:, S - 1 : S]), (H, S))
    decs = [
        remote(decs_ref.at[z], decs_ref.at[z], sems(dec_sem), d - 1, **row[d - 1])
        for d in range(1, NZ)
    ]
    for copy in decs:
        copy.start()
    up_a.wait_recv()
    on_up = remote(rows(down, 0, half), rows(down, 0, half), ws, 4, fsdp=up)
    on_up.start()
    down_a.wait_recv()
    on_down = remote(rows(up, half, half), rows(up, half, half), ws, 5, fsdp=down)
    on_down.start()
    up_b.wait_recv()
    sib_down = remote(rows(down), rows(down), ws, 6, **sib)
    sib_down.start()
    down_b.wait_recv()
    sib_up = remote(rows(up), rows(up), ws, 7, **sib)
    sib_up.start()
    on_up.wait_recv()
    sib_a = remote(rows(far, 0, half), rows(far, 0, half), ws, 8, **sib)
    sib_a.start()
    on_down.wait_recv()
    sib_b = remote(rows(far, half, half), rows(far, half, half), ws, 9, **sib)
    sib_b.start()
    for copy in loads:
        copy.wait()
    for copy in [halo] + decs:
        copy.wait_recv()
    before = jnp.ones((H, S), F32)
    after = jnp.ones((H, S), F32)
    for i in range(NZ):
        d = decs_ref[i]
        before = before * jnp.where(i < z, d, 1.0)
        after = after * jnp.where(i > z, d, 1.0)
    mine = decs_ref[z]
    mul_ref[0] = before
    mul_ref[1] = after
    mul_ref[2] = mine
    mul_ref[3] = before * mine * after
    dscores_ref[...] = jnp.zeros_like(dscores_ref)
    dbt_ref[...] = jnp.zeros_like(dbt_ref)
    dct_ref[...] = jnp.zeros_like(dct_ref)
    for first, land in ((z == 0, rr_ref), (z == NZ - 1, lr_ref), (x == 0, dr_ref), (x == NX - 1, ur_ref)):
        @pl.when(first)
        def _():
            land[...] = jnp.zeros(land.shape, BF)

    other = 1 - 2 * c
    projected = shard(f) + shard(down) + shard(up) + shard(far)
    for copy in (to_sib, sib_down, sib_up):
        copy.wait_recv()
    projected = projected + shard(f + other) + shard(down + other) + shard(up + other)
    sib_a.wait_recv()
    sib_b.wait_recv()
    projected = projected + shard(far + other)

    pad_ref[...] = projected[8:, :]
    pad_ref[0:8, :] = jnp.where(k > 0, pad_ref[0:8, :], jnp.zeros((8, W2), F32))
    conv = cb_ref[...] + cw_ref[0:1, :] * pad_ref[5 : 5 + S, :]
    for tap in range(1, 4):
        conv = conv + cw_ref[tap : tap + 1, :] * pad_ref[5 + tap : 5 + tap + S, :]
    conv_ref[...] = conv
    act = conv * jax.nn.sigmoid(conv)
    b_ref[...] = act[:, :S].astype(BF)
    c_ref[...] = act[:, S:].astype(BF)
    scores_ref[...] = dot(c_ref[...], b_ref[...], 1, 1)
    mask = r_id >= c_id
    eye = r_id == c_id

    def at(h):
        return pl.ds(pl.multiple_of(h * S, S), S)

    def prep(h):
        one = pl.ds(h, 1)
        cum_r = cum_ref[one, :]
        falling = jnp.broadcast_to(cum_r, (S, S)).T
        down_ref[h] = falling
        ew = jnp.exp(cum_r[:, S - 1 : S] - cum_r) * dt_ref[one, :]
        ew = jnp.broadcast_to(ew, (S, S)).T
        ew_ref[h] = ew
        u = (ew * v_ref[:, at(h)].astype(F32)).astype(BF)
        u_ref[:, at(h)] = u
        s_ref[h] = dot(b_ref[...], u, 0, 0)
        q = (jnp.exp(falling) * g_ref[:, at(h)].astype(F32)).astype(BF)
        q_ref[:, at(h)] = q
        de_ref[h] = dot(c_ref[...], q, 0, 0)

    def mix(h):
        one = pl.ds(h, 1)
        dt_r = dt_ref[one, :]
        gap = down_ref[h] - cum_ref[one, :]
        grid = jnp.where(mask, jnp.exp(jnp.where(mask, gap, 0.0)), 0.0)
        v = v_ref[:, at(h)]
        g = g_ref[:, at(h)]
        skip = skipt_ref[one, :]
        a1 = scores_ref[...] * grid
        weight = (a1 * dt_r).astype(BF)
        yin_ref[:, at(h)] = dot(weight, v) + skip * v.astype(F32)
        dvin_ref[:, at(h)] = dot(weight, g, 0, 0) + skip * g.astype(F32)
        dm = dot(g, v, 1, 1)
        dskip_ref[one, :] = jnp.sum(jnp.where(eye, dm, 0.0), axis=0, keepdims=True)
        xx = dm * a1
        ddt_ref[one, :] = jnp.sum(xx, axis=0, keepdims=True)
        ww = xx * dt_r
        dcum_ref[one, :] = jnp.sum(ww.T - ww, axis=0, keepdims=True)
        return dm * (grid * dt_r)

    def post(h):
        one = pl.ds(h, 1)
        e = e_ref[h]
        f = f_ref[h]
        ce = dot(c_ref[...], e)
        bf = dot(b_ref[...], f)
        out_ref[:, at(h)] = (yin_ref[:, at(h)] + jnp.exp(down_ref[h]) * ce).astype(BF)
        gv_ref[:, at(h)] = (dvin_ref[:, at(h)] + ew_ref[h] * bf).astype(BF)
        dgrow_ref[one, :] = row_sums(g_ref[:, at(h)].astype(F32) * ce)
        dew_ref[one, :] = row_sums(v_ref[:, at(h)].astype(F32) * bf)
        ddec_ref[one, :] = jnp.sum(e.astype(F32) * f.astype(F32), axis=0, keepdims=True)
        return dot(q_ref[:, at(h)], e, 1, 1), dot(u_ref[:, at(h)], f, 1, 1)

    def part(i):
        return i // SUB, pl.ds(pl.multiple_of((i % SUB) * PART, PART), PART)

    def both(ref, i):
        h, rr = part(i)
        return ref.at[h, :, rr, :]

    def single(ref, i):
        h, rr = part(i)
        return ref.at[h, rr, :]

    def go_right(i):
        return remote(both(rs_ref, i), both(rr_ref, i), sems(r_sem), i, **z_dev(1))

    def go_left(i):
        return remote(both(ls_ref, i), both(lr_ref, i), sems(l_sem), i, **z_dev(NZ - 1))

    def go_below(i):
        return remote(single(ds_ref, i), single(dr_ref, i), sems(d_sem2), i, **x_dev(1))

    def go_above(i):
        return remote(single(us_ref, i), single(ur_ref, i), sems(u_sem), i, **x_dev(NX - 1))

    def factor(which, h):
        return mul_ref[which, pl.ds(h, 1), :]

    def arrive(i, first, copy):
        @pl.when(jnp.logical_not(first))
        def _():
            copy(i).wait_recv()

    def to_right(i):
        h, p = part(i)
        arrive(i, z == 0, go_right)

        @pl.when(z < NZ - 1)
        def _():
            states = factor(2, h) * rr_ref[h, 0, p, :].astype(F32) + s_ref[h, p, :]
            rs_ref[h, 0, p, :] = states.astype(BF)
            sums = rr_ref[h, 1, p, :].astype(F32) + factor(0, h) * de_ref[h, p, :]
            rs_ref[h, 1, p, :] = sums.astype(BF)
            go_right(i).start()

    def to_left(i):
        h, p = part(i)
        arrive(i, z == NZ - 1, go_left)

        @pl.when(z > 0)
        def _():
            sums = lr_ref[h, 0, p, :].astype(F32) + factor(1, h) * s_ref[h, p, :]
            ls_ref[h, 0, p, :] = sums.astype(BF)
            states = factor(2, h) * lr_ref[h, 1, p, :].astype(F32) + de_ref[h, p, :]
            ls_ref[h, 1, p, :] = states.astype(BF)
            go_left(i).start()

    def to_below(i):
        h, p = part(i)
        arrive(i, x == 0, go_below)
        entering = dr_ref[h, p, :].astype(F32)
        inside = rr_ref[h, 0, p, :].astype(F32)
        e_ref[h, p, :] = (factor(0, h) * entering + inside).astype(BF)

        @pl.when(x < NX - 1)
        def _():
            total = factor(1, h) * (factor(2, h) * inside + s_ref[h, p, :])
            total = total + lr_ref[h, 0, p, :].astype(F32)
            ds_ref[h, p, :] = (factor(3, h) * entering + total).astype(BF)
            go_below(i).start()

    def to_above(i):
        h, p = part(i)
        arrive(i, x == NX - 1, go_above)
        entering = ur_ref[h, p, :].astype(F32)
        inside = lr_ref[h, 1, p, :].astype(F32)
        f_ref[h, p, :] = (factor(1, h) * entering + inside).astype(BF)

        @pl.when(x > 0)
        def _():
            total = factor(0, h) * (factor(2, h) * inside + de_ref[h, p, :])
            total = total + rr_ref[h, 1, p, :].astype(F32)
            us_ref[h, p, :] = (factor(3, h) * entering + total).astype(BF)
            go_above(i).start()

    late = jnp.maximum(z, NZ - 1 - z)
    late = late * SKEW
    starts = (z * SKEW, (NZ - 1 - z) * SKEW, late + x * X_SKEW, late + (NX - 1 - x) * X_SKEW)
    lag = (jnp.maximum(starts[2], starts[3]) + 2 * SUB - 1) // (2 * SUB)

    def turns(t):
        for start, turn in zip(starts, (to_right, to_left, to_below, to_above)):
            i = t - start

            @pl.when(jnp.logical_and(i >= 0, i < PIECES))
            def _():
                turn(i)

    def slots(n, _):
        h = 2 * n
        t = 2 * SUB * n
        todo = h < H

        @pl.when(todo)
        def _():
            prep(h)
            prep(h + 1)

        turns(t)

        @pl.when(todo)
        def _():
            dscores_ref[...] += mix(h)

        turns(t + 1)
        turns(t + 2)

        @pl.when(todo)
        def _():
            dscores_ref[...] += mix(h + 1)

        turns(t + 3)
        i = 2 * (n - lag)

        @pl.when(jnp.logical_and(i >= 0, i < H))
        def _():
            dc0, db0 = post(i)
            dc1, db1 = post(i + 1)
            dct_ref[...] += dc0 + dc1
            dbt_ref[...] += db0 + db1

        return 0

    most = ((NZ - 1) * SKEW + (NX - 1) * X_SKEW + 2 * SUB - 1) // (2 * SUB)
    lax.fori_loop(0, H // 2 + most, slots, 0)

    stores = [
        pltpu.make_async_copy(out_ref, out_hbm.at[0], here_sem.at[3]),
        pltpu.make_async_copy(gv_ref, gv_hbm.at[0], here_sem.at[4]),
    ]
    for copy in stores:
        copy.start()

    ds = dscores_ref[...].astype(BF)
    dct = dct_ref[...] + dot(ds, b_ref[...])
    dbt = dbt_ref[...] + dot(ds, c_ref[...], 0, 0)
    conv = conv_ref[...]
    sig = jax.nn.sigmoid(conv)
    slope = sig * (1.0 + conv * (1.0 - sig))
    dconv_ref[0:8, :] = jnp.zeros((8, W2), F32)
    dconv_ref[8 + S :, :] = jnp.zeros((8, W2), F32)
    dconv_ref[8 : 8 + S, 0:S] = dbt * slope[:, :S]
    dconv_ref[8 : 8 + S, S:] = dct * slope[:, S:]
    grads = cw_ref[3:4, :] * dconv_ref[0 : 8 + S, :]
    for tap in range(3):
        grads = grads + cw_ref[tap : tap + 1, :] * dconv_ref[3 - tap : 3 - tap + 8 + S, :]
    gpad_ref[...] = grads
    rim = remote(gpad_ref.at[0:8, :], rim_ref, sems(rim_sem), 0, ctx=prv)
    rim.start()
    gx_ref[...] = jnp.concatenate(
        [
            jnp.zeros((8, W2), F32),
            jnp.where(k > 0, gpad_ref[0:8, :], jnp.zeros((8, W2), F32)),
            gpad_ref[8:, :],
        ],
        axis=0,
    ).astype(BF)

    gx = gx_ref[...]

    def term(block):
        return dot(tokx_ref[:, pl.ds(pl.multiple_of(block * ROWS, ROWS), ROWS)], gx, 0, 0)

    def x_rows(d):
        return pl.ds(pl.multiple_of(at_x(d) * PX, PX), PX)

    order = (2, 1, 3, 0)
    copies = {}
    for d in order:
        sa_ref[d] = term(at_y(d) * 2 + (1 - c)).astype(BF)
        copies[d] = remote(sa_ref.at[d], ra_ref.at[d], sems(a_sem), d, **sib)
        copies[d].start()
    to_y, over_x = {}, {}
    for d in order:
        mine = term(at_y(d) * 2 + c)
        copies[d].wait_recv()
        mine = (mine + ra_ref[d].astype(F32)).astype(BF)
        if d:
            sb_ref[d - 1] = mine[:, :S]
            to_y[d] = remote(sb_ref.at[d - 1], rb_ref.at[d - 1], sems(b_sem), d - 1, **y_dev(d))
            to_y[d].start()
        else:
            ta_ref[...] = mine[:, :S]
        mx_ref[d] = mine[:, S:]
        for e in (2, 1, 3):
            over_x[e, d] = remote(
                mx_ref.at[d, x_rows(e), :], rx_ref.at[e - 1, d], sems(x_sem), (e - 1) * NY + d,
                **x_dev(e)
            )
            over_x[e, d].start()

    cum = cum_ref[...]
    dt = dt_ref[...]
    rate = rate_ref[...]
    tail = jnp.exp(cum[:, S - 1 : S] - cum)
    dew = dew_ref[...]
    pull = dew * tail * dt
    at_last = jnp.sum(pull, axis=1, keepdims=True) + jnp.sum(
        ddec_ref[...] * mul_ref[2], axis=1, keepdims=True
    )
    lanes = lax.broadcasted_iota(jnp.int32, (H, S), 1)
    dcum = dcum_ref[...] + dgrow_ref[...] * jnp.exp(cum) - pull
    dcum = dcum + jnp.where(lanes == S - 1, at_last, 0.0)
    dld = dot(dcum, mask.astype(F32), precision=HIGH)
    ddt = ddt_ref[...] + dew * tail - rate * dld
    graw = ddt * sig_ref[...]
    graw_ref[0] = graw
    ma_ref[...] = jnp.zeros_like(ma_ref)
    ma_ref[5:6, 0:H] = row_sums(graw)
    ma_ref[6:7, 0:H] = row_sums(-dt * rate * dld)
    ma_ref[7:8, 0:H] = row_sums(dskip_ref[...])
    dconv = dconv_ref[8 : 8 + S, :]
    for tap in range(4):
        ma_ref[tap : tap + 1, :] = jnp.sum(
            dconv * pad_ref[5 + tap : 5 + tap + S, :], axis=0, keepdims=True
        )
    ma_ref[4:5, :] = jnp.sum(dconv, axis=0, keepdims=True)
    m_a = remote(ma_ref, mra_ref, sems(ma_sem), 0, **sib)
    m_a.start()
    rim.wait_recv()
    rest = jnp.where(k < CTX - 1, rim_ref[...], jnp.zeros_like(rim_ref))
    gr_ref[0 : S - 8, :] = gpad_ref[8:S, :].astype(BF)
    gr_ref[S - 8 : S, :] = (gpad_ref[S : S + 8, :] + rest).astype(BF)
    gr = gr_ref[...]
    m_a.wait_recv()
    low = jnp.where(c == 0, ma_ref[...], mra_ref[...])
    high = jnp.where(c == 0, mra_ref[...], ma_ref[...])
    mb_ref[y] = low + high
    m_b = [remote(mb_ref.at[y], mb_ref.at[y], sems(mb_sem), d - 1, **y_dev(d)) for d in range(1, NY)]
    for copy in m_b:
        copy.start()
    for i in range(D // 1024):
        cols = slice(i * 1024, i * 1024 + 1024)
        gtok_ref[:, cols] = dot(gr, full_ref[cols, :], 1, 1).astype(BF)
    stores.append(pltpu.make_async_copy(gtok_ref, gtok_hbm.at[0], here_sem.at[5]))
    stores[-1].start()
    def drain(i, _):
        for here, copy in (
            (z < NZ - 1, go_right), (z > 0, go_left), (x < NX - 1, go_below), (x > 0, go_above)
        ):
            @pl.when(here)
            def _():
                copy(i).wait_send()

        return 0

    lax.fori_loop(0, PIECES, drain, 0)
    sent = [up_a, up_b, down_a, down_b, to_sib, halo, on_up, on_down, sib_down, sib_up, sib_a, sib_b]
    for copy in sent + decs:
        copy.wait_send()
    own = pl.ds(pl.multiple_of(x * PX, PX), PX)
    to_y2 = {}
    for d in order:
        acc = mx_ref[d, own, :].astype(F32)
        for e in (1, 3, 2):
            over_x[e, d].wait_recv()
            acc = acc + rx_ref[e - 1, d].astype(F32)
        if d:
            sy_ref[d - 1] = acc.astype(BF)
            to_y2[d] = remote(sy_ref.at[d - 1], ry_ref.at[d - 1], sems(y_sem), d - 1, **y_dev(d))
            to_y2[d].start()
        else:
            pz_ref[:, S:] = acc
    acc = ta_ref[...].astype(F32)
    for d in (1, 3, 2):
        to_y[d].wait_recv()
        acc = acc + rb_ref[d - 1].astype(F32)
    ta_ref[...] = acc.astype(BF)
    to_x = {}
    for d in (2, 1, 3):
        to_x[d] = remote(
            ta_ref.at[x_rows(d), :], rc_ref.at[d - 1], sems(c_sem), d - 1, **x_dev(d)
        )
        to_x[d].start()
    for copy in m_b:
        copy.wait_recv()
    mc_ref[x] = mb_ref[0] + mb_ref[1] + mb_ref[2] + mb_ref[3]
    m_c = [remote(mc_ref.at[x], mc_ref.at[x], sems(mc_sem), d - 1, **x_dev(d)) for d in range(1, NX)]
    for copy in m_c:
        copy.start()
    acc = pz_ref[:, S:]
    for d in (1, 3, 2):
        to_y2[d].wait_recv()
        acc = acc + ry_ref[d - 1].astype(F32)
    pz_ref[:, S:] = acc
    acc = ta_ref[own, :].astype(F32)
    for d in (1, 3, 2):
        to_x[d].wait_recv()
        acc = acc + rc_ref[d - 1].astype(F32)
    pz_ref[:, :S] = acc
    px, pzr = PX, PZ
    to_z = {}
    for d in (4, 3, 5, 2, 6, 1, 7):
        sd_ref[d - 1] = pz_ref[pl.ds(pl.multiple_of(at_z(d) * pzr, pzr), pzr), :].astype(BF)
        to_z[d] = remote(sd_ref.at[d - 1], rd_ref.at[d - 1], sems(d_sem), d - 1, **z_dev(d))
        to_z[d].start()
    for copy in m_c:
        copy.wait_recv()
    mrd_ref[z] = mc_ref[0] + mc_ref[1] + mc_ref[2] + mc_ref[3]
    m_d = [remote(mrd_ref.at[z], mrd_ref.at[z], sems(md_sem), d - 1, **z_dev(d)) for d in range(1, NZ)]
    for copy in m_d:
        copy.start()
    acc = pz_ref[pl.ds(pl.multiple_of(z * pzr, pzr), pzr), :]
    for d in (1, 7, 2, 6, 3, 5, 4):
        to_z[d].wait_recv()
        acc = acc + rd_ref[d - 1].astype(F32)
    fin_ref[...] = acc.astype(BF)

    def piece(xx, first, size):
        return all_ref.at[pl.ds(pl.multiple_of(xx * px + first, pzr), size), :]

    done = [
        remote(fin_ref, piece(x, z * pzr, pzr), sems(e_sem), d - 1, **z_dev(d))
        for d in (4, 3, 5, 2, 6, 1, 7)
    ]
    for copy in done:
        copy.start()
    all_ref[pl.ds(pl.multiple_of(x * px + z * pzr, pzr), pzr), :] = fin_ref[...]
    for copy in m_d:
        copy.wait_recv()
    total = mrd_ref[0]
    for i in range(1, NZ):
        total = total + mrd_ref[i]
    sums_ref[...] = total
    for copy in done:
        copy.wait_recv()
    last = [
        remote(piece(x, 0, px), piece(x, 0, px), sems(f_sem), d - 1, **x_dev(d)) for d in (2, 1, 3)
    ]
    for copy in last:
        copy.start()
    for copy in last:
        copy.wait_recv()
    late_sends = [rim, m_a] + m_b + m_c + m_d + done + last
    late_sends += list(over_x.values()) + list(to_y2.values()) + list(copies.values()) + list(to_y.values()) + list(to_x.values()) + list(to_z.values())
    for copy in late_sends:
        copy.wait_send()

    for copy in stores:
        copy.wait()


def run_all(*args):
    anywhere = pl.BlockSpec(memory_space=pl.ANY)
    return pl.pallas_call(
        layer_kernel,
        out_shape=tuple(jax.ShapeDtypeStruct(o[1], o[2]) for o in OUTPUTS),
        in_specs=[pl.BlockSpec(memory_space=pltpu.HBM) if name.endswith("_hbm") else VMEM for name in INPUTS],
        out_specs=tuple(VMEM if o[3] else anywhere for o in OUTPUTS),
        scratch_shapes=[pltpu.VMEM(b[1], b[2]) for b in BUFFERS]
        + [pltpu.SemaphoreType.DMA(m[1]) for m in SEMAPHORES],
        compiler_params=pltpu.CompilerParams(
            collective_id=0, has_side_effects=True, vmem_limit_bytes=BIG
        ),
        name="ssm_layer",
    )(*args)


def last_kernel(
    out_ref, gv_ref, gtok_ref, graw_ref, all_ref, sums_ref,
    out_to, gv_to, gtok_to, graw_to, gw_ref, gcw_ref, gcb_ref, gbias_ref, galog_ref, gskip_ref,
    sem,
):
    pairs = ((gv_ref, gv_to), (out_ref, out_to), (gtok_ref, gtok_to))
    put = [pltpu.make_async_copy(src, dst, sem.at[i]) for i, (src, dst) in enumerate(pairs)]
    for copy in put:
        copy.start()
    graw_to[...] = graw_ref[...]
    gw_ref[...] = all_ref[...].astype(F32)
    gcw_ref[...] = sums_ref[0:4, :]
    gcb_ref[...] = sums_ref[4:5, :]
    gbias_ref[...] = sums_ref[5:6, 0:H]
    galog_ref[...] = sums_ref[6:7, 0:H]
    gskip_ref[...] = sums_ref[7:8, 0:H]
    for copy in put:
        copy.wait()


def hand_out(*args):
    head = jax.ShapeDtypeStruct((1, H), F32)
    anywhere = pl.BlockSpec(memory_space=pl.ANY)
    wide = jax.ShapeDtypeStruct((1, S, D), BF)
    return pl.pallas_call(
        last_kernel,
        out_shape=(
            wide, wide, wide,
            jax.ShapeDtypeStruct((1, H, S), F32),
            jax.ShapeDtypeStruct((ROWS, W2), F32),
            jax.ShapeDtypeStruct((4, W2), F32),
            jax.ShapeDtypeStruct((1, W2), F32),
            head, head, head,
        ),
        in_specs=[VMEM] * 6,
        out_specs=(anywhere,) * 3 + (VMEM,) * 7,
        scratch_shapes=[pltpu.SemaphoreType.DMA((3,))],
        compiler_params=pltpu.CompilerParams(vmem_limit_bytes=SMALL),
        name="hand_out",
    )(*args)


def body(layer_in, w_bc, conv_w, conv_b, ssm_in, dt_raw, dt_bias, a_log, skip_scale, grad_out):
    made = run_all(
        w_bc, layer_in, conv_w, conv_b[None], ssm_in, jnp.swapaxes(dt_raw, 1, 2), dt_bias[None],
        a_log[None], skip_scale[None], grad_out,
    )
    out, gv, gtok, graw, gw, gcw, gcb, gbias, galog, gskip = hand_out(*made)
    return (
        out, gv, gtok, jnp.swapaxes(graw, 1, 2), gw, gcw, gcb[0], gbias[0], galog[0], gskip[0]
    )


def solution(mesh):
    split = P("fsdp", "ctx", None)
    in_specs = (
        split, P("fsdp", None), P(), P(), split, split, P(), P(), P(), split,
    )
    out_specs = (
        split, split, split, split, P("fsdp", None), P(), P(), P(), P(), P(),
    )
    return jax.shard_map(body, mesh=mesh, in_specs=in_specs, out_specs=out_specs, check_vma=False)
```
